32 devices in a mesh: rows: 8 (over z, y), heads: 4 (over x, core).
Axes of the slice: x: 2, y: 2, z: 4, core: 2. Of those that a mesh axis runs over, the one named last changes fastest.
Arguments:
- hidden_in: bfloat16 [64, 512, 768], P('rows', 'heads'), may hold values from -6 to 6
- lengths: int32 [64, 4], P('rows'), may hold values from 1 to 256, 512 in all within a row
- qkv_weight: bfloat16 [768, 2304], replicated, may hold values from -0.21875 to 0.21875
- query_bias: bfloat16 [768], replicated, may hold values from -3 to 3
- value_bias: bfloat16 [768], replicated, may hold values from -0.59765625 to 0.59765625
- out_weight: bfloat16 [768, 768], replicated, may hold values from -1.75 to 1.75
- out_bias: bfloat16 [768], replicated, may hold values from -1.1953125 to 1.1953125
- gain_one: bfloat16 [768], replicated, may hold values from 0.5 to 1.5
- shift_one: bfloat16 [768], replicated, may hold values from -1.1953125 to 1.1953125
- up_weight: bfloat16 [768, 3072], replicated, may hold values from -0.21875 to 0.21875
- up_bias: bfloat16 [3072], replicated, may hold values from -1.1953125 to 1.1953125
- down_weight: bfloat16 [3072, 768], replicated, may hold values from -0.15625 to 0.15625
- down_bias: bfloat16 [768], replicated, may hold values from -1.1953125 to 1.1953125
- gain_two: bfloat16 [768], replicated, may hold values from 0.5 to 1.5
- shift_two: bfloat16 [768], replicated, may hold values from -1.1953125 to 1.1953125
- cotangent: bfloat16 [64, 512, 768], P('rows', 'heads'), may hold values from -6 to 6
Outputs:
- layer_out: bfloat16 [64, 512, 768], P('rows', 'heads')
- input_grad: float32 [64, 512, 768], P('rows', 'heads')
- qkv_grad: float32 [768, 2304], P('rows', 'heads')
- querybias_grad: float32 [768], replicated
- valuebias_grad: float32 [768], replicated
- outweight_grad: float32 [768, 768], P('rows', 'heads')
- outbias_grad: float32 [768], replicated
- gainone_grad: float32 [768], replicated
- shiftone_grad: float32 [768], replicated
- upweight_grad: float32 [768, 3072], P('rows', 'heads')
- upbias_grad: float32 [3072], replicated
- downweight_grad: float32 [3072, 768], P('rows', 'heads')
- downbias_grad: float32 [768], replicated
- gaintwo_grad: float32 [768], replicated
- shifttwo_grad: float32 [768], replicated
The draws below stay inside these ranges and needn't reach their ends.
Inputs may be any that keep to these rules, and one draw needn't show every extreme that they name: The 4 lengths of a packed row sum to 512; in every row the longest is 256.
All inputs are finite; a program needn't handle non-finite values.
Results may differ from the reference program's by a relative error of at most 0.017.
Values may be sent and summed in bfloat16 or wider, within the bound.
A program may use at most 192 MiB of HBM per device.

```python
import math
import jax
import jax.numpy as jnp
import numpy as np
from jax import lax

H = 12
DH = 64
D = 768
FF = 3072
L = 512
EX = 4
MOST = 256
ROWS_DEV = 2
NROWS = 64
N_HEADS = 4


def shard_levels(key, extent, cuts, low, high):
    level, own = 1.0, jax.random.fold_in(key, 6)
    for position, parts in cuts:
        steps = jnp.exp(jax.random.uniform(jax.random.fold_in(own, position), (parts,), jnp.float32, low / len(cuts), high / len(cuts)))
        level = level * jnp.repeat(steps, extent[position] // parts).reshape([-1 if axis == position else 1 for axis in range(len(extent))])
    return level


def profile(number_of, total, limit, lean):
    portions = [(1 << 20) // math.isqrt(standing ** lean) + 1 for standing in range(2, number_of + 1)]
    rest, given = total - limit - (number_of - 1), [1] * (number_of - 1)
    while rest > 0:
        free = [i for i in range(number_of - 1) if given[i] < limit]
        mass, left = sum([portions[i] for i in free]), rest
        for i in free:
            more = min(limit - given[i], max(1, left * portions[i] // mass), rest)
            given[i] = given[i] + more
            rest = rest - more
    return np.array([limit] + given)


def uneven(own_key, amount, total, bound, skew):
    if amount == 2:
        one = jax.random.randint(own_key, (), max(1, total - bound), min(bound, total - 1) + 1)
        return jnp.stack([one, total - one])
    tallies = jnp.asarray(profile(amount, total, bound, skew), jnp.int32)
    twos = (amount - 1) // 2
    donor, taker = tallies[1:1 + 2 * twos:2], tallies[2:2 + 2 * twos:2]
    margin = jnp.minimum(donor - 1, bound - taker)
    moved = jax.random.randint(jax.random.fold_in(own_key, 1), (twos,), 0, 1 << 20) % (margin + 1)
    tallies = tallies.at[1:1 + 2 * twos:2].set(donor - moved).at[2:2 + 2 * twos:2].set(taker + moved)
    return tallies[jax.random.permutation(jax.random.fold_in(own_key, 2), amount)]


def normal_values(rng, extent, deviation, limit, cuts=(), kind=jnp.bfloat16):
    array = deviation * jax.random.normal(rng, extent, jnp.float32)
    if cuts:
        array = array * shard_levels(rng, extent, cuts, -0.22, 0.18)
    return jnp.clip(array, -limit, limit).astype(kind)


def setup_inputs(seed: int = 0) -> dict:
    arg_keys = jax.random.split(jax.random.key(seed), 17)
    hidden_in = normal_values(arg_keys[0], (NROWS, L, D), 1.0, 6.0, ((0, 8), (1, 4)))
    lengths = jax.vmap(lambda own: uneven(own, EX, L, MOST, 2))(jax.random.split(arg_keys[1], NROWS)).reshape((NROWS, EX)).astype(jnp.int32)
    qkv_weight = normal_values(arg_keys[2], (D, 3 * D), D ** -0.5, 0.21875)
    query_bias = normal_values(arg_keys[3], (D,), 0.5, 3.0)
    value_bias = normal_values(arg_keys[4], (D,), 0.1, 0.59765625)
    out_weight = normal_values(arg_keys[5], (D, D), (D // 64) ** -0.5, 1.75)
    out_bias = normal_values(arg_keys[6], (D,), 0.2, 1.1953125)
    gain_one = jnp.clip(1.0 + 0.1 * jax.random.normal(arg_keys[7], (D,), jnp.float32), 0.5, 1.5).astype(jnp.bfloat16)
    shift_one = normal_values(arg_keys[8], (D,), 0.2, 1.1953125)
    up_weight = normal_values(arg_keys[9], (D, FF), D ** -0.5, 0.21875)
    up_bias = normal_values(arg_keys[10], (FF,), 0.2, 1.1953125)
    down_weight = normal_values(arg_keys[11], (FF, D), (FF // 2) ** -0.5, 0.15625)
    down_bias = normal_values(arg_keys[12], (D,), 0.2, 1.1953125)
    gain_two = jnp.clip(1.0 + 0.1 * jax.random.normal(arg_keys[13], (D,), jnp.float32), 0.5, 1.5).astype(jnp.bfloat16)
    shift_two = normal_values(arg_keys[14], (D,), 0.2, 1.1953125)
    cotangent = normal_values(arg_keys[15], (NROWS, L, D), 1.0, 6.0, ((0, 8), (1, 4)))
    return {"hidden_in": hidden_in, "lengths": lengths, "qkv_weight": qkv_weight, "query_bias": query_bias, "value_bias": value_bias, "out_weight": out_weight, "out_bias": out_bias, "gain_one": gain_one, "shift_one": shift_one, "up_weight": up_weight, "up_bias": up_bias, "down_weight": down_weight, "down_bias": down_bias, "gain_two": gain_two, "shift_two": shift_two, "cotangent": cotangent}


@jax.custom_vjp
def low(v):
    return lax.optimization_barrier(v.astype(jnp.bfloat16)).astype(jnp.float32)

@jax.custom_vjp
def low_back(v):
    return v

def low_keep(v):
    return (low(v), None)

def low_pass(kept, grad):
    return (grad,)

def back_keep(v):
    return (v, None)

def back_low(kept, grad):
    return (low(grad),)
low.defvjp(low_keep, low_pass)
low_back.defvjp(back_keep, back_low)
EPSILON = 1e-12
HIGH = lax.Precision.HIGHEST

def segment_ids(lengths):
    ends = jnp.cumsum(lengths, axis=-1).astype(jnp.int32)
    places = jnp.arange(L, dtype=jnp.int32)
    return lax.optimization_barrier(jnp.sum((places[None, :, None] >= ends[:, None, :]).astype(jnp.int32), axis=-1)).astype(jnp.int32)

def layer_norm(values, gain, shift):
    middle = lax.optimization_barrier(jnp.mean(values, axis=-1, keepdims=True))
    center = values - middle
    spread = lax.optimization_barrier(jnp.mean(center * center, axis=-1, keepdims=True))
    return center * lax.rsqrt(spread + EPSILON) * gain + shift

def attend_row(queries, key_rows, value_rows, segment):
    scores = jnp.einsum('qhd,khd->hqk', queries, key_rows, precision=HIGH) * DH ** (-0.5)
    scores = low_back(scores)
    same = segment[:, None] == segment[None, :]
    scores = jnp.where(same[None], scores, -1e+30)
    chance = jax.nn.softmax(scores, axis=-1)
    return jnp.einsum('hqk,khd->qhd', low(chance), value_rows, precision=HIGH)

def forward(params, hidden, segment):
    qkv_weight, query_bias, value_bias, out_weight, out_bias, gain_one, shift_one, up_weight, up_bias, down_weight, down_bias, gain_two, shift_two = params
    count = hidden.shape[0] // L
    joint = jnp.dot(hidden, qkv_weight, precision=HIGH)
    queries = low_back(low(joint[:, :D] + query_bias))
    key_rows = low_back(low(joint[:, D:2 * D]))
    value_rows = low_back(low(joint[:, 2 * D:] + value_bias))

    def shaped(values):
        return values.reshape(count, L, H, DH)
    row_fn = jax.checkpoint(attend_row)
    context = lax.map(lambda item: row_fn(item[0], item[1], item[2], item[3]), (shaped(queries), shaped(key_rows), shaped(value_rows), segment))
    context = low_back(low(context.reshape(count * L, D)))
    branch = low_back(jnp.dot(context, out_weight, precision=HIGH) + out_bias)
    first = layer_norm(hidden + branch, gain_one, shift_one)
    inner = low_back(jnp.dot(low(first), up_weight, precision=HIGH) + up_bias)
    active = low(jax.nn.gelu(inner, approximate=False))
    outer = low_back(jnp.dot(active, down_weight, precision=HIGH) + down_bias)
    return layer_norm(first + outer, gain_two, shift_two)

def reference(hidden_in, lengths, qkv_weight, query_bias, value_bias, out_weight, out_bias, gain_one, shift_one, up_weight, up_bias, down_weight, down_bias, gain_two, shift_two, cotangent):
    params = tuple((item.astype(jnp.float32) for item in (qkv_weight, query_bias, value_bias, out_weight, out_bias, gain_one, shift_one, up_weight, up_bias, down_weight, down_bias, gain_two, shift_two)))
    group_rows = ROWS_DEV * N_HEADS
    group_tokens = group_rows * L
    groups = NROWS // group_rows
    inputs = hidden_in.astype(jnp.float32).reshape(groups, group_tokens, D)
    grads_out = cotangent.astype(jnp.float32).reshape(groups, group_tokens, D)
    grouped_lengths = lengths.reshape(groups, group_rows, EX)

    def one_group(totals, item):
        hidden, grad_out, lens_group = item
        segment = segment_ids(lens_group)
        result, pullback = jax.vjp(lambda weights, values: forward(weights, values, segment), params, hidden)
        grad_params, grad_hidden = pullback(grad_out)
        totals = jax.tree.map(lambda left, right: left + right, totals, grad_params)
        return (totals, (result.astype(jnp.bfloat16), grad_hidden))
    zeros = jax.tree.map(jnp.zeros_like, params)
    totals, (outputs, input_grads) = lax.scan(one_group, zeros, (inputs, grads_out, grouped_lengths))
    scaled = [item / NROWS for item in totals]
    return (outputs.reshape(NROWS, L, D), input_grads.reshape(NROWS, L, D), scaled[0], scaled[1], scaled[2], scaled[3], scaled[4], scaled[5], scaled[6], scaled[7], scaled[8], scaled[9], scaled[10], scaled[11], scaled[12])
```

```python
import functools

import jax
import jax.numpy as jnp
from jax import lax
from jax.experimental import pallas as pl
from jax.experimental.pallas import tpu as pltpu
from jax.sharding import PartitionSpec as P

DH = 64
D = 768
L = 512
EPSILON = 1e-12
OFF = -(2.0**100)
F32 = jnp.float32
BF16 = jnp.bfloat16
NN = (((1,), (0,)), ((), ()))
NT = (((1,), (1,)), ((), ()))
TN = (((0,), (0,)), ((), ()))

TAIL = (
    0.09881087227319621,
    0.11230449770687516,
    0.02424904968806795,
    0.2825055677430211,
    -0.268648558796486,
    0.34262844642428514,
    -0.09184987882933851,
)


def mm(left, right, dims=NN):
    return lax.dot_general(left, right, dims, preferred_element_type=F32)


def normal_parts(u):
    bell = jnp.exp(u * u * -0.5)
    t = pltpu.reciprocal(1.0 + 0.25 * jnp.abs(u))
    poly = TAIL[-1]
    for item in TAIL[-2::-1]:
        poly = poly * t + item
    tail = poly * t * bell
    return jnp.where(u >= 0, 1.0 - tail, tail), bell * 0.3989422804014327


def norm_parts(values):
    middle = jnp.mean(values, axis=-1, keepdims=True)
    center = values - middle
    spread = jnp.mean(center * center, axis=-1, keepdims=True)
    scale = lax.rsqrt(spread + EPSILON)
    return center * scale, scale


def norm_back(grad, normed, scale, gain):
    dn = grad * gain
    first = jnp.mean(dn, axis=-1, keepdims=True)
    second = jnp.mean(dn * normed, axis=-1, keepdims=True)
    return (dn - first - normed * second) * scale


def split3(values):
    high = values.astype(BF16)
    rest = values - high.astype(F32)
    mid = rest.astype(BF16)
    return high, mid, (rest - mid.astype(F32)).astype(BF16)


def features(ends, key_feat, query_feat, start):
    token = lax.broadcasted_iota(jnp.int32, (L, 128), 0)
    place = lax.broadcasted_iota(jnp.int32, (L, 128), 1) & (DH - 1)
    seg = jnp.zeros((L, 128), jnp.int32)
    for end in ends:
        seg = seg + (token >= end).astype(jnp.int32)
    count = len(ends)
    ones = (place == seg) | ((place >= count) & (place < count + 3))
    key_feat[pl.ds(start, L), :] = jnp.where(ones, 1.0, 0.0).astype(BF16)
    off = (place < count) & (place != seg)
    query_feat[pl.ds(start, L), :] = jnp.where(off, OFF, 0.0).astype(BF16)


def attend(rows, group, pairs, qkv, ctx, lse, key_feat, query_feat):
    lane = lax.broadcasted_iota(jnp.int32, (1, 128), 1)
    kf, qf = key_feat[rows, :], query_feat[rows, :]
    ops, values = [], []
    for pair in range(pairs):
        col = pl.multiple_of(group * (pairs * 128) + pair * 128, 128)
        q2 = qkv[rows, pl.ds(col, 128)]
        k2 = qkv[rows, pl.ds(D + col, 128)]
        values.append(qkv[rows, pl.ds(2 * D + col, 128)])
        for own in (lane < DH, lane >= DH):
            ops.append((jnp.where(own, q2, qf), jnp.where(own, k2, kf)))
    count = 2 * pairs
    scores = [None] * count
    outs, sums = [], []
    scores[0] = mm(*ops[0], NT)
    for head in range(count):
        if head + 1 < count:
            scores[head + 1] = mm(*ops[head + 1], NT)
        peak = jnp.max(scores[head], axis=1, keepdims=True)
        expo = jnp.exp(scores[head] - peak)
        total = jnp.sum(expo, axis=1, keepdims=True)
        out = mm(expo.astype(BF16), values[head // 2])
        outs.append(out * (1.0 / total))
        sums.append(peak + jnp.log(total))
    keep = jnp.zeros((L, 128), F32)
    for head in range(count):
        keep = jnp.where(lane == head, sums[head], keep)
    lse[group, rows, :] = keep
    for pair in range(pairs):
        col = pl.multiple_of(group * (pairs * 128) + pair * 128, 128)
        both = jnp.where(lane < DH, outs[2 * pair], outs[2 * pair + 1])
        ctx[rows, pl.ds(col, 128)] = both.astype(BF16)


def attend_back(rows, group, pairs, qkv, ctx, dctx, lse, grads, key_feat, query_feat):
    lane = lax.broadcasted_iota(jnp.int32, (1, 128), 1)
    place = lane & (DH - 1)
    kf, qf = key_feat[rows, :], query_feat[rows, :]
    vf = jnp.where((place >= 4) & (place < 7), 1.0, 0.0).astype(BF16)
    keep = lse[group, rows, :]

    def spread(column, base):
        high, mid, small = split3(-column)
        return jnp.where(
            place == 4, high, jnp.where(place == 5, mid, jnp.where(place == 6, small, base))
        )

    ops = []
    for pair in range(pairs):
        col = pl.multiple_of(group * (pairs * 128) + pair * 128, 128)
        q2 = qkv[rows, pl.ds(col, 128)]
        k2 = qkv[rows, pl.ds(D + col, 128)]
        v2 = qkv[rows, pl.ds(2 * D + col, 128)]
        d2 = dctx[rows, pl.ds(col, 128)]
        both = d2.astype(F32) * ctx[rows, pl.ds(col, 128)].astype(F32)
        zero = jnp.zeros_like(q2)
        for side, own in enumerate((lane < DH, lane >= DH)):
            inner = jnp.sum(jnp.where(own, both, 0.0), axis=1, keepdims=True)
            total = keep[:, 2 * pair + side : 2 * pair + side + 1]
            ops.append(
                (
                    jnp.where(own, k2, kf),
                    jnp.where(own, q2, spread(total, qf)),
                    jnp.where(own, v2, vf),
                    jnp.where(own, d2, spread(inner, zero)),
                    jnp.where(own, q2, zero),
                    jnp.where(own, k2, zero),
                    jnp.where(own, d2, zero),
                )
            )
    count = 2 * pairs
    scores, chances = [None] * count, [None] * count
    dq, dk, dv = [0] * pairs, [0] * pairs, [0] * pairs

    def start(head):
        scores[head] = mm(ops[head][0], ops[head][1], NT)
        chances[head] = mm(ops[head][2], ops[head][3], NT)

    start(0)
    for head in range(count):
        if head + 1 < count:
            start(head + 1)
        chance = jnp.exp(scores[head])
        low = chance.astype(BF16)
        ds = (chance * chances[head]).astype(BF16)
        pair = head // 2
        dk[pair] += mm(ds, ops[head][4])
        dv[pair] += mm(low, ops[head][6])
        dq[pair] += mm(ds, ops[head][5], TN)
    for pair in range(pairs):
        col = pl.multiple_of(group * (pairs * 128) + pair * 128, 128)
        grads[rows, pl.ds(col, 128)] = (dq[pair] * DH**-0.5).astype(BF16)
        grads[rows, pl.ds(D + col, 128)] = dk[pair].astype(BF16)
        grads[rows, pl.ds(2 * D + col, 128)] = dv[pair].astype(BF16)


def first_kernel(x, lens, wqkv, bqkv, wout, bout, qkv, ctx, r1, lse, key_feat, query_feat):
    for row in range(x.shape[0] // L):
        ends, total = [], 0
        for item in range(lens.shape[1]):
            total = total + lens[row, item]
            ends.append(total)
        features(ends, key_feat, query_feat, row * L)

        rows = pl.ds(row * L, L)
        for part in range(3):
            cols = pl.ds(part * D, D)
            acc = mm(x[rows, :], wqkv[:, cols]) + bqkv[:, cols]
            if part == 0:
                acc = acc * DH**-0.5
            qkv[rows, cols] = acc.astype(BF16)

        def heads(group, carry):
            attend(rows, group, 3, qkv, ctx, lse, key_feat, query_feat)
            return carry

        lax.fori_loop(0, 2, heads, 0)
        r1[rows, :] = mm(ctx[rows, :], wout[...]) + bout[...] + x[rows, :].astype(F32)


def middle_kernel(
    r1, ctx, cot, vecs, wup, bup, wdown, wout,
    y, dr1, dctx, downg, upg, outg, vec_grads, upb_grad,
    fb, act, slope, acc, dfb, dab,
):
    tokens = r1.shape[0]
    step = 256
    parts = tokens // step
    width = 768
    chunks = wup.shape[1] // width
    g1, s1, g2, s2, bd = (vecs[i : i + 1, :] for i in range(5))
    vec_grads[...] = jnp.zeros_like(vec_grads)
    upb_grad[...] = jnp.zeros_like(upb_grad)

    def lead(i, carry):
        rows = pl.ds(pl.multiple_of(i * step, step), step)
        normed, _ = norm_parts(r1[rows, :])
        first = normed * g1 + s1
        fb[rows, :] = first.astype(BF16)
        acc[rows, :] = first + bd
        return carry

    lax.fori_loop(0, parts, lead, 0)

    def forward(c, carry):
        cols = pl.ds(pl.multiple_of(c * width, width), width)
        u, e = [None] * parts, [None] * parts
        for s in range(parts + 2):
            if s < parts:
                u[s] = mm(fb[s * step : (s + 1) * step, :], wup[:, cols]) + bup[:, cols]
            if 0 <= s - 1 < parts:
                j = s - 1
                rows = slice(j * step, (j + 1) * step)
                cdf, pdf = normal_parts(u[j])
                e[j] = (u[j] * cdf).astype(BF16)
                act[rows, cols] = e[j]
                slope[rows, cols] = (cdf + u[j] * pdf).astype(BF16)
            if 0 <= s - 2 < parts:
                j = s - 2
                acc[j * step : (j + 1) * step, :] += mm(e[j], wdown[cols, :])
        return carry

    lax.fori_loop(0, chunks, forward, 0)

    def second(i, carry):
        rows = pl.ds(pl.multiple_of(i * step, step), step)
        normed, scale = norm_parts(acc[rows, :])
        y[rows, :] = (normed * g2 + s2).astype(BF16)
        dy = cot[rows, :].astype(F32)
        dr2 = norm_back(dy, normed, scale, g2)
        acc[rows, :] = dr2
        low = dr2.astype(BF16)
        dfb[rows, :] = low
        vec_grads[0:1, :] += jnp.sum(dy * normed, axis=0, keepdims=True)
        vec_grads[1:2, :] += jnp.sum(dy, axis=0, keepdims=True)
        vec_grads[2:3, :] += jnp.sum(low.astype(F32), axis=0, keepdims=True)
        return carry

    lax.fori_loop(0, parts, second, 0)

    def down(c, carry):
        cols = pl.ds(pl.multiple_of(c * width, width), width)
        downg[:, cols] = mm(dfb[...], act[:, cols], TN).astype(BF16)
        return carry

    lax.fori_loop(0, chunks, down, 0)

    def backward(c, carry):
        cols = pl.ds(pl.multiple_of(c * width, width), width)
        de, du = [None] * parts, [None] * parts
        sums = jnp.zeros((1, width), F32)
        for s in range(parts + 2):
            if s < parts:
                de[s] = mm(dfb[s * step : (s + 1) * step, :], wdown[cols, :], NT)
            if 0 <= s - 1 < parts:
                j = s - 1
                rows = slice(j * step, (j + 1) * step)
                du[j] = (de[j] * slope[rows, cols].astype(F32)).astype(BF16)
                slope[rows, cols] = du[j]
                sums = sums + jnp.sum(du[j].astype(F32), axis=0, keepdims=True)
            if 0 <= s - 2 < parts:
                j = s - 2
                acc[j * step : (j + 1) * step, :] += mm(du[j], wup[:, cols], NT)
        upb_grad[:, cols] = sums
        return carry

    lax.fori_loop(0, chunks, backward, 0)

    def third(i, carry):
        rows = pl.ds(pl.multiple_of(i * step, step), step)
        normed, scale = norm_parts(r1[rows, :])
        grad = acc[rows, :]
        dr = norm_back(grad, normed, scale, g1)
        dr1[rows, :] = dr
        low = dr.astype(BF16)
        dab[rows, :] = low
        vec_grads[3:4, :] += jnp.sum(grad * normed, axis=0, keepdims=True)
        vec_grads[4:5, :] += jnp.sum(grad, axis=0, keepdims=True)
        vec_grads[5:6, :] += jnp.sum(low.astype(F32), axis=0, keepdims=True)
        return carry

    lax.fori_loop(0, parts, third, 0)
    dctx[...] = mm(dab[...], wout[...], NT).astype(BF16)
    outg[...] = mm(ctx[...], dab[...], TN).astype(BF16)

    def up(c, carry):
        cols = pl.ds(pl.multiple_of(c * width, width), width)
        upg[:, cols] = mm(fb[...], slope[:, cols], TN).astype(BF16)
        return carry

    lax.fori_loop(0, chunks, up, 0)


def last_kernel(x, lens, qkv, ctx, dctx, lse, dr1, wqkv, xg, qkvg, vec_grads, grads, key_feat, query_feat):
    vec_grads[...] = jnp.zeros_like(vec_grads)
    for row in range(x.shape[0] // L):
        ends, total = [], 0
        for item in range(lens.shape[1]):
            total = total + lens[row, item]
            ends.append(total)
        features(ends, key_feat, query_feat, row * L)

        rows = pl.ds(row * L, L)

        def heads(group, carry):
            attend_back(rows, group, 3, qkv, ctx, dctx, lse, grads, key_feat, query_feat)
            return carry

        lax.fori_loop(0, 2, heads, 0)
    vec_grads[0:1, :] = jnp.sum(grads[:, 0:D].astype(F32), axis=0, keepdims=True)
    vec_grads[1:2, :] = jnp.sum(grads[:, 2 * D : 3 * D].astype(F32), axis=0, keepdims=True)
    for part in range(3):
        cols = slice(part * D, (part + 1) * D)
        qkvg[:, cols] = mm(x[...], grads[:, cols], TN).astype(BF16)
    xg[...] = (mm(grads[...], wqkv[...], NT) + dr1[...]).astype(xg.dtype)


VMEM = pl.BlockSpec(memory_space=pltpu.VMEM)
SMEM = pl.BlockSpec(memory_space=pltpu.SMEM)


def shape(dims, kind):
    return jax.ShapeDtypeStruct(dims, kind)


def params(**more):
    return pltpu.CompilerParams(vmem_limit_bytes=63 * 2**20, **more)


def local(
    hidden_in, lengths, qkv_weight, query_bias, value_bias, out_weight, out_bias, gain_one,
    shift_one, up_weight, up_bias, down_weight, down_bias, gain_two, shift_two, cotangent,
):
    row_count, part_len = hidden_in.shape[0], hidden_in.shape[1]
    heads = lax.axis_size("heads")
    mine = row_count // heads
    tokens = mine * L
    ff = up_weight.shape[1]
    place = lax.axis_index("heads")
    x = lax.all_to_all(hidden_in, "heads", split_axis=0, concat_axis=1, tiled=True).reshape(tokens, D)
    cot = lax.all_to_all(cotangent, "heads", split_axis=0, concat_axis=1, tiled=True).reshape(tokens, D)
    lens = lax.dynamic_slice_in_dim(lengths, place * mine, mine, 0)
    bqkv = jnp.concatenate([query_bias, jnp.zeros_like(query_bias), value_bias]).astype(F32)[None]
    qkv, ctx, r1, lse = pl.pallas_call(
        first_kernel,
        out_shape=(
            shape((tokens, 3 * D), BF16), shape((tokens, D), BF16), shape((tokens, D), F32),
            shape((2, tokens, 128), F32),
        ),
        in_specs=[VMEM, SMEM] + [VMEM] * 4,
        out_specs=(VMEM,) * 4,
        scratch_shapes=[pltpu.VMEM((tokens, 128), BF16)] * 2,
        compiler_params=params(),
        name="first",
    )(x, lens, qkv_weight, bqkv, out_weight, out_bias.astype(F32)[None])
    vecs = jnp.stack([gain_one, shift_one, gain_two, shift_two, down_bias]).astype(F32)
    y, dr1, dctx, downg, upg, outg, vec_mid, upb = pl.pallas_call(
        middle_kernel,
        out_shape=(
            shape((tokens, D), BF16), shape((tokens, D), F32), shape((tokens, D), BF16),
            shape((D, ff), BF16), shape((D, ff), BF16), shape((D, D), BF16),
            shape((8, D), F32), shape((1, ff), F32),
        ),
        in_specs=[VMEM] * 8,
        out_specs=(VMEM,) * 8,
        scratch_shapes=[
            pltpu.VMEM((tokens, D), BF16), pltpu.VMEM((tokens, ff), BF16), pltpu.VMEM((tokens, ff), BF16),
            pltpu.VMEM((tokens, D), F32), pltpu.VMEM((tokens, D), BF16), pltpu.VMEM((tokens, D), BF16),
        ],
        compiler_params=params(),
        name="middle",
    )(r1, ctx, cot, vecs, up_weight, up_bias.astype(F32)[None], down_weight, out_weight)
    xg, qkvg, vec_last = pl.pallas_call(
        last_kernel,
        out_shape=(shape((tokens, D), BF16), shape((D, 3 * D), BF16), shape((8, D), F32)),
        in_specs=[VMEM, SMEM] + [VMEM] * 6,
        out_specs=(VMEM,) * 3,
        scratch_shapes=[pltpu.VMEM((tokens, 3 * D), BF16)] + [pltpu.VMEM((tokens, 128), BF16)] * 2,
        compiler_params=params(),
        name="last",
    )(x, lens, qkv, ctx, dctx, lse, dr1, qkv_weight)

    def back(values):
        values = values.reshape(mine, L, D)
        return lax.all_to_all(values, "heads", split_axis=1, concat_axis=0, tiled=True)

    layer_out = back(y)
    input_grad = back(xg).astype(F32)
    scale = 1.0 / (row_count * lax.axis_size("rows"))
    vec_mid, vec_last, upb = lax.psum((vec_mid, vec_last, upb), ("rows", "heads"))

    def reduce(values, flip):
        one, two = (0, 1) if flip else (1, 0)
        half = lax.psum_scatter(values, "heads", scatter_dimension=one, tiled=True).astype(F32)
        total = lax.psum_scatter(half, "rows", scatter_dimension=two, tiled=True) * scale
        return total.T if flip else total

    vm, vl = vec_mid * scale, vec_last * scale
    return (
        layer_out, input_grad, reduce(qkvg, False), vl[0], vl[1], reduce(outg, False), vm[5], vm[3], vm[4],
        reduce(upg, False), upb[0] * scale, reduce(downg, True), vm[2], vm[0], vm[1],
    )


def solution(mesh):
    split = P("rows", "heads", None)
    grid = P("rows", "heads")
    in_specs = (split, P("rows", None)) + (P(),) * 13 + (split,)
    out_specs = (split, split, grid, P(), P(), grid, P(), P(), P(), grid, P(), grid, P(), P(), P())
    return jax.shard_map(local, mesh=mesh, in_specs=in_specs, out_specs=out_specs, check_vma=False)
```

```python
import functools

import jax
import jax.numpy as jnp
from jax import lax
from jax.experimental import pallas as pl
from jax.experimental.pallas import tpu as pltpu
from jax.sharding import PartitionSpec as P

DH = 64
D = 768
L = 512
EPSILON = 1e-12
OFF = -(2.0**100)
F32 = jnp.float32
BF16 = jnp.bfloat16
NN = (((1,), (0,)), ((), ()))
NT = (((1,), (1,)), ((), ()))
TN = (((0,), (0,)), ((), ()))

TAIL = (
    0.09881087227319621,
    0.11230449770687516,
    0.02424904968806795,
    0.2825055677430211,
    -0.268648558796486,
    0.34262844642428514,
    -0.09184987882933851,
)


def mm(left, right, dims=NN):
    return lax.dot_general(left, right, dims, preferred_element_type=F32)


def normal_parts(u):
    bell = jnp.exp(u * u * -0.5)
    t = pltpu.reciprocal(1.0 + 0.25 * jnp.abs(u))
    poly = TAIL[-1]
    for item in TAIL[-2::-1]:
        poly = poly * t + item
    tail = poly * t * bell
    return jnp.where(u >= 0, 1.0 - tail, tail), bell * 0.3989422804014327


def norm_parts(values):
    middle = jnp.mean(values, axis=-1, keepdims=True)
    center = values - middle
    spread = jnp.mean(center * center, axis=-1, keepdims=True)
    scale = lax.rsqrt(spread + EPSILON)
    return center * scale, scale


def norm_back(grad, normed, scale, gain):
    dn = grad * gain
    first = jnp.mean(dn, axis=-1, keepdims=True)
    second = jnp.mean(dn * normed, axis=-1, keepdims=True)
    return (dn - first - normed * second) * scale


def split3(values):
    high = values.astype(BF16)
    rest = values - high.astype(F32)
    mid = rest.astype(BF16)
    return high, mid, (rest - mid.astype(F32)).astype(BF16)


def features(ends, key_feat, query_feat, start):
    token = lax.broadcasted_iota(jnp.int32, (L, 128), 0)
    place = lax.broadcasted_iota(jnp.int32, (L, 128), 1) & (DH - 1)
    seg = jnp.zeros((L, 128), jnp.int32)
    for end in ends:
        seg = seg + (token >= end).astype(jnp.int32)
    count = len(ends)
    ones = (place == seg) | ((place >= count) & (place < count + 3))
    key_feat[pl.ds(start, L), :] = jnp.where(ones, 1.0, 0.0).astype(BF16)
    off = (place < count) & (place != seg)
    query_feat[pl.ds(start, L), :] = jnp.where(off, OFF, 0.0).astype(BF16)


def attend(rows, group, pairs, qkv, ctx, lse, key_feat, query_feat):
    lane = lax.broadcasted_iota(jnp.int32, (1, 128), 1)
    kf, qf = key_feat[rows, :], query_feat[rows, :]
    ops, values = [], []
    for pair in range(pairs):
        col = pl.multiple_of(group * (pairs * 128) + pair * 128, 128)
        q2 = qkv[rows, pl.ds(col, 128)]
        k2 = qkv[rows, pl.ds(D + col, 128)]
        values.append(qkv[rows, pl.ds(2 * D + col, 128)])
        for own in (lane < DH, lane >= DH):
            ops.append((jnp.where(own, q2, qf), jnp.where(own, k2, kf)))
    count = 2 * pairs
    scores = [None] * count
    outs, sums = [], []
    scores[0] = mm(*ops[0], NT)
    for head in range(count):
        if head + 1 < count:
            scores[head + 1] = mm(*ops[head + 1], NT)
        peak = jnp.max(scores[head], axis=1, keepdims=True)
        expo = jnp.exp(scores[head] - peak)
        total = jnp.sum(expo, axis=1, keepdims=True)
        out = mm(expo.astype(BF16), values[head // 2])
        outs.append(out * (1.0 / total))
        sums.append(peak + jnp.log(total))
    keep = jnp.zeros((L, 128), F32)
    for head in range(count):
        keep = jnp.where(lane == head, sums[head], keep)
    lse[group, rows, :] = keep
    for pair in range(pairs):
        col = pl.multiple_of(group * (pairs * 128) + pair * 128, 128)
        both = jnp.where(lane < DH, outs[2 * pair], outs[2 * pair + 1])
        ctx[rows, pl.ds(col, 128)] = both.astype(BF16)


def attend_back(rows, group, pairs, qkv, ctx, dctx, keep, grads, key_feat, query_feat):
    lane = lax.broadcasted_iota(jnp.int32, (1, 128), 1)
    place = lane & (DH - 1)
    kf, qf = key_feat[rows, :], query_feat[rows, :]
    vf = jnp.where((place >= 4) & (place < 7), 1.0, 0.0).astype(BF16)

    def spread(column, base):
        high, mid, small = split3(-column)
        return jnp.where(
            place == 4, high, jnp.where(place == 5, mid, jnp.where(place == 6, small, base))
        )

    ops = []
    for pair in range(pairs):
        col = pl.multiple_of(group * (pairs * 128) + pair * 128, 128)
        q2 = qkv[rows, pl.ds(col, 128)]
        k2 = qkv[rows, pl.ds(D + col, 128)]
        v2 = qkv[rows, pl.ds(2 * D + col, 128)]
        d2 = dctx[rows, pl.ds(col, 128)]
        both = d2.astype(F32) * ctx[rows, pl.ds(col, 128)].astype(F32)
        zero = jnp.zeros_like(q2)
        for side, own in enumerate((lane < DH, lane >= DH)):
            inner = jnp.sum(jnp.where(own, both, 0.0), axis=1, keepdims=True)
            total = keep[:, 2 * pair + side : 2 * pair + side + 1]
            ops.append(
                (
                    jnp.where(own, k2, kf),
                    jnp.where(own, q2, spread(total, qf)),
                    jnp.where(own, v2, vf),
                    jnp.where(own, d2, spread(inner, zero)),
                    jnp.where(own, q2, zero),
                    jnp.where(own, k2, zero),
                    jnp.where(own, d2, zero),
                )
            )
    count = 2 * pairs
    scores, chances = [None] * count, [None] * count
    dq, dk, dv = [0] * pairs, [0] * pairs, [0] * pairs

    def start(head):
        scores[head] = mm(ops[head][0], ops[head][1], NT)
        chances[head] = mm(ops[head][2], ops[head][3], NT)

    start(0)
    for head in range(count):
        if head + 1 < count:
            start(head + 1)
        chance = jnp.exp(scores[head])
        low = chance.astype(BF16)
        ds = (chance * chances[head]).astype(BF16)
        pair = head // 2
        dk[pair] += mm(ds, ops[head][4])
        dv[pair] += mm(low, ops[head][6])
        dq[pair] += mm(ds, ops[head][5], TN)
    for pair in range(pairs):
        col = pl.multiple_of(group * (pairs * 128) + pair * 128, 128)
        grads[rows, pl.ds(col, 128)] = (dq[pair] * DH**-0.5).astype(BF16)
        grads[rows, pl.ds(D + col, 128)] = dk[pair].astype(BF16)
        grads[rows, pl.ds(2 * D + col, 128)] = dv[pair].astype(BF16)


def first_kernel(x, lens, wqkv, bqkv, wout, bout, qkv, ctx, r1, lse, key_feat, query_feat):
    for row in range(x.shape[0] // L):
        ends, total = [], 0
        for item in range(lens.shape[1]):
            total = total + lens[row, item]
            ends.append(total)
        features(ends, key_feat, query_feat, row * L)

        rows = pl.ds(row * L, L)
        for part in range(3):
            cols = pl.ds(part * D, D)
            acc = mm(x[rows, :], wqkv[:, cols]) + bqkv[:, cols]
            if part == 0:
                acc = acc * DH**-0.5
            qkv[rows, cols] = acc.astype(BF16)

        def heads(group, carry):
            attend(rows, group, 3, qkv, ctx, lse, key_feat, query_feat)
            return carry

        lax.fori_loop(0, 2, heads, 0)
        r1[rows, :] = mm(ctx[rows, :], wout[...]) + bout[...] + x[rows, :].astype(F32)


def middle_kernel(
    r1, ctx, cot, vecs, wup, bup, wdown, wout,
    y, dr1, dctx, downg, upg, outg, vec_grads, upb_grad,
    fb, act, slope, acc, dfb, dab,
):
    tokens = r1.shape[0]
    step = 256
    parts = tokens // step
    width = 768
    chunks = wup.shape[1] // width
    g1, s1, g2, s2, bd = (vecs[i : i + 1, :] for i in range(5))
    vec_grads[...] = jnp.zeros_like(vec_grads)
    upb_grad[...] = jnp.zeros_like(upb_grad)

    def lead(i, carry):
        rows = pl.ds(pl.multiple_of(i * step, step), step)
        normed, _ = norm_parts(r1[rows, :])
        first = normed * g1 + s1
        fb[rows, :] = first.astype(BF16)
        acc[rows, :] = first + bd
        return carry

    lax.fori_loop(0, parts, lead, 0)

    def forward(c, carry):
        cols = pl.ds(pl.multiple_of(c * width, width), width)
        u, e = [None] * parts, [None] * parts
        for s in range(parts + 2):
            if s < parts:
                u[s] = mm(fb[s * step : (s + 1) * step, :], wup[:, cols]) + bup[:, cols]
            if 0 <= s - 1 < parts:
                j = s - 1
                rows = slice(j * step, (j + 1) * step)
                cdf, pdf = normal_parts(u[j])
                e[j] = (u[j] * cdf).astype(BF16)
                act[rows, cols] = e[j]
                slope[rows, cols] = (cdf + u[j] * pdf).astype(BF16)
            if 0 <= s - 2 < parts:
                j = s - 2
                acc[j * step : (j + 1) * step, :] += mm(e[j], wdown[cols, :])
        return carry

    lax.fori_loop(0, chunks, forward, 0)

    def second(i, carry):
        rows = pl.ds(pl.multiple_of(i * step, step), step)
        normed, scale = norm_parts(acc[rows, :])
        y[rows, :] = (normed * g2 + s2).astype(BF16)
        dy = cot[rows, :].astype(F32)
        dr2 = norm_back(dy, normed, scale, g2)
        acc[rows, :] = dr2
        low = dr2.astype(BF16)
        dfb[rows, :] = low
        vec_grads[0:1, :] += jnp.sum(dy * normed, axis=0, keepdims=True)
        vec_grads[1:2, :] += jnp.sum(dy, axis=0, keepdims=True)
        vec_grads[2:3, :] += jnp.sum(low.astype(F32), axis=0, keepdims=True)
        return carry

    lax.fori_loop(0, parts, second, 0)

    def down(c, carry):
        cols = pl.ds(pl.multiple_of(c * width, width), width)
        downg[:, cols] = mm(dfb[...], act[:, cols], TN).astype(BF16)
        return carry

    lax.fori_loop(0, chunks, down, 0)

    def backward(c, carry):
        cols = pl.ds(pl.multiple_of(c * width, width), width)
        de, du = [None] * parts, [None] * parts
        sums = jnp.zeros((1, width), F32)
        for s in range(parts + 2):
            if s < parts:
                de[s] = mm(dfb[s * step : (s + 1) * step, :], wdown[cols, :], NT)
            if 0 <= s - 1 < parts:
                j = s - 1
                rows = slice(j * step, (j + 1) * step)
                du[j] = (de[j] * slope[rows, cols].astype(F32)).astype(BF16)
                slope[rows, cols] = du[j]
                sums = sums + jnp.sum(du[j].astype(F32), axis=0, keepdims=True)
            if 0 <= s - 2 < parts:
                j = s - 2
                acc[j * step : (j + 1) * step, :] += mm(du[j], wup[:, cols], NT)
        upb_grad[:, cols] = sums
        return carry

    lax.fori_loop(0, chunks, backward, 0)

    def third(i, carry):
        rows = pl.ds(pl.multiple_of(i * step, step), step)
        normed, scale = norm_parts(r1[rows, :])
        grad = acc[rows, :]
        dr = norm_back(grad, normed, scale, g1)
        dr1[rows, :] = dr
        low = dr.astype(BF16)
        dab[rows, :] = low
        vec_grads[3:4, :] += jnp.sum(grad * normed, axis=0, keepdims=True)
        vec_grads[4:5, :] += jnp.sum(grad, axis=0, keepdims=True)
        vec_grads[5:6, :] += jnp.sum(low.astype(F32), axis=0, keepdims=True)
        return carry

    lax.fori_loop(0, parts, third, 0)
    dctx[...] = mm(dab[...], wout[...], NT).astype(BF16)
    outg[...] = mm(ctx[...], dab[...], TN).astype(BF16)

    def up(c, carry):
        cols = pl.ds(pl.multiple_of(c * width, width), width)
        upg[:, cols] = mm(fb[...], slope[:, cols], TN).astype(BF16)
        return carry

    lax.fori_loop(0, chunks, up, 0)


def last_kernel(x, lens, qkv, ctx, dctx, lse, dr1, wqkv, xg, qkvg, vec_grads, grads, key_feat, query_feat):
    vec_grads[...] = jnp.zeros_like(vec_grads)
    for row in range(x.shape[0] // L):
        ends, total = [], 0
        for item in range(lens.shape[1]):
            total = total + lens[row, item]
            ends.append(total)
        features(ends, key_feat, query_feat, row * L)

        rows = pl.ds(row * L, L)

        def heads(group, carry):
            attend_back(rows, group, 3, qkv, ctx, dctx, lse[group, rows, :], grads, key_feat, query_feat)
            return carry

        lax.fori_loop(0, 2, heads, 0)
    vec_grads[0:1, :] = jnp.sum(grads[:, 0:D].astype(F32), axis=0, keepdims=True)
    vec_grads[1:2, :] = jnp.sum(grads[:, 2 * D : 3 * D].astype(F32), axis=0, keepdims=True)
    for part in range(3):
        cols = slice(part * D, (part + 1) * D)
        qkvg[:, cols] = mm(x[...], grads[:, cols], TN).astype(BF16)
    xg[...] = (mm(grads[...], wqkv[...], NT) + dr1[...]).astype(xg.dtype)


MESH = pl.DeviceIdType.MESH


def load(source, target, sem):
    copy = pltpu.make_async_copy(source, target, sem)
    copy.start()
    return copy


def send(source, target, out_sem, in_sem, device):
    copy = pltpu.make_async_remote_copy(
        src_ref=source, dst_ref=target, send_sem=out_sem, recv_sem=in_sem,
        device_id=device, device_id_type=MESH,
    )
    copy.start()
    return copy


def arrived(target, in_sem, device):
    pltpu.make_async_remote_copy(
        src_ref=target, dst_ref=target, send_sem=in_sem, recv_sem=in_sem,
        device_id=device, device_id_type=MESH,
    ).wait_recv()


def meet(devices):
    barrier = pltpu.get_barrier_semaphore()
    for device in devices:
        pl.semaphore_signal(barrier, inc=1, device_id=device, device_id_type=MESH)
    pl.semaphore_wait(barrier, len(devices))


def gather_kernel(
    hidden, cotan, lens, wqkv_in, bq, bv, wout_in, bout,
    x_out, cot_out, qkv_out, ctx_out, r1_out, lse_out,
    x, qkv, ctx, r1, lse, wqkv, wout, key_feat, query_feat,
    load_sem, own_sem, keep_sem, out_sems, in_sems,
):
    me = lax.axis_index("heads")
    row_id = lax.axis_index("rows")
    heads = lax.axis_size("heads")
    part = hidden.shape[1]
    rows_mine = x.shape[0] // L
    loads = [load(wqkv_in, wqkv, load_sem.at[0]), load(wout_in, wout, load_sem.at[1])]
    others = [lax.rem(me + step, heads) for step in range(1, heads)]
    device = lambda other: {"rows": row_id, "heads": other}
    meet([device(other) for other in others])
    sent, kept = [], []
    for kind, (source, target) in enumerate(((hidden, x), (cotan, cot_out))):
        for row in range(rows_mine):
            place = pl.ds(row * L + me * part, part)
            for step, other in enumerate(others):
                sent.append(
                    send(
                        source.at[other * rows_mine + row], target.at[place], out_sems.at[kind, row, step],
                        in_sems.at[kind, row, me], device(other),
                    )
                )
            kept.append(load(source.at[me * rows_mine + row], target.at[place], own_sem.at[kind, row]))
    for row in range(rows_mine):
        ends, total = [], 0
        for item in range(lens.shape[1]):
            total = total + lens[me * rows_mine + row, item]
            ends.append(total)
        features(ends, key_feat, query_feat, row * L)
    stores = []
    for row in range(rows_mine):
        rows = pl.ds(row * L, L)
        kept[row].wait()
        for other in others:
            arrived(x.at[pl.ds(row * L + other * part, part)], in_sems.at[0, row, other], device(other))
        stores.append(load(x.at[rows], x_out.at[rows], keep_sem.at[0, row]))
        if row == 0:
            loads[0].wait()
        for item in range(3):
            cols = pl.ds(item * D, D)
            acc = mm(x[rows, :], wqkv[:, cols])
            if item == 0:
                acc = (acc + bq[...].astype(F32)) * DH**-0.5
            if item == 2:
                acc = acc + bv[...].astype(F32)
            qkv[rows, cols] = acc.astype(BF16)
        stores.append(load(qkv.at[rows], qkv_out.at[rows], keep_sem.at[1, row]))

        def group_heads(group, carry):
            attend(rows, group, 3, qkv, ctx, lse, key_feat, query_feat)
            return carry

        lax.fori_loop(0, 2, group_heads, 0)
        stores.append(load(ctx.at[rows], ctx_out.at[rows], keep_sem.at[2, row]))
        stores.append(load(lse.at[:, rows], lse_out.at[:, rows], keep_sem.at[3, row]))
        if row == 0:
            loads[1].wait()
        r1[rows, :] = mm(ctx[rows, :], wout[...]) + bout[...].astype(F32) + x[rows, :].astype(F32)
        stores.append(load(r1.at[rows], r1_out.at[rows], keep_sem.at[4, row]))
    for row in range(rows_mine):
        kept[rows_mine + row].wait()
        for other in others:
            arrived(cot_out.at[pl.ds(row * L + other * part, part)], in_sems.at[1, row, other], device(other))
    for copy in sent:
        copy.wait_send()
    for copy in stores:
        copy.wait()


class Place:
    def __init__(self):
        self.row, self.head = lax.axis_index("rows"), lax.axis_index("heads")
        self.z, self.y = self.row // 2, lax.rem(self.row, 2)
        self.x, self.c = self.head // 2, lax.rem(self.head, 2)
        self.over = {
            "c": self.at(c=1 - self.c), "y": self.at(y=1 - self.y), "x": self.at(x=1 - self.x),
        }

    def at(self, **new):
        z, y, x, c = (new.get(name, getattr(self, name)) for name in "zyxc")
        return {"rows": z * 2 + y, "heads": x * 2 + c}

    def turn(self, step):
        return lax.rem(self.z + step, 4)


class Total:
    def __init__(self, where, order, got, mid, far, near, sems):
        self.where, self.order = where, order
        self.got, self.mid, self.far, self.near = got, mid, far, near
        self.core_out, self.core_in, self.out, self.inn, self.z_out, self.z_in, self.end = sems
        self.open = []

    @staticmethod
    def scratch(order, rows, cols):
        if order == "yzx":
            shapes = [(2, 4, 2, rows, cols), (2, 4, rows, cols), (4, 2, rows, cols), (rows, cols)]
        else:
            shapes = [(2, 4, 2, rows, cols), (4, 2, rows, cols), (4, rows, cols), (4, rows, cols)]
        sems = [(4,), (4,), (2, 4), (2, 4), (4,), (4,), (2,)]
        return [pltpu.VMEM(dims, BF16) for dims in shapes] + [pltpu.SemaphoreType.DMA(dims) for dims in sems]

    def core_send(self, index, source, target):
        self.open.append(
            send(source, target, self.core_out.at[index], self.core_in.at[index], self.where.over["c"])
        )

    def core_wait(self, index, target):
        arrived(target, self.core_in.at[index], self.where.over["c"])

    def first(self, step):
        w = self.where
        z = w.turn(step + 1)
        if self.order == "yzx":
            source, target = self.got.at[:, z, 1 - w.y], self.mid.at[:, z]
        else:
            source, target = self.got.at[1 - w.x, z], self.mid.at[z]
        self.open.append(
            send(source, target, self.out.at[0, step], self.inn.at[0, step], w.over[self.order[0]])
        )

    def second(self, step):
        w = self.where
        z = w.turn(step + 1)
        if self.order == "yzx":
            arrived(self.mid.at[:, z], self.inn.at[0, step], w.over["y"])
            self.mid[:, z] = (self.mid[:, z].astype(F32) + self.got[:, z, w.y].astype(F32)).astype(BF16)
            self.z_send(step, self.mid.at[:, z])
        else:
            arrived(self.mid.at[z], self.inn.at[0, step], w.over["x"])
            self.mid[z] = (self.mid[z].astype(F32) + self.got[w.x, z].astype(F32)).astype(BF16)
            self.open.append(
                send(
                    self.mid.at[z, 1 - w.y], self.far.at[z], self.out.at[1, step], self.inn.at[1, step],
                    w.over["y"],
                )
            )

    def third(self, step):
        w = self.where
        z = w.turn(step + 1)
        arrived(self.far.at[z], self.inn.at[1, step], w.over["y"])
        self.far[z] = (self.far[z].astype(F32) + self.mid[z, w.y].astype(F32)).astype(BF16)
        self.z_send(step, self.far.at[z])

    def z_send(self, step, source):
        w = self.where
        if step < 3:
            target = self.far if self.order == "yzx" else self.near
            self.open.append(
                send(
                    source, target.at[w.z], self.z_out.at[step], self.z_in.at[w.z],
                    w.at(z=w.turn(step + 1)),
                )
            )

    def z_sum(self):
        w = self.where
        slots = self.far if self.order == "yzx" else self.near
        total = (self.mid[:, w.z] if self.order == "yzx" else self.far[w.z]).astype(F32)
        for step in range(3):
            z = w.turn(step + 1)
            arrived(slots.at[z], self.z_in.at[z], w.at(z=z))
            total = total + slots[z].astype(F32)
        return total

    def fourth(self):
        w = self.where
        self.far[w.z] = self.z_sum().astype(BF16)
        self.open.append(
            send(self.far.at[w.z, 1 - w.x], self.near, self.end.at[0], self.end.at[1], w.over["x"])
        )

    def result(self):
        w = self.where
        if self.order == "xyz":
            return self.z_sum()
        arrived(self.near, self.end.at[1], w.over["x"])
        return self.far[w.z, w.x].astype(F32) + self.near[...].astype(F32)

    def core_done(self):
        for copy in self.open:
            copy.wait_send()
        self.open = []


class Everyone:
    def __init__(self, where, slots, got, all_z, sems):
        self.where, self.slots, self.got, self.all_z, self.sems = where, slots, got, all_z, sems
        self.open = []

    @staticmethod
    def scratch(rows):
        return [
            pltpu.VMEM((4, rows, D), F32), pltpu.VMEM((3, rows, D), F32), pltpu.VMEM((4, rows, D), F32),
            pltpu.SemaphoreType.DMA((4, 6)),
        ]

    def start(self, level):
        w = self.where
        self.open.append(
            send(
                self.slots.at[level], self.got.at[level], self.sems.at[0, level], self.sems.at[1, level],
                w.over["cyx"[level]],
            )
        )

    def step(self, level):
        w = self.where
        arrived(self.got.at[level], self.sems.at[1, level], w.over["cyx"[level]])
        self.slots[level + 1] = self.slots[level] + self.got[level]
        if level < 2:
            self.start(level + 1)
            return
        self.all_z[w.z] = self.slots[3]
        for step in range(3):
            z = w.turn(step + 1)
            self.open.append(
                send(
                    self.slots.at[3], self.all_z.at[w.z], self.sems.at[2, step], self.sems.at[3, w.z],
                    w.at(z=z),
                )
            )

    def result(self):
        w = self.where
        for step in range(3):
            z = w.turn(step + 1)
            arrived(self.all_z.at[z], self.sems.at[3, z], w.at(z=z))
        for copy in self.open:
            copy.wait_send()
        return (self.all_z[0] + self.all_z[1]) + (self.all_z[2] + self.all_z[3])


def rest_kernel(
    scale,
    r1_in, cot_in, ctx_in, qkv_in, lse_in, x_in, lens, wup_in, wdown_in, wout_in, wqkv_in,
    g1v, s1v, g2v, s2v, bdv, bup,
    lay, xgr, downo, upo, outo, qkvo, vec_out, upb_out,
    r1, ycot, fb, act, slope, acc, dfb, dfbt, wup, wdown, wout, key_feat, query_feat, down_send,
    load_sem, lay_sem, xg_sem, own_sem,
    *scratch,
):
    where = Place()
    w = where
    scratch = list(scratch)

    def take(count):
        return [scratch.pop(0) for _ in range(count)]

    totals = []
    for order in ("yzx", "xyz", "yzx", "yzx", "xyz"):
        refs = take(11)
        totals.append(Total(where, order, *refs[:4], refs[4:]))
    down, up, out, qkva, qkvb = totals
    everyone = Everyone(where, *take(4))

    loads = [
        load(r1_in, r1, load_sem.at[0]), load(wup_in, wup, load_sem.at[1]), load(wdown_in, wdown, load_sem.at[2]),
        load(cot_in, ycot, load_sem.at[3]), load(wout_in, wout, load_sem.at[4]),
    ]
    peers = [where.at(x=1 - w.x), where.over["c"], where.at(x=1 - w.x, c=1 - w.c), where.over["y"]]
    peers += [where.at(z=where.turn(step)) for step in (1, 2, 3)]
    meet(peers)

    tokens = r1.shape[0]
    step_rows = 256
    parts = tokens // step_rows
    width = 768
    chunks = wup_in.shape[1] // width
    rows_mine = tokens // L
    part = lay.shape[1]
    g1, s1, g2, s2, bd = (item[...].astype(F32) for item in (g1v, s1v, g2v, s2v, bdv))
    mine = everyone.slots.at[0]
    mine[...] = jnp.zeros(mine.shape, F32)
    others = [lax.rem(w.head + step, 4) for step in range(1, 4)]

    for row in range(rows_mine):
        ends, total = [], 0
        for item in range(lens.shape[1]):
            total = total + lens[w.head * rows_mine + row, item]
            ends.append(total)
        features(ends, key_feat, query_feat, row * L)

    loads[0].wait()

    def lead(i, carry):
        rows = pl.ds(pl.multiple_of(i * step_rows, step_rows), step_rows)
        normed, _ = norm_parts(r1[rows, :])
        first = normed * g1 + s1
        fb[rows, :] = first.astype(BF16)
        acc[rows, :] = first + bd
        return carry

    lax.fori_loop(0, parts, lead, 0)
    loads[1].wait()
    loads[2].wait()

    def forward(c, carry):
        cols = pl.ds(pl.multiple_of(c * width, width), width)
        u, e = [None] * parts, [None] * parts
        for s in range(parts + 2):
            if s < parts:
                u[s] = mm(fb[s * step_rows : (s + 1) * step_rows, :], wup[:, cols]) + bup[:, cols].astype(F32)
            if 0 <= s - 1 < parts:
                j = s - 1
                rows = slice(j * step_rows, (j + 1) * step_rows)
                cdf, pdf = normal_parts(u[j])
                e[j] = (u[j] * cdf).astype(BF16)
                act[rows, cols] = e[j]
                slope[rows, cols] = (cdf + u[j] * pdf).astype(BF16)
            if 0 <= s - 2 < parts:
                j = s - 2
                acc[j * step_rows : (j + 1) * step_rows, :] += mm(e[j], wdown[cols, :])
        return carry

    lax.fori_loop(0, chunks, forward, 0)
    loads[3].wait()

    def second(i, carry):
        rows = pl.ds(pl.multiple_of(i * step_rows, step_rows), step_rows)
        normed, spread = norm_parts(acc[rows, :])
        dy = ycot[rows, :].astype(F32)
        ycot[rows, :] = (normed * g2 + s2).astype(BF16)
        dr2 = norm_back(dy, normed, spread, g2)
        acc[rows, :] = dr2
        low = dr2.astype(BF16)
        dfb[rows, :] = low
        dfbt[:, :, rows] = low.T.reshape(4, D // 4, step_rows)
        mine[0:1, :] += jnp.sum(dy * normed, axis=0, keepdims=True)
        mine[1:2, :] += jnp.sum(dy, axis=0, keepdims=True)
        mine[2:3, :] += jnp.sum(low.astype(F32), axis=0, keepdims=True)
        return carry

    lax.fori_loop(0, parts, second, 0)

    def give_back(source, target, sems, row):
        copies = []
        slot = w.head * rows_mine + row
        for step, other in enumerate(others):
            tokens_there = source.at[pl.ds(row * L + other * part, part)]
            copies.append(
                send(
                    tokens_there, target.at[slot], sems.at[0, row, step], sems.at[1, row, w.head],
                    {"rows": w.row, "heads": other},
                )
            )
        return copies

    def taken_back(target, sems):
        for row in range(rows_mine):
            for other in others:
                arrived(target.at[other * rows_mine + row], sems.at[1, row, other], {"rows": w.row, "heads": other})

    sent, kept = [], []
    for row in range(rows_mine):
        sent += give_back(ycot, lay, lay_sem, row)
        kept.append(
            load(ycot.at[pl.ds(row * L + w.head * part, part)], lay.at[w.head * rows_mine + row], own_sem.at[0, row])
        )

    def down_half(core, z):
        left = jnp.concatenate([dfbt[core], dfbt[2 + core]], axis=0)
        cols = pl.ds(pl.multiple_of(z * width, width), width)
        return mm(left, act[:, cols])

    quarter, eighth = D // 4, width // 2
    for step in range(4):
        z = where.turn(step + 1)
        total = down_half(1 - w.c, z)
        for x in range(2):
            for y in range(2):
                piece = total[x * quarter : (x + 1) * quarter, y * eighth : (y + 1) * eighth]
                down_send[x, z, y] = piece.astype(BF16)
        down.core_send(step, down_send.at[:, z], down.got.at[:, z])
    for step in range(4):
        z = where.turn(step + 1)
        total = down_half(w.c, z)
        down.core_wait(step, down.got.at[:, z])
        for x in range(2):
            for y in range(2):
                piece = total[x * quarter : (x + 1) * quarter, y * eighth : (y + 1) * eighth]
                down.got[x, z, y] = (piece + down.got[x, z, y].astype(F32)).astype(BF16)
        down.first(step)
    qkv_load = load(qkv_in, act.at[:, pl.ds(0, 3 * D)], load_sem.at[6])

    def backward(c, carry):
        cols = pl.ds(pl.multiple_of(c * width, width), width)
        de, du = [None] * parts, [None] * parts
        sums = jnp.zeros((1, width), F32)
        for s in range(parts + 2):
            if s < parts:
                de[s] = mm(dfb[s * step_rows : (s + 1) * step_rows, :], wdown[cols, :], NT)
            if 0 <= s - 1 < parts:
                j = s - 1
                rows = slice(j * step_rows, (j + 1) * step_rows)
                du[j] = (de[j] * slope[rows, cols].astype(F32)).astype(BF16)
                slope[rows, cols] = du[j]
                sums = sums + jnp.sum(du[j].astype(F32), axis=0, keepdims=True)
            if 0 <= s - 2 < parts:
                j = s - 2
                acc[j * step_rows : (j + 1) * step_rows, :] += mm(du[j], wup[:, cols], NT)
        mine[pl.ds(3 + c, 1), :] = sums
        return carry

    half = chunks // 2
    lax.fori_loop(0, half, backward, 0)
    down.second(0)
    lax.fori_loop(half, chunks, backward, 0)
    down.second(1)
    wqkv = wup.at[:, pl.ds(0, 3 * D)]
    x = wdown.at[pl.ds(2 * D, tokens)]
    wqkv_load = load(wqkv_in, wqkv, load_sem.at[7])
    x_load = load(x_in, x, load_sem.at[8])
    dab = dfb

    def third(i, carry):
        rows = pl.ds(pl.multiple_of(i * step_rows, step_rows), step_rows)
        normed, spread = norm_parts(r1[rows, :])
        grad = acc[rows, :]
        dr = norm_back(grad, normed, spread, g1)
        acc[rows, :] = dr
        low = dr.astype(BF16)
        dab[rows, :] = low
        mine[7:8, :] += jnp.sum(grad * normed, axis=0, keepdims=True)
        mine[8:9, :] += jnp.sum(grad, axis=0, keepdims=True)
        mine[9:10, :] += jnp.sum(low.astype(F32), axis=0, keepdims=True)
        return carry

    lax.fori_loop(0, parts, third, 0)
    lse_load = [load(lse_in.at[g], r1.at[:, pl.ds(g * 128, 128)], load_sem.at[10 + g]) for g in range(2)]

    def up_half(core, x_side):
        cols = pl.ds(pl.multiple_of((2 * x_side + core) * width, width), width)
        return mm(fb[...], slope[:, cols], TN)

    for side in range(2):
        wdown[side * D : (side + 1) * D, :] = up_half(1 - w.c, side).astype(BF16)
        up.core_send(side, wdown.at[pl.ds(side * D, D)], up.got.at[side].reshape(D, width))
    down.second(2)
    for turn in (1, 0):
        side = w.x if turn == 0 else 1 - w.x
        total = up_half(w.c, side).reshape(4, 2, D // 8, width)
        if turn == 1:
            for item in range(2):
                up.core_wait(item, up.got.at[item])
        up.got[side] = (total + up.got[side].astype(F32)).astype(BF16)
        if turn == 1:
            for step in range(4):
                up.first(step)
    down.second(3)
    ctx = slope.at[:, pl.ds(3 * D, D)]
    grads = slope.at[:, pl.ds(0, 3 * D)]
    dctx = act.at[:, pl.ds(3 * D, D)]
    ctx_load = load(ctx_in, ctx, load_sem.at[9])
    loads[4].wait()
    dctx[...] = mm(dab[...], wout[...], NT).astype(BF16)
    ctx_load.wait()

    def out_half(core, side):
        cols = pl.ds(pl.multiple_of(384 * side + 128 * core, 128), 256)
        return mm(ctx[...], dab[:, cols], TN)

    wqkv_load.wait()
    for side in range(2):
        spot = wup.at[:, pl.ds(3 * D + 256 * side, 256)]
        spot[...] = out_half(1 - w.c, side).astype(BF16)
        out.core_send(side, spot, out.got.at[side].reshape(D, 256))
    for side in range(2):
        total = out_half(w.c, side).reshape(4, 2, D // 8, 256)
        out.core_wait(side, out.got.at[side])
        out.got[side] = (total + out.got[side].astype(F32)).astype(BF16)
    for step in range(4):
        out.first(step)

    qkv = act.at[:, pl.ds(0, 3 * D)]
    qkv_load.wait()
    for copy in lse_load:
        copy.wait()

    def heads_back(row, group):
        rows = pl.ds(row * L, L)
        keep = r1[rows, group * 128 : (group + 1) * 128]
        attend_back(rows, group, 3, qkv, ctx, dctx, keep, grads, key_feat, query_feat)

    heads_back(0, 0)
    down.fourth()
    up.second(0)
    heads_back(0, 1)
    up.second(1)
    out.second(0)
    out.second(1)
    heads_back(1, 0)
    up.second(2)
    up.third(0)
    out.second(2)
    out.second(3)
    downo[...] = (down.result() * scale).T
    heads_back(1, 1)
    up.second(3)
    up.third(1)
    out.fourth()

    mine[10:11, :] = jnp.sum(grads[:, 0:D].astype(F32), axis=0, keepdims=True)
    mine[11:12, :] = jnp.sum(grads[:, 2 * D : 3 * D].astype(F32), axis=0, keepdims=True)
    everyone.start(0)
    x_load.wait()

    def qkv_half(core, side):
        cols = pl.ds(pl.multiple_of(1152 * side + 512 * core, 128), 640)
        return mm(x[...], grads[:, cols], TN).reshape(4, 2, 2, D // 16, 640)

    up.core_done()
    for side in range(2):
        total = qkv_half(1 - w.c, side).astype(BF16)
        for index, each in enumerate((qkva, qkvb)):
            spot = wdown.at[pl.ds(side * D + index * (D // 2), D // 2), pl.ds(0, 640)]
            spot[...] = total[:, :, index].reshape(D // 2, 640)
            each.core_send(side, spot, each.got.at[side].reshape(D // 2, 640))
    up.third(2)
    everyone.step(0)
    for turn in (1, 0):
        side = w.x if turn == 0 else 1 - w.x
        total = qkv_half(w.c, side)
        for each, item in ((qkva, 0), (qkvb, 1)):
            if turn == 1:
                for index in range(2):
                    each.core_wait(index, each.got.at[index])
            each.got[side] = (total[:, :, item] + each.got[side].astype(F32)).astype(BF16)
        if turn == 1:
            for step in range(4):
                qkvb.first(step)
    for step in range(4):
        qkva.first(step)
    up.third(3)
    everyone.step(1)
    outo[...] = pick(out.result() * scale, w.c, 192)
    for row in range(rows_mine):
        rows = pl.ds(row * L, L)
        fb[rows, :] = (mm(grads[rows, :], wqkv[...], NT) + acc[rows, :]).astype(BF16)
        sent += give_back(fb, xgr, xg_sem, row)
        kept.append(
            load(fb.at[pl.ds(row * L + w.head * part, part)], xgr.at[w.head * rows_mine + row], own_sem.at[1, row])
        )
        if row == 0:
            everyone.step(2)
            qkva.second(0)
            qkvb.second(0)
    for step in range(1, 4):
        qkva.second(step)
        qkvb.second(step)
    for step in range(4):
        qkvb.third(step)
    upo[...] = up.result() * scale
    vectors = everyone.result() * scale
    for index, item in enumerate((10, 11, 9, 7, 8, 2, 0, 1)):
        vec_out[index] = vectors[item : item + 1, :]
    for index in range(4):
        upb_out[:, index * width : (index + 1) * width] = vectors[3 + index : 4 + index, :]
    qkva.fourth()
    qkvo[D // 16 :, :] = pick(qkvb.result() * scale, w.c, 576)
    qkvo[0 : D // 16, :] = pick(qkva.result() * scale, w.c, 576)
    taken_back(lay, lay_sem)
    taken_back(xgr, xg_sem)
    for copy in sent:
        copy.wait_send()
    for copy in kept:
        copy.wait()
    for total in totals:
        total.core_done()


def pick(values, core, width):
    return jnp.where(core == 0, values[:, :width], values[:, 64 : 64 + width])


VMEM = pl.BlockSpec(memory_space=pltpu.VMEM)
SMEM = pl.BlockSpec(memory_space=pltpu.SMEM)


def shape(dims, kind):
    return jax.ShapeDtypeStruct(dims, kind)


def params(**more):
    return pltpu.CompilerParams(vmem_limit_bytes=63 * 2**20, **more)


def local(
    hidden_in, lengths, qkv_weight, query_bias, value_bias, out_weight, out_bias, gain_one,
    shift_one, up_weight, up_bias, down_weight, down_bias, gain_two, shift_two, cotangent,
):
    row_count, part_len = hidden_in.shape[0], hidden_in.shape[1]
    heads = lax.axis_size("heads")
    mine = row_count // heads
    tokens = mine * L
    ff = up_weight.shape[1]
    place = lax.axis_index("heads")
    x = lax.all_to_all(hidden_in, "heads", split_axis=0, concat_axis=1, tiled=True).reshape(tokens, D)
    cot = lax.all_to_all(cotangent, "heads", split_axis=0, concat_axis=1, tiled=True).reshape(tokens, D)
    lens = lax.dynamic_slice_in_dim(lengths, place * mine, mine, 0)
    bqkv = jnp.concatenate([query_bias, jnp.zeros_like(query_bias), value_bias]).astype(F32)[None]
    qkv, ctx, r1, lse = pl.pallas_call(
        first_kernel,
        out_shape=(
            shape((tokens, 3 * D), BF16), shape((tokens, D), BF16), shape((tokens, D), F32),
            shape((2, tokens, 128), F32),
        ),
        in_specs=[VMEM, SMEM] + [VMEM] * 4,
        out_specs=(VMEM,) * 4,
        scratch_shapes=[pltpu.VMEM((tokens, 128), BF16)] * 2,
        compiler_params=params(),
        name="first",
    )(x, lens, qkv_weight, bqkv, out_weight, out_bias.astype(F32)[None])
    vecs = jnp.stack([gain_one, shift_one, gain_two, shift_two, down_bias]).astype(F32)
    y, dr1, dctx, downg, upg, outg, vec_mid, upb = pl.pallas_call(
        middle_kernel,
        out_shape=(
            shape((tokens, D), BF16), shape((tokens, D), F32), shape((tokens, D), BF16),
            shape((D, ff), BF16), shape((D, ff), BF16), shape((D, D), BF16),
            shape((8, D), F32), shape((1, ff), F32),
        ),
        in_specs=[VMEM] * 8,
        out_specs=(VMEM,) * 8,
        scratch_shapes=[
            pltpu.VMEM((tokens, D), BF16), pltpu.VMEM((tokens, ff), BF16), pltpu.VMEM((tokens, ff), BF16),
            pltpu.VMEM((tokens, D), F32), pltpu.VMEM((tokens, D), BF16), pltpu.VMEM((tokens, D), BF16),
        ],
        compiler_params=params(),
        name="middle",
    )(r1, ctx, cot, vecs, up_weight, up_bias.astype(F32)[None], down_weight, out_weight)
    xg, qkvg, vec_last = pl.pallas_call(
        last_kernel,
        out_shape=(shape((tokens, D), BF16), shape((D, 3 * D), BF16), shape((8, D), F32)),
        in_specs=[VMEM, SMEM] + [VMEM] * 6,
        out_specs=(VMEM,) * 3,
        scratch_shapes=[pltpu.VMEM((tokens, 3 * D), BF16)] + [pltpu.VMEM((tokens, 128), BF16)] * 2,
        compiler_params=params(),
        name="last",
    )(x, lens, qkv, ctx, dctx, lse, dr1, qkv_weight)

    def back(values):
        values = values.reshape(mine, L, D)
        return lax.all_to_all(values, "heads", split_axis=1, concat_axis=0, tiled=True)

    layer_out = back(y)
    input_grad = back(xg).astype(F32)
    scale = 1.0 / (row_count * lax.axis_size("rows"))
    vec_mid, vec_last, upb = lax.psum((vec_mid, vec_last, upb), ("rows", "heads"))

    def reduce(values, flip):
        one, two = (0, 1) if flip else (1, 0)
        half = lax.psum_scatter(values, "heads", scatter_dimension=one, tiled=True).astype(F32)
        total = lax.psum_scatter(half, "rows", scatter_dimension=two, tiled=True) * scale
        return total.T if flip else total

    vm, vl = vec_mid * scale, vec_last * scale
    return (
        layer_out, input_grad, reduce(qkvg, False), vl[0], vl[1], reduce(outg, False), vm[5], vm[3], vm[4],
        reduce(upg, False), upb[0] * scale, reduce(downg, True), vm[2], vm[0], vm[1],
    )


ANY = pl.BlockSpec(memory_space=pl.ANY)
DMA = pltpu.SemaphoreType.DMA


def local_fast(
    hidden_in, lengths, qkv_weight, query_bias, value_bias, out_weight, out_bias, gain_one,
    shift_one, up_weight, up_bias, down_weight, down_bias, gain_two, shift_two, cotangent,
):
    row_count, part_len = hidden_in.shape[0], hidden_in.shape[1]
    mine = row_count // lax.axis_size("heads")
    heads = lax.axis_size("heads")
    tokens = mine * L
    ff = up_weight.shape[1]
    flat = lambda item: item[None]
    x, cot, qkv, ctx, r1, lse = pl.pallas_call(
        gather_kernel,
        out_shape=(
            shape((tokens, D), BF16), shape((tokens, D), BF16), shape((tokens, 3 * D), BF16),
            shape((tokens, D), BF16), shape((tokens, D), F32), shape((2, tokens, 128), F32),
        ),
        in_specs=[ANY, ANY, SMEM, ANY, VMEM, VMEM, ANY, VMEM],
        out_specs=(ANY,) * 6,
        scratch_shapes=[
            pltpu.VMEM((tokens, D), BF16), pltpu.VMEM((tokens, 3 * D), BF16), pltpu.VMEM((tokens, D), BF16),
            pltpu.VMEM((tokens, D), F32), pltpu.VMEM((2, tokens, 128), F32), pltpu.VMEM((D, 3 * D), BF16),
            pltpu.VMEM((D, D), BF16), pltpu.VMEM((tokens, 128), BF16), pltpu.VMEM((tokens, 128), BF16),
            DMA((2,)), DMA((2, mine)), DMA((5, mine)), DMA((2, mine, heads - 1)), DMA((2, mine, heads)),
        ],
        compiler_params=params(collective_id=0, has_side_effects=True),
        name="gather",
    )(hidden_in, cotangent, lengths, qkv_weight, flat(query_bias), flat(value_bias), out_weight, flat(out_bias))
    scale = 1.0 / (row_count * lax.axis_size("rows"))
    bf = lambda *dims: pltpu.VMEM(dims, BF16)
    totals = []
    for order, rows, cols in (
        ("yzx", 192, 384), ("xyz", 96, 768), ("yzx", 96, 256), ("yzx", 48, 640), ("xyz", 48, 640),
    ):
        totals += Total.scratch(order, rows, cols)
    lay, xgr, downg, upg, outg, qkvg, vec, upb = pl.pallas_call(
        functools.partial(rest_kernel, scale),
        out_shape=(
            shape((row_count, part_len, D), BF16), shape((row_count, part_len, D), BF16),
            shape((384, 192), F32), shape((96, 768), F32), shape((96, 192), F32), shape((96, 576), F32),
            shape((8, 1, D), F32), shape((1, ff), F32),
        ),
        in_specs=[ANY] * 6 + [SMEM] + [ANY] * 4 + [VMEM] * 6,
        out_specs=(ANY, ANY) + (VMEM,) * 6,
        scratch_shapes=[
            pltpu.VMEM((tokens, D), F32), bf(tokens, D), bf(tokens, D), bf(tokens, ff), bf(tokens, ff),
            pltpu.VMEM((tokens, D), F32), bf(tokens, D), bf(4, D // 4, tokens), bf(D, ff), bf(ff, D), bf(D, D),
            bf(tokens, 128), bf(tokens, 128),
            bf(2, 4, 2, 192, 384), DMA((12,)), DMA((2, mine, 4)), DMA((2, mine, 4)), DMA((2, mine)),
        ]
        + totals
        + Everyone.scratch(16),
        compiler_params=params(collective_id=1, has_side_effects=True),
        name="rest",
    )(
        r1, cot, ctx, qkv, lse, x, lengths, up_weight, down_weight, out_weight, qkv_weight,
        flat(gain_one), flat(shift_one), flat(gain_two), flat(shift_two), flat(down_bias), flat(up_bias),
    )
    vec = [vec[item, 0] for item in range(8)]
    return (
        lay, xgr.astype(F32), qkvg, vec[0], vec[1], outg, vec[2], vec[3], vec[4],
        upg, upb[0], downg, vec[5], vec[6], vec[7],
    )


def solution(mesh):
    split = P("rows", "heads", None)
    grid = P("rows", "heads")
    in_specs = (split, P("rows", None)) + (P(),) * 13 + (split,)
    out_specs = (split, split, grid, P(), P(), grid, P(), P(), P(), grid, P(), grid, P(), P(), P())
    fast = mesh.shape["rows"] == 8 and mesh.shape["heads"] == 4
    return jax.shard_map(
        local_fast if fast else local, mesh=mesh, in_specs=in_specs, out_specs=out_specs, check_vma=False
    )
```

```python
import functools

import jax
import jax.numpy as jnp
from jax import lax
from jax.experimental import pallas as pl
from jax.experimental.pallas import tpu as pltpu
from jax.sharding import PartitionSpec as P

DH = 64
D = 768
L = 512
EPSILON = 1e-12
OFF = -(2.0**100)
F32 = jnp.float32
BF16 = jnp.bfloat16
NN = (((1,), (0,)), ((), ()))
NT = (((1,), (1,)), ((), ()))
TN = (((0,), (0,)), ((), ()))

TAIL = (
    0.09881087227319621,
    0.11230449770687516,
    0.02424904968806795,
    0.2825055677430211,
    -0.268648558796486,
    0.34262844642428514,
    -0.09184987882933851,
)


def mm(left, right, dims=NN):
    return lax.dot_general(left, right, dims, preferred_element_type=F32)


def normal_parts(u):
    bell = jnp.exp(u * u * -0.5)
    t = pltpu.reciprocal(1.0 + 0.25 * jnp.abs(u))
    poly = TAIL[-1]
    for item in TAIL[-2::-1]:
        poly = poly * t + item
    tail = poly * t * bell
    return jnp.where(u >= 0, 1.0 - tail, tail), bell * 0.3989422804014327


def norm_parts(values):
    middle = jnp.mean(values, axis=-1, keepdims=True)
    center = values - middle
    spread = jnp.mean(center * center, axis=-1, keepdims=True)
    scale = lax.rsqrt(spread + EPSILON)
    return center * scale, scale


def norm_back(grad, normed, scale, gain):
    dn = grad * gain
    first = jnp.mean(dn, axis=-1, keepdims=True)
    second = jnp.mean(dn * normed, axis=-1, keepdims=True)
    return (dn - first - normed * second) * scale


def split3(values):
    high = values.astype(BF16)
    rest = values - high.astype(F32)
    mid = rest.astype(BF16)
    return high, mid, (rest - mid.astype(F32)).astype(BF16)


def features(ends, key_feat, query_feat, start):
    token = lax.broadcasted_iota(jnp.int32, (L, 128), 0)
    place = lax.broadcasted_iota(jnp.int32, (L, 128), 1) & (DH - 1)
    seg = jnp.zeros((L, 128), jnp.int32)
    for end in ends:
        seg = seg + (token >= end).astype(jnp.int32)
    count = len(ends)
    ones = (place == seg) | ((place >= count) & (place < count + 3))
    key_feat[pl.ds(start, L), :] = jnp.where(ones, 1.0, 0.0).astype(BF16)
    off = (place < count) & (place != seg)
    query_feat[pl.ds(start, L), :] = jnp.where(off, OFF, 0.0).astype(BF16)


def attend(rows, group, pairs, qkv, ctx, lse, key_feat, query_feat):
    lane = lax.broadcasted_iota(jnp.int32, (1, 128), 1)
    kf, qf = key_feat[rows, :], query_feat[rows, :]
    ops, values = [], []
    for pair in range(pairs):
        col = pl.multiple_of(group * (pairs * 128) + pair * 128, 128)
        q2 = qkv[rows, pl.ds(col, 128)]
        k2 = qkv[rows, pl.ds(D + col, 128)]
        values.append(qkv[rows, pl.ds(2 * D + col, 128)])
        for own in (lane < DH, lane >= DH):
            ops.append((jnp.where(own, q2, qf), jnp.where(own, k2, kf)))
    count = 2 * pairs
    scores = [None] * count
    outs, sums = [], []
    scores[0] = mm(*ops[0], NT)
    for head in range(count):
        if head + 1 < count:
            scores[head + 1] = mm(*ops[head + 1], NT)
        peak = jnp.max(scores[head], axis=1, keepdims=True)
        expo = jnp.exp(scores[head] - peak)
        total = jnp.sum(expo, axis=1, keepdims=True)
        out = mm(expo.astype(BF16), values[head // 2])
        outs.append(out * (1.0 / total))
        sums.append(peak + jnp.log(total))
    keep = jnp.zeros((L, 128), F32)
    for head in range(count):
        keep = jnp.where(lane == head, sums[head], keep)
    lse[group, rows, :] = keep
    for pair in range(pairs):
        col = pl.multiple_of(group * (pairs * 128) + pair * 128, 128)
        both = jnp.where(lane < DH, outs[2 * pair], outs[2 * pair + 1])
        ctx[rows, pl.ds(col, 128)] = both.astype(BF16)


def attend_back(rows, group, pairs, qkv, ctx, dctx, keep, grads, key_feat, query_feat):
    lane = lax.broadcasted_iota(jnp.int32, (1, 128), 1)
    place = lane & (DH - 1)
    kf, qf = key_feat[rows, :], query_feat[rows, :]
    vf = jnp.where((place >= 4) & (place < 7), 1.0, 0.0).astype(BF16)

    def spread(column, base):
        high, mid, small = split3(-column)
        return jnp.where(
            place == 4, high, jnp.where(place == 5, mid, jnp.where(place == 6, small, base))
        )

    ops = []
    for pair in range(pairs):
        col = pl.multiple_of(group * (pairs * 128) + pair * 128, 128)
        q2 = qkv[rows, pl.ds(col, 128)]
        k2 = qkv[rows, pl.ds(D + col, 128)]
        v2 = qkv[rows, pl.ds(2 * D + col, 128)]
        d2 = dctx[rows, pl.ds(col, 128)]
        both = d2.astype(F32) * ctx[rows, pl.ds(col, 128)].astype(F32)
        zero = jnp.zeros_like(q2)
        for side, own in enumerate((lane < DH, lane >= DH)):
            inner = jnp.sum(jnp.where(own, both, 0.0), axis=1, keepdims=True)
            total = keep[:, 2 * pair + side : 2 * pair + side + 1]
            ops.append(
                (
                    jnp.where(own, k2, kf),
                    jnp.where(own, q2, spread(total, qf)),
                    jnp.where(own, v2, vf),
                    jnp.where(own, d2, spread(inner, zero)),
                    jnp.where(own, q2, zero),
                    jnp.where(own, k2, zero),
                    jnp.where(own, d2, zero),
                )
            )
    count = 2 * pairs
    scores, chances = [None] * count, [None] * count
    dq, dk, dv = [0] * pairs, [0] * pairs, [0] * pairs

    def start(head):
        scores[head] = mm(ops[head][0], ops[head][1], NT)
        chances[head] = mm(ops[head][2], ops[head][3], NT)

    start(0)
    for head in range(count):
        if head + 1 < count:
            start(head + 1)
        chance = jnp.exp(scores[head])
        low = chance.astype(BF16)
        ds = (chance * chances[head]).astype(BF16)
        pair = head // 2
        dk[pair] += mm(ds, ops[head][4])
        dv[pair] += mm(low, ops[head][6])
        dq[pair] += mm(ds, ops[head][5], TN)
    for pair in range(pairs):
        col = pl.multiple_of(group * (pairs * 128) + pair * 128, 128)
        grads[rows, pl.ds(col, 128)] = (dq[pair] * DH**-0.5).astype(BF16)
        grads[rows, pl.ds(D + col, 128)] = dk[pair].astype(BF16)
        grads[rows, pl.ds(2 * D + col, 128)] = dv[pair].astype(BF16)


def first_kernel(x, lens, wqkv, bqkv, wout, bout, qkv, ctx, r1, lse, key_feat, query_feat):
    for row in range(x.shape[0] // L):
        ends, total = [], 0
        for item in range(lens.shape[1]):
            total = total + lens[row, item]
            ends.append(total)
        features(ends, key_feat, query_feat, row * L)

        rows = pl.ds(row * L, L)
        for part in range(3):
            cols = pl.ds(part * D, D)
            acc = mm(x[rows, :], wqkv[:, cols]) + bqkv[:, cols]
            if part == 0:
                acc = acc * DH**-0.5
            qkv[rows, cols] = acc.astype(BF16)

        def heads(group, carry):
            attend(rows, group, 3, qkv, ctx, lse, key_feat, query_feat)
            return carry

        lax.fori_loop(0, 2, heads, 0)
        r1[rows, :] = mm(ctx[rows, :], wout[...]) + bout[...] + x[rows, :].astype(F32)


def middle_kernel(
    r1, ctx, cot, vecs, wup, bup, wdown, wout,
    y, dr1, dctx, downg, upg, outg, vec_grads, upb_grad,
    fb, act, slope, acc, dfb, dab,
):
    tokens = r1.shape[0]
    step = 256
    parts = tokens // step
    width = 768
    chunks = wup.shape[1] // width
    g1, s1, g2, s2, bd = (vecs[i : i + 1, :] for i in range(5))
    vec_grads[...] = jnp.zeros_like(vec_grads)
    upb_grad[...] = jnp.zeros_like(upb_grad)

    def lead(i, carry):
        rows = pl.ds(pl.multiple_of(i * step, step), step)
        normed, _ = norm_parts(r1[rows, :])
        first = normed * g1 + s1
        fb[rows, :] = first.astype(BF16)
        acc[rows, :] = first + bd
        return carry

    lax.fori_loop(0, parts, lead, 0)

    def forward(c, carry):
        cols = pl.ds(pl.multiple_of(c * width, width), width)
        u, e = [None] * parts, [None] * parts
        for s in range(parts + 2):
            if s < parts:
                u[s] = mm(fb[s * step : (s + 1) * step, :], wup[:, cols]) + bup[:, cols]
            if 0 <= s - 1 < parts:
                j = s - 1
                rows = slice(j * step, (j + 1) * step)
                cdf, pdf = normal_parts(u[j])
                e[j] = (u[j] * cdf).astype(BF16)
                act[rows, cols] = e[j]
                slope[rows, cols] = (cdf + u[j] * pdf).astype(BF16)
            if 0 <= s - 2 < parts:
                j = s - 2
                acc[j * step : (j + 1) * step, :] += mm(e[j], wdown[cols, :])
        return carry

    lax.fori_loop(0, chunks, forward, 0)

    def second(i, carry):
        rows = pl.ds(pl.multiple_of(i * step, step), step)
        normed, scale = norm_parts(acc[rows, :])
        y[rows, :] = (normed * g2 + s2).astype(BF16)
        dy = cot[rows, :].astype(F32)
        dr2 = norm_back(dy, normed, scale, g2)
        acc[rows, :] = dr2
        low = dr2.astype(BF16)
        dfb[rows, :] = low
        vec_grads[0:1, :] += jnp.sum(dy * normed, axis=0, keepdims=True)
        vec_grads[1:2, :] += jnp.sum(dy, axis=0, keepdims=True)
        vec_grads[2:3, :] += jnp.sum(low.astype(F32), axis=0, keepdims=True)
        return carry

    lax.fori_loop(0, parts, second, 0)

    def down(c, carry):
        cols = pl.ds(pl.multiple_of(c * width, width), width)
        downg[:, cols] = mm(dfb[...], act[:, cols], TN).astype(BF16)
        return carry

    lax.fori_loop(0, chunks, down, 0)

    def backward(c, carry):
        cols = pl.ds(pl.multiple_of(c * width, width), width)
        de, du = [None] * parts, [None] * parts
        sums = jnp.zeros((1, width), F32)
        for s in range(parts + 2):
            if s < parts:
                de[s] = mm(dfb[s * step : (s + 1) * step, :], wdown[cols, :], NT)
            if 0 <= s - 1 < parts:
                j = s - 1
                rows = slice(j * step, (j + 1) * step)
                du[j] = (de[j] * slope[rows, cols].astype(F32)).astype(BF16)
                slope[rows, cols] = du[j]
                sums = sums + jnp.sum(du[j].astype(F32), axis=0, keepdims=True)
            if 0 <= s - 2 < parts:
                j = s - 2
                acc[j * step : (j + 1) * step, :] += mm(du[j], wup[:, cols], NT)
        upb_grad[:, cols] = sums
        return carry

    lax.fori_loop(0, chunks, backward, 0)

    def third(i, carry):
        rows = pl.ds(pl.multiple_of(i * step, step), step)
        normed, scale = norm_parts(r1[rows, :])
        grad = acc[rows, :]
        dr = norm_back(grad, normed, scale, g1)
        dr1[rows, :] = dr
        low = dr.astype(BF16)
        dab[rows, :] = low
        vec_grads[3:4, :] += jnp.sum(grad * normed, axis=0, keepdims=True)
        vec_grads[4:5, :] += jnp.sum(grad, axis=0, keepdims=True)
        vec_grads[5:6, :] += jnp.sum(low.astype(F32), axis=0, keepdims=True)
        return carry

    lax.fori_loop(0, parts, third, 0)
    dctx[...] = mm(dab[...], wout[...], NT).astype(BF16)
    outg[...] = mm(ctx[...], dab[...], TN).astype(BF16)

    def up(c, carry):
        cols = pl.ds(pl.multiple_of(c * width, width), width)
        upg[:, cols] = mm(fb[...], slope[:, cols], TN).astype(BF16)
        return carry

    lax.fori_loop(0, chunks, up, 0)


def last_kernel(x, lens, qkv, ctx, dctx, lse, dr1, wqkv, xg, qkvg, vec_grads, grads, key_feat, query_feat):
    vec_grads[...] = jnp.zeros_like(vec_grads)
    for row in range(x.shape[0] // L):
        ends, total = [], 0
        for item in range(lens.shape[1]):
            total = total + lens[row, item]
            ends.append(total)
        features(ends, key_feat, query_feat, row * L)

        rows = pl.ds(row * L, L)

        def heads(group, carry):
            attend_back(rows, group, 3, qkv, ctx, dctx, lse[group, rows, :], grads, key_feat, query_feat)
            return carry

        lax.fori_loop(0, 2, heads, 0)
    vec_grads[0:1, :] = jnp.sum(grads[:, 0:D].astype(F32), axis=0, keepdims=True)
    vec_grads[1:2, :] = jnp.sum(grads[:, 2 * D : 3 * D].astype(F32), axis=0, keepdims=True)
    for part in range(3):
        cols = slice(part * D, (part + 1) * D)
        qkvg[:, cols] = mm(x[...], grads[:, cols], TN).astype(BF16)
    xg[...] = (mm(grads[...], wqkv[...], NT) + dr1[...]).astype(xg.dtype)


MESH = pl.DeviceIdType.MESH


def load(source, target, sem):
    copy = pltpu.make_async_copy(source, target, sem)
    copy.start()
    return copy


def remote(source, target, out_sem, in_sem, device):
    return pltpu.make_async_remote_copy(
        src_ref=source, dst_ref=target, send_sem=out_sem, recv_sem=in_sem,
        device_id=device, device_id_type=MESH,
    )


def arrived(target, in_sem, device):
    remote(target, target, in_sem, in_sem, device).wait_recv()


def meet(devices):
    barrier = pltpu.get_barrier_semaphore()
    for device in devices:
        pl.semaphore_signal(barrier, inc=1, device_id=device, device_id_type=MESH)
    pl.semaphore_wait(barrier, len(devices))


def example_ends(lens, row):
    place = lax.broadcasted_iota(jnp.int32, lens.shape, 1)
    counts = jnp.sum(jnp.where(place == row, lens[...], 0).astype(F32), axis=1, keepdims=True)
    ends, total = [], 0
    for item in range(lens.shape[0]):
        total = total + counts[item : item + 1, :]
        ends.append(total.astype(jnp.int32))
    return ends


def wide(vector):
    return vector[...].astype(F32).reshape(1, vector.shape[0])


def gather_kernel(
    hidden, lens, wqkv_in, bq, bv, wout_in, bout,
    x_out, qkv_out, ctx_out, r1_out, lse_out,
    x, qkv, ctx, r1, lse, wqkv, wout, bias, key_feat, query_feat,
    load_sem, own_sem, keep_sem, out_sems, in_sems,
):
    me = lax.axis_index("heads")
    row_id = lax.axis_index("rows")
    heads = lax.axis_size("heads")
    part = hidden.shape[1]
    rows_mine = x.shape[0] // L
    wqkv_load = load(wqkv_in, wqkv, load_sem.at[0])
    wout_load = load(wout_in, wout, load_sem.at[1])
    others = [lax.rem(me + step, heads) for step in range(1, heads)]
    device = lambda other: {"rows": row_id, "heads": other}

    def kept(row):
        return pltpu.make_async_copy(
            hidden.at[me * rows_mine + row], x.at[pl.ds(row * L + me * part, part)], own_sem.at[row]
        )

    def passed(row, step):
        other = others[step]
        return remote(
            hidden.at[other * rows_mine + row], x.at[pl.ds(row * L + me * part, part)],
            out_sems.at[row, step], in_sems.at[row, me], device(other),
        )

    def stores(row):
        rows = pl.ds(pl.multiple_of(row * L, L), L)
        return [
            pltpu.make_async_copy(source, target, keep_sem.at[index, row])
            for index, (source, target) in enumerate(
                (
                    (x.at[rows], x_out.at[rows]), (qkv.at[rows], qkv_out.at[rows]), (ctx.at[rows], ctx_out.at[rows]),
                    (lse.at[:, rows], lse_out.at[:, rows]), (r1.at[rows], r1_out.at[rows]),
                )
            )
        ]

    meet([device(other) for other in others])
    for row in range(rows_mine):
        for step in range(heads - 1):
            passed(row, step).start()
        kept(row).start()
    bias[0:1, :] = wide(bq)
    bias[1:2, :] = jnp.zeros((1, D), F32)
    bias[2:3, :] = wide(bv)
    out_bias = wide(bout)
    for row in range(rows_mine):
        features(example_ends(lens, me * rows_mine + row), key_feat, query_feat, row * L)
    wqkv_load.wait()
    wout_load.wait()

    def whole_row(row, carry):
        rows = pl.ds(pl.multiple_of(row * L, L), L)
        kept(row).wait()
        for other in others:
            arrived(x.at[pl.ds(row * L + other * part, part)], in_sems.at[row, other], device(other))
        keep = stores(row)
        keep[0].start()
        for item in range(3):
            cols = pl.ds(item * D, D)
            acc = mm(x[rows, :], wqkv[:, cols]) + bias[item : item + 1, :]
            if item == 0:
                acc = acc * DH**-0.5
            qkv[rows, cols] = acc.astype(BF16)
        keep[1].start()

        def group_heads(group, carry):
            attend(rows, group, 3, qkv, ctx, lse, key_feat, query_feat)
            return carry

        lax.fori_loop(0, 2, group_heads, 0)
        keep[2].start()
        keep[3].start()
        r1[rows, :] = mm(ctx[rows, :], wout[...]) + out_bias + x[rows, :].astype(F32)
        keep[4].start()
        return carry

    lax.fori_loop(0, rows_mine, whole_row, 0)
    for row in range(rows_mine):
        for step in range(heads - 1):
            passed(row, step).wait_send()
        for copy in stores(row):
            copy.wait()


class Place:
    def __init__(self):
        self.row, self.head = lax.axis_index("rows"), lax.axis_index("heads")
        self.z, self.y = self.row // 2, lax.rem(self.row, 2)
        self.x, self.c = self.head // 2, lax.rem(self.head, 2)
        self.over = {
            "c": self.at(c=1 - self.c), "y": self.at(y=1 - self.y), "x": self.at(x=1 - self.x),
        }

    def at(self, **new):
        z, y, x, c = (new.get(name, getattr(self, name)) for name in "zyxc")
        return {"rows": z * 2 + y, "heads": x * 2 + c}

    def turn(self, step):
        return lax.rem(self.z + step, 4)


class Total:
    def __init__(self, where, order, got, mid, far, near, sems):
        self.where, self.order = where, order
        self.got, self.mid, self.far, self.near = got, mid, far, near
        self.core_out, self.core_in, self.out, self.inn, self.z_out, self.z_in, self.end = sems
        self.cores = []

    @staticmethod
    def scratch(order, rows, cols):
        if order == "yzx":
            shapes = [(2, 4, 2, rows, cols), (2, 4, rows, cols), (4, 2, rows, cols), (rows, cols)]
        else:
            shapes = [(2, 4, 2, rows, cols), (4, 2, rows, cols), (4, rows, cols), (4, rows, cols)]
        sems = [(4,), (4,), (2, 4), (2, 4), (4,), (4,), (2,)]
        return [pltpu.VMEM(dims, BF16) for dims in shapes] + [pltpu.SemaphoreType.DMA(dims) for dims in sems]

    def core_send(self, index, parts):
        def copy(index):
            source, target = parts(index)
            return remote(source, target, self.core_out.at[index], self.core_in.at[index], self.where.over["c"])

        copy(index).start()
        return copy

    def core_wait(self, index, target):
        arrived(target, self.core_in.at[index], self.where.over["c"])

    def first_copy(self, step):
        w = self.where
        z = w.turn(step + 1)
        if self.order == "yzx":
            source, target = self.got.at[:, z, 1 - w.y], self.mid.at[:, z]
        else:
            source, target = self.got.at[1 - w.x, z], self.mid.at[z]
        return remote(source, target, self.out.at[0, step], self.inn.at[0, step], w.over[self.order[0]])

    def first(self, step):
        self.first_copy(step).start()

    def over_y(self, step):
        w = self.where
        z = w.turn(step + 1)
        return remote(
            self.mid.at[z, 1 - w.y], self.far.at[z], self.out.at[1, step], self.inn.at[1, step], w.over["y"]
        )

    def second(self, step):
        w = self.where
        z = w.turn(step + 1)
        if self.order == "yzx":
            arrived(self.mid.at[:, z], self.inn.at[0, step], w.over["y"])
            self.mid[:, z] = (self.mid[:, z].astype(F32) + self.got[:, z, w.y].astype(F32)).astype(BF16)
            self.z_send(step)
        else:
            arrived(self.mid.at[z], self.inn.at[0, step], w.over["x"])
            self.mid[z] = (self.mid[z].astype(F32) + self.got[w.x, z].astype(F32)).astype(BF16)
            self.over_y(step).start()

    def third(self, step):
        w = self.where
        z = w.turn(step + 1)
        arrived(self.far.at[z], self.inn.at[1, step], w.over["y"])
        self.far[z] = (self.far[z].astype(F32) + self.mid[z, w.y].astype(F32)).astype(BF16)
        self.z_send(step)

    def z_copy(self, step):
        w = self.where
        z = w.turn(step + 1)
        source, target = (self.mid.at[:, z], self.far) if self.order == "yzx" else (self.far.at[z], self.near)
        return remote(source, target.at[w.z], self.z_out.at[step], self.z_in.at[w.z], w.at(z=z))

    def z_send(self, step):
        if step < 3:
            self.z_copy(step).start()

    def z_sum(self):
        w = self.where
        slots = self.far if self.order == "yzx" else self.near
        total = (self.mid[:, w.z] if self.order == "yzx" else self.far[w.z]).astype(F32)
        for step in range(3):
            z = w.turn(step + 1)
            arrived(slots.at[z], self.z_in.at[z], w.at(z=z))
            total = total + slots[z].astype(F32)
        return total

    def x_copy(self):
        w = self.where
        return remote(self.far.at[w.z, 1 - w.x], self.near, self.end.at[0], self.end.at[1], w.over["x"])

    def fourth(self):
        self.far[self.where.z] = self.z_sum().astype(BF16)
        self.x_copy().start()

    def result(self):
        w = self.where
        if self.order == "xyz":
            return self.z_sum()
        arrived(self.near, self.end.at[1], w.over["x"])
        return self.far[w.z, w.x].astype(F32) + self.near[...].astype(F32)

    def sent(self):
        for step in range(4):
            self.first_copy(step).wait_send()
            if self.order == "xyz":
                self.over_y(step).wait_send()
        for step in range(3):
            self.z_copy(step).wait_send()
        if self.order == "yzx":
            self.x_copy().wait_send()


class Everyone:
    def __init__(self, where, slots, got, all_z, sems):
        self.where, self.slots, self.got, self.all_z, self.sems = where, slots, got, all_z, sems

    @staticmethod
    def scratch(rows):
        return [
            pltpu.VMEM((4, rows, D), F32), pltpu.VMEM((3, rows, D), F32), pltpu.VMEM((4, rows, D), F32),
            pltpu.SemaphoreType.DMA((4, 6)),
        ]

    def copy(self, level):
        w = self.where
        return remote(
            self.slots.at[level], self.got.at[level], self.sems.at[0, level], self.sems.at[1, level],
            w.over["cyx"[level]],
        )

    def z_copy(self, step):
        w = self.where
        return remote(
            self.slots.at[3], self.all_z.at[w.z], self.sems.at[2, step], self.sems.at[3, w.z],
            w.at(z=w.turn(step + 1)),
        )

    def start(self):
        self.copy(0).start()

    def step(self, level):
        w = self.where
        arrived(self.got.at[level], self.sems.at[1, level], w.over["cyx"[level]])
        self.slots[level + 1] = self.slots[level] + self.got[level]
        if level < 2:
            self.copy(level + 1).start()
            return
        self.all_z[w.z] = self.slots[3]
        for step in range(3):
            self.z_copy(step).start()

    def result(self):
        w = self.where
        for step in range(3):
            z = w.turn(step + 1)
            arrived(self.all_z.at[z], self.sems.at[3, z], w.at(z=z))
        return (self.all_z[0] + self.all_z[1]) + (self.all_z[2] + self.all_z[3])

    def sent(self):
        for item in range(3):
            self.copy(item).wait_send()
            self.z_copy(item).wait_send()


def rest_kernel(
    scale,
    r1_in, cotan, ctx_in, qkv_in, lse_in, x_in, lens, wup_in, wdown_in, wout_in, wqkv_in,
    g1v, s1v, g2v, s2v, bdv, bup,
    lay, xgr, downo, upo, outo, qkvo, vec_out,
    r1, ycot, fb, act, slope, acc, dfb, dfbt, wup, wdown, key_feat, query_feat, down_send,
    load_sem, cot_sem, lay_sem, xg_sem, own_sem,
    *scratch,
):
    where = w = Place()
    scratch = list(scratch)

    def take(count):
        return [scratch.pop(0) for _ in range(count)]

    totals = []
    for order, _, _ in BLOCKS:
        refs = take(11)
        totals.append(Total(where, order, *refs[:4], refs[4:]))
    down, up, out, qkva, qkvb = totals
    everyone = Everyone(where, *take(4))

    tokens = r1.shape[0]
    step_rows = 256
    parts = tokens // step_rows
    width = 768
    chunks = wup_in.shape[1] // width
    rows_mine = tokens // L
    part = lay.shape[1]
    r1_load = load(r1_in, r1, load_sem.at[0])
    wup_load = load(wup_in, wup, load_sem.at[1])
    wdown_load = load(wdown_in, wdown, load_sem.at[2])
    others = [lax.rem(w.head + step, 4) for step in range(1, 4)]
    partner = lambda other: {"rows": w.row, "heads": other}
    meet([partner(other) for other in others] + [where.over["y"]] + [where.at(z=where.turn(step)) for step in (1, 2, 3)])

    def mine_in(row):
        place = pl.ds(row * L + w.head * part, part)
        return pltpu.make_async_copy(cotan.at[w.head * rows_mine + row], ycot.at[place], own_sem.at[2, row])

    def cot_copy(row, step):
        place = pl.ds(row * L + w.head * part, part)
        other = others[step]
        return remote(
            cotan.at[other * rows_mine + row], ycot.at[place], cot_sem.at[0, row, step], cot_sem.at[1, row, w.head],
            partner(other),
        )

    def give_back(source, target, sems, row, step):
        other = others[step]
        return remote(
            source.at[pl.ds(row * L + other * part, part)], target.at[w.head * rows_mine + row],
            sems.at[0, row, step], sems.at[1, row, w.head], partner(other),
        )

    def mine_out(source, target, index, row):
        place = pl.ds(row * L + w.head * part, part)
        return pltpu.make_async_copy(source.at[place], target.at[w.head * rows_mine + row], own_sem.at[index, row])

    for row in range(rows_mine):
        for step in range(3):
            cot_copy(row, step).start()
        mine_in(row).start()

    g1, s1, g2, s2, bd = (wide(item) for item in (g1v, s1v, g2v, s2v, bdv))
    mine = everyone.slots.at[0]
    mine[...] = jnp.zeros(mine.shape, F32)
    for row in range(rows_mine):
        features(example_ends(lens, w.head * rows_mine + row), key_feat, query_feat, row * L)

    r1_load.wait()

    def lead(i, carry):
        rows = pl.ds(pl.multiple_of(i * step_rows, step_rows), step_rows)
        normed, _ = norm_parts(r1[rows, :])
        first = normed * g1 + s1
        fb[rows, :] = first.astype(BF16)
        acc[rows, :] = first + bd
        return carry

    lax.fori_loop(0, parts, lead, 0)
    wup_load.wait()
    wdown_load.wait()

    def forward(c, carry):
        cols = pl.ds(pl.multiple_of(c * width, width), width)
        u, e = [None] * parts, [None] * parts
        for s in range(parts + 2):
            if s < parts:
                u[s] = mm(fb[s * step_rows : (s + 1) * step_rows, :], wup[:, cols]) + wide(bup.at[cols])
            if 0 <= s - 1 < parts:
                j = s - 1
                rows = slice(j * step_rows, (j + 1) * step_rows)
                cdf, pdf = normal_parts(u[j])
                e[j] = (u[j] * cdf).astype(BF16)
                act[rows, cols] = e[j]
                slope[rows, cols] = (cdf + u[j] * pdf).astype(BF16)
            if 0 <= s - 2 < parts:
                j = s - 2
                acc[j * step_rows : (j + 1) * step_rows, :] += mm(e[j], wdown[cols, :])
        return carry

    lax.fori_loop(0, chunks, forward, 0)
    for row in range(rows_mine):
        mine_in(row).wait()
        for other in others:
            arrived(ycot.at[pl.ds(row * L + other * part, part)], cot_sem.at[1, row, other], partner(other))

    def second(i, carry):
        rows = pl.ds(pl.multiple_of(i * step_rows, step_rows), step_rows)
        normed, spread = norm_parts(acc[rows, :])
        dy = ycot[rows, :].astype(F32)
        ycot[rows, :] = (normed * g2 + s2).astype(BF16)
        dr2 = norm_back(dy, normed, spread, g2)
        acc[rows, :] = dr2
        low = dr2.astype(BF16)
        dfb[rows, :] = low
        dfbt[:, :, rows] = low.T.reshape(4, D // 4, step_rows)
        mine[0:1, :] += jnp.sum(dy * normed, axis=0, keepdims=True)
        mine[1:2, :] += jnp.sum(dy, axis=0, keepdims=True)
        mine[2:3, :] += jnp.sum(low.astype(F32), axis=0, keepdims=True)
        return carry

    lax.fori_loop(0, parts, second, 0)

    for row in range(rows_mine):
        for step in range(3):
            give_back(ycot, lay, lay_sem, row, step).start()
        mine_out(ycot, lay, 0, row).start()

    def down_half(core, z):
        left = jnp.concatenate([dfbt[core], dfbt[2 + core]], axis=0)
        cols = pl.ds(pl.multiple_of(z * width, width), width)
        return mm(left, act[:, cols])

    quarter, eighth = D // 4, width // 2

    def down_parts(step):
        z = where.turn(step + 1)
        return down_send.at[:, z], down.got.at[:, z]

    def down_other(step, carry):
        z = where.turn(step + 1)
        total = down_half(1 - w.c, z)
        for x in range(2):
            for y in range(2):
                piece = total[x * quarter : (x + 1) * quarter, y * eighth : (y + 1) * eighth]
                down_send[x, z, y] = piece.astype(BF16)
        down.core_send(step, down_parts)
        return carry

    def down_own(step, carry):
        z = where.turn(step + 1)
        total = down_half(w.c, z)
        down.core_wait(step, down.got.at[:, z])
        for x in range(2):
            for y in range(2):
                piece = total[x * quarter : (x + 1) * quarter, y * eighth : (y + 1) * eighth]
                down.got[x, z, y] = (piece + down.got[x, z, y].astype(F32)).astype(BF16)
        down.first(step)
        return carry

    lax.fori_loop(0, 4, down_other, 0)
    lax.fori_loop(0, 4, down_own, 0)
    qkv_load = load(qkv_in, act.at[:, pl.ds(0, 3 * D)], load_sem.at[4])

    def backward(c, carry):
        cols = pl.ds(pl.multiple_of(c * width, width), width)
        de, du = [None] * parts, [None] * parts
        sums = jnp.zeros((1, width), F32)
        for s in range(parts + 2):
            if s < parts:
                de[s] = mm(dfb[s * step_rows : (s + 1) * step_rows, :], wdown[cols, :], NT)
            if 0 <= s - 1 < parts:
                j = s - 1
                rows = slice(j * step_rows, (j + 1) * step_rows)
                du[j] = (de[j] * slope[rows, cols].astype(F32)).astype(BF16)
                slope[rows, cols] = du[j]
                sums = sums + jnp.sum(du[j].astype(F32), axis=0, keepdims=True)
            if 0 <= s - 2 < parts:
                j = s - 2
                acc[j * step_rows : (j + 1) * step_rows, :] += mm(du[j], wup[:, cols], NT)
        mine[pl.ds(3 + c, 1), :] = sums
        return carry

    half = chunks // 2
    lax.fori_loop(0, half, backward, 0)
    down.second(0)
    lax.fori_loop(half, chunks, backward, 0)
    down.second(1)
    wqkv = wup.at[:, pl.ds(0, 3 * D)]
    x = wdown.at[pl.ds(2 * D, tokens)]
    wout = wup.at[:, pl.ds(3 * D, D)]
    wqkv_load = load(wqkv_in, wqkv, load_sem.at[5])
    wout_load = load(wout_in, wout, load_sem.at[3])
    x_load = load(x_in, x, load_sem.at[6])
    dab = dfb

    def third(i, carry):
        rows = pl.ds(pl.multiple_of(i * step_rows, step_rows), step_rows)
        normed, spread = norm_parts(r1[rows, :])
        grad = acc[rows, :]
        dr = norm_back(grad, normed, spread, g1)
        acc[rows, :] = dr
        low = dr.astype(BF16)
        dab[rows, :] = low
        mine[7:8, :] += jnp.sum(grad * normed, axis=0, keepdims=True)
        mine[8:9, :] += jnp.sum(grad, axis=0, keepdims=True)
        mine[9:10, :] += jnp.sum(low.astype(F32), axis=0, keepdims=True)
        return carry

    lax.fori_loop(0, parts, third, 0)
    lse_load = [load(lse_in.at[g], r1.at[:, pl.ds(g * 128, 128)], load_sem.at[8 + g]) for g in range(2)]

    def up_half(core, x_side):
        cols = pl.ds(pl.multiple_of((2 * x_side + core) * width, width), width)
        return mm(fb[...], slope[:, cols], TN)

    def up_parts(side):
        return wdown.at[pl.ds(pl.multiple_of(side * D, D), D)], up.got.at[side].reshape(D, width)

    def up_other(side, carry):
        wdown[pl.ds(pl.multiple_of(side * D, D), D), :] = up_half(1 - w.c, side).astype(BF16)
        up.core_send(side, up_parts)
        return carry

    lax.fori_loop(0, 2, up_other, 0)
    down.second(2)

    def up_own(turn, carry):
        side = lax.rem(w.x + 1 + turn, 2)
        total = up_half(w.c, side).reshape(4, 2, D // 8, width)
        up.core_wait(side, up.got.at[side])
        up.got[side] = (total + up.got[side].astype(F32)).astype(BF16)

        @pl.when(turn == 0)
        def _():
            for step in range(4):
                up.first(step)

        return carry

    lax.fori_loop(0, 2, up_own, 0)
    down.second(3)
    ctx = slope.at[:, pl.ds(3 * D, D)]
    grads = slope.at[:, pl.ds(0, 3 * D)]
    dctx = act.at[:, pl.ds(3 * D, D)]
    ctx_load = load(ctx_in, ctx, load_sem.at[7])
    wout_load.wait()
    dctx[...] = mm(dab[...], wout[...], NT).astype(BF16)
    ctx_load.wait()

    def out_half(core, side):
        cols = pl.ds(pl.multiple_of(384 * side + 128 * core, 128), 256)
        return mm(ctx[...], dab[:, cols], TN)

    wqkv_load.wait()
    out_spots = [wup.at[:, pl.ds(3 * D + 256 * side, 256)] for side in range(2)]

    def out_parts(side):
        return out_spots[side], out.got.at[side].reshape(D, 256)

    for side in range(2):
        out_spots[side][...] = out_half(1 - w.c, side).astype(BF16)
        out.core_send(side, out_parts)
    for side in range(2):
        total = out_half(w.c, side).reshape(4, 2, D // 8, 256)
        out.core_wait(side, out.got.at[side])
        out.got[side] = (total + out.got[side].astype(F32)).astype(BF16)
    for step in range(4):
        out.first(step)

    qkv = act.at[:, pl.ds(0, 3 * D)]
    qkv_load.wait()
    for copy in lse_load:
        copy.wait()
    x_load.wait()

    def input_grad(row):
        rows = pl.ds(pl.multiple_of(row * L, L), L)
        fb[rows, :] = (mm(grads[rows, :], wqkv[...], NT) + acc[rows, :]).astype(BF16)
        for step in range(3):
            give_back(fb, xgr, xg_sem, row, step).start()
        mine_out(fb, xgr, 1, row).start()

    def heads_back(i, carry):
        row, group = i // 2, lax.rem(i, 2)
        rows = pl.ds(pl.multiple_of(row * L, L), L)
        keep = r1[rows, pl.ds(pl.multiple_of(group * 128, 128), 128)]
        attend_back(rows, group, 3, qkv, ctx, dctx, keep, grads, key_feat, query_feat)

        @pl.when(i == 0)
        def _():
            up.second(0)
            out.second(0)
            out.second(1)

        @pl.when(i == 1)
        def _():
            down.fourth()
            up.second(1)
            out.second(2)
            out.second(3)

        @pl.when(group == 1)
        def _():
            input_grad(row)

        @pl.when(i == 2)
        def _():
            up.second(2)
            up.third(0)

        @pl.when(i == 3)
        def _():
            up.second(3)
            up.third(1)
            out.fourth()

        return carry

    lax.fori_loop(0, 4, heads_back, 0)
    mine[10:11, :] = jnp.sum(grads[:, 0:D].astype(F32), axis=0, keepdims=True)
    mine[11:12, :] = jnp.sum(grads[:, 2 * D : 3 * D].astype(F32), axis=0, keepdims=True)
    everyone.start()

    def qkv_half(core, side):
        cols = pl.ds(pl.multiple_of(1152 * side + 512 * core, 128), 640)
        return mm(x[...], grads[:, cols], TN).reshape(4, 2, 2, D // 16, 640)

    def qkv_spot(side, index):
        return wdown.at[pl.ds(pl.multiple_of(side * D + index * (D // 2), D // 2), D // 2), pl.ds(0, 640)]

    def qkv_parts(index, each):
        return lambda side: (qkv_spot(side, index), each.got.at[side].reshape(D // 2, 640))

    def up_sent(side):
        remote(*up_parts(side), up.core_out.at[side], up.core_in.at[side], where.over["c"]).wait_send()

    for side in range(2):
        up_sent(side)

    def qkv_other(side, carry):
        total = qkv_half(1 - w.c, side).astype(BF16)
        for index, each in enumerate((qkva, qkvb)):
            qkv_spot(side, index)[...] = total[:, :, index].reshape(D // 2, 640)
            each.core_send(side, qkv_parts(index, each))
        return carry

    lax.fori_loop(0, 2, qkv_other, 0)
    up.third(2)
    everyone.step(0)

    def qkv_own(turn, carry):
        side = lax.rem(w.x + 1 + turn, 2)
        total = qkv_half(w.c, side)
        for index, each in enumerate((qkva, qkvb)):
            each.core_wait(side, each.got.at[side])
            each.got[side] = (total[:, :, index] + each.got[side].astype(F32)).astype(BF16)

        @pl.when(turn == 0)
        def _():
            for step in range(4):
                qkvb.first(step)

        @pl.when(turn == 1)
        def _():
            for step in range(4):
                qkva.first(step)

        return carry

    lax.fori_loop(0, 2, qkv_own, 0)
    up.third(3)
    everyone.step(1)
    outo[...] = pick(out.result() * scale, w.c, 192)
    downo[...] = down.result() * scale
    everyone.step(2)
    for step in range(4):
        qkva.second(step)
        qkvb.second(step)
    upo[...] = up.result() * scale
    vectors = everyone.result() * scale
    for index, item in enumerate((10, 11, 9, 7, 8, 2, 0, 1)):
        vec_out[index : index + 1, :] = vectors[item : item + 1, :]
    for index in range(4):
        vec_out[8 + index : 9 + index, :] = vectors[3 + index : 4 + index, :]
    for step in range(4):
        qkvb.third(step)
    qkva.fourth()
    qkvo[D // 16 :, :] = pick(qkvb.result() * scale, w.c, 576)
    qkvo[0 : D // 16, :] = pick(qkva.result() * scale, w.c, 576)
    for row in range(rows_mine):
        for target, sems in ((lay, lay_sem), (xgr, xg_sem)):
            for other in others:
                arrived(target.at[other * rows_mine + row], sems.at[1, row, other], partner(other))
        for step in range(3):
            cot_copy(row, step).wait_send()
            give_back(ycot, lay, lay_sem, row, step).wait_send()
            give_back(fb, xgr, xg_sem, row, step).wait_send()
        mine_out(ycot, lay, 0, row).wait()
        mine_out(fb, xgr, 1, row).wait()
    for total, parts_of, count in (
        (down, down_parts, 4), (out, out_parts, 2), (qkva, qkv_parts(0, qkva), 2), (qkvb, qkv_parts(1, qkvb), 2),
    ):
        for index in range(count):
            remote(*parts_of(index), total.core_out.at[index], total.core_in.at[index], where.over["c"]).wait_send()
    for total in totals:
        total.sent()
    everyone.sent()


def pick(values, core, width):
    return jnp.where(core == 0, values[:, :width], values[:, 64 : 64 + width])


VMEM = pl.BlockSpec(memory_space=pltpu.VMEM)
SMEM = pl.BlockSpec(memory_space=pltpu.SMEM)


def shape(dims, kind):
    return jax.ShapeDtypeStruct(dims, kind)


def params(**more):
    return pltpu.CompilerParams(vmem_limit_bytes=255 * 2**18, **more)


def local(
    hidden_in, lengths, qkv_weight, query_bias, value_bias, out_weight, out_bias, gain_one,
    shift_one, up_weight, up_bias, down_weight, down_bias, gain_two, shift_two, cotangent,
):
    row_count, part_len = hidden_in.shape[0], hidden_in.shape[1]
    heads = lax.axis_size("heads")
    mine = row_count // heads
    tokens = mine * L
    ff = up_weight.shape[1]
    place = lax.axis_index("heads")
    x = lax.all_to_all(hidden_in, "heads", split_axis=0, concat_axis=1, tiled=True).reshape(tokens, D)
    cot = lax.all_to_all(cotangent, "heads", split_axis=0, concat_axis=1, tiled=True).reshape(tokens, D)
    lens = lax.dynamic_slice_in_dim(lengths, place * mine, mine, 0)
    bqkv = jnp.concatenate([query_bias, jnp.zeros_like(query_bias), value_bias]).astype(F32)[None]
    qkv, ctx, r1, lse = pl.pallas_call(
        first_kernel,
        out_shape=(
            shape((tokens, 3 * D), BF16), shape((tokens, D), BF16), shape((tokens, D), F32),
            shape((2, tokens, 128), F32),
        ),
        in_specs=[VMEM, SMEM] + [VMEM] * 4,
        out_specs=(VMEM,) * 4,
        scratch_shapes=[pltpu.VMEM((tokens, 128), BF16)] * 2,
        compiler_params=params(),
        name="first",
    )(x, lens, qkv_weight, bqkv, out_weight, out_bias.astype(F32)[None])
    vecs = jnp.stack([gain_one, shift_one, gain_two, shift_two, down_bias]).astype(F32)
    y, dr1, dctx, downg, upg, outg, vec_mid, upb = pl.pallas_call(
        middle_kernel,
        out_shape=(
            shape((tokens, D), BF16), shape((tokens, D), F32), shape((tokens, D), BF16),
            shape((D, ff), BF16), shape((D, ff), BF16), shape((D, D), BF16),
            shape((8, D), F32), shape((1, ff), F32),
        ),
        in_specs=[VMEM] * 8,
        out_specs=(VMEM,) * 8,
        scratch_shapes=[
            pltpu.VMEM((tokens, D), BF16), pltpu.VMEM((tokens, ff), BF16), pltpu.VMEM((tokens, ff), BF16),
            pltpu.VMEM((tokens, D), F32), pltpu.VMEM((tokens, D), BF16), pltpu.VMEM((tokens, D), BF16),
        ],
        compiler_params=params(),
        name="middle",
    )(r1, ctx, cot, vecs, up_weight, up_bias.astype(F32)[None], down_weight, out_weight)
    xg, qkvg, vec_last = pl.pallas_call(
        last_kernel,
        out_shape=(shape((tokens, D), BF16), shape((D, 3 * D), BF16), shape((8, D), F32)),
        in_specs=[VMEM, SMEM] + [VMEM] * 6,
        out_specs=(VMEM,) * 3,
        scratch_shapes=[pltpu.VMEM((tokens, 3 * D), BF16)] + [pltpu.VMEM((tokens, 128), BF16)] * 2,
        compiler_params=params(),
        name="last",
    )(x, lens, qkv, ctx, dctx, lse, dr1, qkv_weight)

    def back(values):
        values = values.reshape(mine, L, D)
        return lax.all_to_all(values, "heads", split_axis=1, concat_axis=0, tiled=True)

    layer_out = back(y)
    input_grad = back(xg).astype(F32)
    scale = 1.0 / (row_count * lax.axis_size("rows"))
    vec_mid, vec_last, upb = lax.psum((vec_mid, vec_last, upb), ("rows", "heads"))

    def reduce(values, flip):
        one, two = (0, 1) if flip else (1, 0)
        half = lax.psum_scatter(values, "heads", scatter_dimension=one, tiled=True).astype(F32)
        total = lax.psum_scatter(half, "rows", scatter_dimension=two, tiled=True) * scale
        return total.T if flip else total

    vm, vl = vec_mid * scale, vec_last * scale
    return (
        layer_out, input_grad, reduce(qkvg, False), vl[0], vl[1], reduce(outg, False), vm[5], vm[3], vm[4],
        reduce(upg, False), upb[0] * scale, reduce(downg, True), vm[2], vm[0], vm[1],
    )


ANY = pl.BlockSpec(memory_space=pl.ANY)
DMA = pltpu.SemaphoreType.DMA
BLOCKS = (("yzx", 192, 384), ("xyz", 96, 768), ("yzx", 96, 256), ("yzx", 48, 640), ("xyz", 48, 640))


def finish_kernel(count, *refs):
    lay, xgr, vec = refs[:3]
    mats = refs[3 : 3 + count]
    lay_out, xg_out = refs[3 + count : 5 + count]
    mats_out = refs[5 + count : 5 + 2 * count]
    vecs_out = refs[5 + 2 * count : 14 + 2 * count]
    through, low, full, sems = refs[14 + 2 * count :]
    blocks = xgr.shape[0]
    wides = [load(xgr.at[i], low.at[i], sems.at[0, i]) for i in range(blocks)]
    lays = [load(lay.at[i], through.at[i], sems.at[1, i]) for i in range(blocks)]
    for index in range(8):
        vecs_out[index][...] = vec[index, :]
    for index in range(4):
        vecs_out[8][index * D : (index + 1) * D] = vec[8 + index, :]
    copies = []
    for i in range(blocks):
        wides[i].wait()
        full[i] = low[i].astype(F32)
        copies.append(load(full.at[i], xg_out.at[i], sems.at[2, i]))
    for i in range(blocks):
        lays[i].wait()
        copies.append(load(through.at[i], lay_out.at[i], sems.at[3, i]))
    for source, target in zip(mats, mats_out):
        target[...] = source[...]
    for copy in copies:
        copy.wait()


def local_fast(
    hidden_in, lengths, qkv_weight, query_bias, value_bias, out_weight, out_bias, gain_one,
    shift_one, up_weight, up_bias, down_weight, down_bias, gain_two, shift_two, cotangent,
):
    row_count, part_len = hidden_in.shape[0], hidden_in.shape[1]
    mine = row_count // lax.axis_size("heads")
    heads = lax.axis_size("heads")
    tokens = mine * L
    ff = up_weight.shape[1]
    bf = lambda *dims: pltpu.VMEM(dims, BF16)
    fl = lambda *dims: pltpu.VMEM(dims, F32)
    x, qkv, ctx, r1, lse = pl.pallas_call(
        gather_kernel,
        out_shape=(
            shape((tokens, D), BF16), shape((tokens, 3 * D), BF16),
            shape((tokens, D), BF16), shape((tokens, D), F32), shape((2, tokens, 128), F32),
        ),
        in_specs=[ANY, VMEM, ANY, VMEM, VMEM, ANY, VMEM],
        out_specs=(ANY,) * 5,
        scratch_shapes=[
            bf(tokens, D), bf(tokens, 3 * D), bf(tokens, D), fl(tokens, D), fl(2, tokens, 128), bf(D, 3 * D),
            bf(D, D), fl(8, D), bf(tokens, 128), bf(tokens, 128),
            DMA((2,)), DMA((mine,)), DMA((5, mine)), DMA((mine, heads - 1)), DMA((mine, heads)),
        ],
        compiler_params=params(collective_id=0, has_side_effects=True),
        name="gather",
    )(hidden_in, lengths.T, qkv_weight, query_bias, value_bias, out_weight, out_bias)
    scale = 1.0 / (row_count * lax.axis_size("rows"))
    totals = []
    for order, rows, cols in BLOCKS:
        totals += Total.scratch(order, rows, cols)
    mats = (shape((192, 384), F32), shape((96, 768), F32), shape((96, 192), F32), shape((96, 576), F32))
    wide_out = shape((row_count, part_len, D), BF16)
    lay, xgr, downg, upg, outg, qkvg, vec = pl.pallas_call(
        functools.partial(rest_kernel, scale),
        out_shape=(wide_out, wide_out) + mats + (shape((16, D), F32),),
        in_specs=[ANY] * 6 + [VMEM] + [ANY] * 4 + [VMEM] * 6,
        out_specs=(ANY, ANY) + (VMEM,) * 5,
        scratch_shapes=[
            fl(tokens, D), bf(tokens, D), bf(tokens, D), bf(tokens, ff), bf(tokens, ff),
            fl(tokens, D), bf(tokens, D), bf(4, D // 4, tokens), bf(D, ff), bf(ff, D),
            bf(tokens, 128), bf(tokens, 128),
            bf(2, 4, 2, 192, 384), DMA((10,)), DMA((2, mine, 4)), DMA((2, mine, 4)), DMA((2, mine, 4)), DMA((3, mine)),
        ]
        + totals
        + Everyone.scratch(16),
        compiler_params=params(collective_id=1, has_side_effects=True),
        name="rest",
    )(
        r1, cotangent, ctx, qkv, lse, x, lengths.T, up_weight, down_weight, out_weight, qkv_weight,
        gain_one, shift_one, gain_two, shift_two, down_bias, up_bias,
    )
    results = pl.pallas_call(
        functools.partial(finish_kernel, 4),
        out_shape=(wide_out, shape((row_count, part_len, D), F32)) + mats + (shape((D,), F32),) * 8 + (shape((ff,), F32),),
        in_specs=[ANY, ANY] + [VMEM] * 5,
        out_specs=(ANY,) * 2 + (VMEM,) * 13,
        scratch_shapes=[
            bf(row_count, part_len, D), bf(row_count, part_len, D), fl(row_count, part_len, D), DMA((4, row_count)),
        ],
        compiler_params=params(),
        name="finish",
    )(lay, xgr, vec, downg, upg, outg, qkvg)
    layer_out, input_grad, downg, upg, outg, qkvg, qb, vb, ob, go, so, db, gt, st, ub = results
    return layer_out, input_grad, qkvg, qb, vb, outg, ob, go, so, upg, ub, downg.T, db, gt, st


def solution(mesh):
    split = P("rows", "heads", None)
    grid = P("rows", "heads")
    in_specs = (split, P("rows", None)) + (P(),) * 13 + (split,)
    out_specs = (split, split, grid, P(), P(), grid, P(), P(), P(), grid, P(), grid, P(), P(), P())
    fast = mesh.shape["rows"] == 8 and mesh.shape["heads"] == 4
    return jax.shard_map(
        local_fast if fast else local, mesh=mesh, in_specs=in_specs, out_specs=out_specs, check_vma=False
    )
```

```python
import functools

import jax
import jax.numpy as jnp
from jax import lax
from jax.experimental import pallas as pl
from jax.experimental.pallas import tpu as pltpu
from jax.sharding import PartitionSpec as P

DH = 64
D = 768
L = 512
EPSILON = 1e-12
OFF = -(2.0**100)
F32 = jnp.float32
BF16 = jnp.bfloat16
NN = (((1,), (0,)), ((), ()))
NT = (((1,), (1,)), ((), ()))
TN = (((0,), (0,)), ((), ()))

TAIL = (
    0.09881087227319621,
    0.11230449770687516,
    0.02424904968806795,
    0.2825055677430211,
    -0.268648558796486,
    0.34262844642428514,
    -0.09184987882933851,
)


def mm(left, right, dims=NN):
    return lax.dot_general(left, right, dims, preferred_element_type=F32)


def normal_parts(u):
    bell = jnp.exp(u * u * -0.5)
    t = pltpu.reciprocal(1.0 + 0.25 * jnp.abs(u))
    poly = TAIL[-1]
    for item in TAIL[-2::-1]:
        poly = poly * t + item
    tail = poly * t * bell
    return jnp.where(u >= 0, 1.0 - tail, tail), bell * 0.3989422804014327


def norm_parts(values):
    middle = jnp.mean(values, axis=-1, keepdims=True)
    center = values - middle
    spread = jnp.mean(center * center, axis=-1, keepdims=True)
    scale = lax.rsqrt(spread + EPSILON)
    return center * scale, scale


def norm_back(grad, normed, scale, gain):
    dn = grad * gain
    first = jnp.mean(dn, axis=-1, keepdims=True)
    second = jnp.mean(dn * normed, axis=-1, keepdims=True)
    return (dn - first - normed * second) * scale


def split3(values):
    high = values.astype(BF16)
    rest = values - high.astype(F32)
    mid = rest.astype(BF16)
    return high, mid, (rest - mid.astype(F32)).astype(BF16)


def features(ends, key_feat, query_feat, start):
    token = lax.broadcasted_iota(jnp.int32, (L, 128), 0)
    place = lax.broadcasted_iota(jnp.int32, (L, 128), 1) & (DH - 1)
    seg = jnp.zeros((L, 128), jnp.int32)
    for end in ends:
        seg = seg + (token >= end).astype(jnp.int32)
    count = len(ends)
    ones = (place == seg) | ((place >= count) & (place < count + 3))
    key_feat[pl.ds(start, L), :] = jnp.where(ones, 1.0, 0.0).astype(BF16)
    off = (place < count) & (place != seg)
    query_feat[pl.ds(start, L), :] = jnp.where(off, OFF, 0.0).astype(BF16)


def attend(rows, group, pairs, qkv, ctx, lse, key_feat, query_feat):
    lane = lax.broadcasted_iota(jnp.int32, (1, 128), 1)
    kf, qf = key_feat[rows, :], query_feat[rows, :]
    ops, values = [], []
    for pair in range(pairs):
        col = pl.multiple_of(group * (pairs * 128) + pair * 128, 128)
        q2 = qkv[rows, pl.ds(col, 128)]
        k2 = qkv[rows, pl.ds(D + col, 128)]
        values.append(qkv[rows, pl.ds(2 * D + col, 128)])
        for own in (lane < DH, lane >= DH):
            ops.append((jnp.where(own, q2, qf), jnp.where(own, k2, kf)))
    count = 2 * pairs
    scores = [None] * count
    outs, sums = [], []
    scores[0] = mm(*ops[0], NT)
    for head in range(count):
        if head + 1 < count:
            scores[head + 1] = mm(*ops[head + 1], NT)
        peak = jnp.max(scores[head], axis=1, keepdims=True)
        expo = jnp.exp(scores[head] - peak)
        total = jnp.sum(expo, axis=1, keepdims=True)
        out = mm(expo.astype(BF16), values[head // 2])
        outs.append(out * (1.0 / total))
        sums.append(peak + jnp.log(total))
    keep = jnp.zeros((L, 128), F32)
    for head in range(count):
        keep = jnp.where(lane == head, sums[head], keep)
    lse[group, rows, :] = keep
    for pair in range(pairs):
        col = pl.multiple_of(group * (pairs * 128) + pair * 128, 128)
        both = jnp.where(lane < DH, outs[2 * pair], outs[2 * pair + 1])
        ctx[rows, pl.ds(col, 128)] = both.astype(BF16)


def attend_back(rows, group, pairs, qkv, ctx, dctx, keep, grads, kf, qf):
    lane = lax.broadcasted_iota(jnp.int32, (1, 128), 1)
    place = lane & (DH - 1)
    vf = jnp.where((place >= 4) & (place < 7), 1.0, 0.0).astype(BF16)

    def spread(column, base):
        high, mid, small = split3(-column)
        return jnp.where(
            place == 4, high, jnp.where(place == 5, mid, jnp.where(place == 6, small, base))
        )

    ops = []
    for pair in range(pairs):
        col = pl.multiple_of(group * (pairs * 128) + pair * 128, 128)
        q2 = qkv[rows, pl.ds(col, 128)]
        k2 = qkv[rows, pl.ds(D + col, 128)]
        v2 = qkv[rows, pl.ds(2 * D + col, 128)]
        d2 = dctx[rows, pl.ds(col, 128)]
        both = d2.astype(F32) * ctx[rows, pl.ds(col, 128)].astype(F32)
        zero = jnp.zeros_like(q2)
        for side, own in enumerate((lane < DH, lane >= DH)):
            inner = jnp.sum(jnp.where(own, both, 0.0), axis=1, keepdims=True)
            total = keep[:, 2 * pair + side : 2 * pair + side + 1]
            ops.append(
                (
                    jnp.where(own, k2, kf),
                    jnp.where(own, q2, spread(total, qf)),
                    jnp.where(own, v2, vf),
                    jnp.where(own, d2, spread(inner, zero)),
                    jnp.where(own, q2, zero),
                    jnp.where(own, k2, zero),
                    jnp.where(own, d2, zero),
                )
            )
    count = 2 * pairs
    scores, chances = [None] * count, [None] * count
    dq, dk, dv = [0] * pairs, [0] * pairs, [0] * pairs

    def start(head):
        scores[head] = mm(ops[head][0], ops[head][1], NT)
        chances[head] = mm(ops[head][2], ops[head][3], NT)

    start(0)
    for head in range(count):
        if head + 1 < count:
            start(head + 1)
        chance = jnp.exp(scores[head])
        low = chance.astype(BF16)
        ds = (chance * chances[head]).astype(BF16)
        pair = head // 2
        dk[pair] += mm(ds, ops[head][4])
        dv[pair] += mm(low, ops[head][6])
        dq[pair] += mm(ds, ops[head][5], TN)
    for pair in range(pairs):
        col = pl.multiple_of(group * (pairs * 128) + pair * 128, 128)
        grads[rows, pl.ds(col, 128)] = (dq[pair] * DH**-0.5).astype(BF16)
        grads[rows, pl.ds(D + col, 128)] = dk[pair].astype(BF16)
        grads[rows, pl.ds(2 * D + col, 128)] = dv[pair].astype(BF16)


def first_kernel(x, lens, wqkv, bqkv, wout, bout, qkv, ctx, r1, lse, key_feat, query_feat):
    for row in range(x.shape[0] // L):
        ends, total = [], 0
        for item in range(lens.shape[1]):
            total = total + lens[row, item]
            ends.append(total)
        features(ends, key_feat, query_feat, row * L)

        rows = pl.ds(row * L, L)
        for part in range(3):
            cols = pl.ds(part * D, D)
            acc = mm(x[rows, :], wqkv[:, cols]) + bqkv[:, cols]
            if part == 0:
                acc = acc * DH**-0.5
            qkv[rows, cols] = acc.astype(BF16)

        def heads(group, carry):
            attend(rows, group, 3, qkv, ctx, lse, key_feat, query_feat)
            return carry

        lax.fori_loop(0, 2, heads, 0)
        r1[rows, :] = mm(ctx[rows, :], wout[...]) + bout[...] + x[rows, :].astype(F32)


def middle_kernel(
    r1, ctx, cot, vecs, wup, bup, wdown, wout,
    y, dr1, dctx, downg, upg, outg, vec_grads, upb_grad,
    fb, act, slope, acc, dfb, dab,
):
    tokens = r1.shape[0]
    step = 256
    parts = tokens // step
    width = 768
    chunks = wup.shape[1] // width
    g1, s1, g2, s2, bd = (vecs[i : i + 1, :] for i in range(5))
    vec_grads[...] = jnp.zeros_like(vec_grads)
    upb_grad[...] = jnp.zeros_like(upb_grad)

    def lead(i, carry):
        rows = pl.ds(pl.multiple_of(i * step, step), step)
        normed, _ = norm_parts(r1[rows, :])
        first = normed * g1 + s1
        fb[rows, :] = first.astype(BF16)
        acc[rows, :] = first + bd
        return carry

    lax.fori_loop(0, parts, lead, 0)

    def forward(c, carry):
        cols = pl.ds(pl.multiple_of(c * width, width), width)
        u, e = [None] * parts, [None] * parts
        for s in range(parts + 2):
            if s < parts:
                u[s] = mm(fb[s * step : (s + 1) * step, :], wup[:, cols]) + bup[:, cols]
            if 0 <= s - 1 < parts:
                j = s - 1
                rows = slice(j * step, (j + 1) * step)
                cdf, pdf = normal_parts(u[j])
                e[j] = (u[j] * cdf).astype(BF16)
                act[rows, cols] = e[j]
                slope[rows, cols] = (cdf + u[j] * pdf).astype(BF16)
            if 0 <= s - 2 < parts:
                j = s - 2
                acc[j * step : (j + 1) * step, :] += mm(e[j], wdown[cols, :])
        return carry

    lax.fori_loop(0, chunks, forward, 0)

    def second(i, carry):
        rows = pl.ds(pl.multiple_of(i * step, step), step)
        normed, scale = norm_parts(acc[rows, :])
        y[rows, :] = (normed * g2 + s2).astype(BF16)
        dy = cot[rows, :].astype(F32)
        dr2 = norm_back(dy, normed, scale, g2)
        acc[rows, :] = dr2
        low = dr2.astype(BF16)
        dfb[rows, :] = low
        vec_grads[0:1, :] += jnp.sum(dy * normed, axis=0, keepdims=True)
        vec_grads[1:2, :] += jnp.sum(dy, axis=0, keepdims=True)
        vec_grads[2:3, :] += jnp.sum(low.astype(F32), axis=0, keepdims=True)
        return carry

    lax.fori_loop(0, parts, second, 0)

    def down(c, carry):
        cols = pl.ds(pl.multiple_of(c * width, width), width)
        downg[:, cols] = mm(dfb[...], act[:, cols], TN).astype(BF16)
        return carry

    lax.fori_loop(0, chunks, down, 0)

    def backward(c, carry):
        cols = pl.ds(pl.multiple_of(c * width, width), width)
        de, du = [None] * parts, [None] * parts
        sums = jnp.zeros((1, width), F32)
        for s in range(parts + 2):
            if s < parts:
                de[s] = mm(dfb[s * step : (s + 1) * step, :], wdown[cols, :], NT)
            if 0 <= s - 1 < parts:
                j = s - 1
                rows = slice(j * step, (j + 1) * step)
                du[j] = (de[j] * slope[rows, cols].astype(F32)).astype(BF16)
                slope[rows, cols] = du[j]
                sums = sums + jnp.sum(du[j].astype(F32), axis=0, keepdims=True)
            if 0 <= s - 2 < parts:
                j = s - 2
                acc[j * step : (j + 1) * step, :] += mm(du[j], wup[:, cols], NT)
        upb_grad[:, cols] = sums
        return carry

    lax.fori_loop(0, chunks, backward, 0)

    def third(i, carry):
        rows = pl.ds(pl.multiple_of(i * step, step), step)
        normed, scale = norm_parts(r1[rows, :])
        grad = acc[rows, :]
        dr = norm_back(grad, normed, scale, g1)
        dr1[rows, :] = dr
        low = dr.astype(BF16)
        dab[rows, :] = low
        vec_grads[3:4, :] += jnp.sum(grad * normed, axis=0, keepdims=True)
        vec_grads[4:5, :] += jnp.sum(grad, axis=0, keepdims=True)
        vec_grads[5:6, :] += jnp.sum(low.astype(F32), axis=0, keepdims=True)
        return carry

    lax.fori_loop(0, parts, third, 0)
    dctx[...] = mm(dab[...], wout[...], NT).astype(BF16)
    outg[...] = mm(ctx[...], dab[...], TN).astype(BF16)

    def up(c, carry):
        cols = pl.ds(pl.multiple_of(c * width, width), width)
        upg[:, cols] = mm(fb[...], slope[:, cols], TN).astype(BF16)
        return carry

    lax.fori_loop(0, chunks, up, 0)


def last_kernel(x, lens, qkv, ctx, dctx, lse, dr1, wqkv, xg, qkvg, vec_grads, grads, key_feat, query_feat):
    vec_grads[...] = jnp.zeros_like(vec_grads)
    for row in range(x.shape[0] // L):
        ends, total = [], 0
        for item in range(lens.shape[1]):
            total = total + lens[row, item]
            ends.append(total)
        features(ends, key_feat, query_feat, row * L)

        rows = pl.ds(row * L, L)

        def heads(group, carry):
            attend_back(
                rows, group, 3, qkv, ctx, dctx, lse[group, rows, :], grads, key_feat[rows, :], query_feat[rows, :]
            )
            return carry

        lax.fori_loop(0, 2, heads, 0)
    vec_grads[0:1, :] = jnp.sum(grads[:, 0:D].astype(F32), axis=0, keepdims=True)
    vec_grads[1:2, :] = jnp.sum(grads[:, 2 * D : 3 * D].astype(F32), axis=0, keepdims=True)
    for part in range(3):
        cols = slice(part * D, (part + 1) * D)
        qkvg[:, cols] = mm(x[...], grads[:, cols], TN).astype(BF16)
    xg[...] = (mm(grads[...], wqkv[...], NT) + dr1[...]).astype(xg.dtype)


MESH = pl.DeviceIdType.MESH


def load(source, target, sem):
    copy = pltpu.make_async_copy(source, target, sem)
    copy.start()
    return copy


def remote(source, target, out_sem, in_sem, device):
    return pltpu.make_async_remote_copy(
        src_ref=source, dst_ref=target, send_sem=out_sem, recv_sem=in_sem,
        device_id=device, device_id_type=MESH,
    )


def arrived(target, in_sem, device):
    remote(target, target, in_sem, in_sem, device).wait_recv()


def meet(devices):
    barrier = pltpu.get_barrier_semaphore()
    for device in devices:
        pl.semaphore_signal(barrier, inc=1, device_id=device, device_id_type=MESH)
    pl.semaphore_wait(barrier, len(devices))


def example_ends(lens, row):
    place = lax.broadcasted_iota(jnp.int32, lens.shape, 1)
    counts = jnp.sum(jnp.where(place == row, lens[...], 0).astype(F32), axis=1, keepdims=True)
    ends, total = [], 0
    for item in range(lens.shape[0]):
        total = total + counts[item : item + 1, :]
        ends.append(total.astype(jnp.int32))
    return ends


def wide(vector):
    return vector[...].astype(F32).reshape(1, vector.shape[0])


def gather_kernel(
    hidden, lens, wqkv_in, bq, bv, wout_in, bout,
    x_out, qkv_out, ctx_out, r1_out, lse_out,
    x, qkv, ctx, r1, lse, wqkv, wout, bias, key_feat, query_feat,
    load_sem, own_sem, keep_sem, out_sems, in_sems,
):
    me = lax.axis_index("heads")
    row_id = lax.axis_index("rows")
    heads = lax.axis_size("heads")
    part = hidden.shape[1]
    rows_mine = x.shape[0] // L
    wqkv_load = load(wqkv_in, wqkv, load_sem.at[0])
    wout_load = load(wout_in, wout, load_sem.at[1])
    others = [lax.rem(me + step, heads) for step in range(1, heads)]
    device = lambda other: {"rows": row_id, "heads": other}

    def kept(row):
        return pltpu.make_async_copy(
            hidden.at[me * rows_mine + row], x.at[pl.ds(row * L + me * part, part)], own_sem.at[row]
        )

    def passed(row, step):
        other = others[step]
        return remote(
            hidden.at[other * rows_mine + row], x.at[pl.ds(row * L + me * part, part)],
            out_sems.at[row, step], in_sems.at[row, me], device(other),
        )

    def stores(row):
        rows = pl.ds(pl.multiple_of(row * L, L), L)
        return [
            pltpu.make_async_copy(source, target, keep_sem.at[index, row])
            for index, (source, target) in enumerate(
                (
                    (x.at[rows], x_out.at[rows]), (qkv.at[rows], qkv_out.at[rows]), (ctx.at[rows], ctx_out.at[rows]),
                    (lse.at[:, rows], lse_out.at[:, rows]), (r1.at[rows], r1_out.at[rows]),
                )
            )
        ]

    meet([device(other) for other in others])
    for row in range(rows_mine):
        for step in range(heads - 1):
            passed(row, step).start()
        kept(row).start()
    bias[0:1, :] = wide(bq)
    bias[1:2, :] = jnp.zeros((1, D), F32)
    bias[2:3, :] = wide(bv)
    out_bias = wide(bout)
    for row in range(rows_mine):
        features(example_ends(lens, me * rows_mine + row), key_feat, query_feat, row * L)
    wqkv_load.wait()
    wout_load.wait()

    def whole_row(row, carry):
        rows = pl.ds(pl.multiple_of(row * L, L), L)
        kept(row).wait()
        for other in others:
            arrived(x.at[pl.ds(row * L + other * part, part)], in_sems.at[row, other], device(other))
        keep = stores(row)
        keep[0].start()
        for item in range(3):
            cols = pl.ds(item * D, D)
            acc = mm(x[rows, :], wqkv[:, cols]) + bias[item : item + 1, :]
            if item == 0:
                acc = acc * DH**-0.5
            qkv[rows, cols] = acc.astype(BF16)
        keep[1].start()

        def group_heads(group, carry):
            attend(rows, group, 3, qkv, ctx, lse, key_feat, query_feat)
            return carry

        lax.fori_loop(0, 2, group_heads, 0)
        keep[2].start()
        keep[3].start()
        r1[rows, :] = mm(ctx[rows, :], wout[...]) + out_bias + x[rows, :].astype(F32)
        keep[4].start()
        return carry

    lax.fori_loop(0, rows_mine, whole_row, 0)
    for row in range(rows_mine):
        for step in range(heads - 1):
            passed(row, step).wait_send()
        for copy in stores(row):
            copy.wait()


class Place:
    def __init__(self):
        self.row, self.head = lax.axis_index("rows"), lax.axis_index("heads")
        self.z, self.y = self.row // 2, lax.rem(self.row, 2)
        self.x, self.c = self.head // 2, lax.rem(self.head, 2)
        self.half, self.low = self.z // 2, lax.rem(self.z, 2)
        self.next_z = self.at(z=2 * self.half + 1 - self.low)
        self.far_z = self.at(z=2 * (1 - self.half) + self.low)
        self.over = {
            "c": self.at(c=1 - self.c), "y": self.at(y=1 - self.y), "x": self.at(x=1 - self.x),
        }

    def at(self, **new):
        z, y, x, c = (new.get(name, getattr(self, name)) for name in "zyxc")
        return {"rows": z * 2 + y, "heads": x * 2 + c}

    def turn(self, step):
        first, second = lax.rem(step, 2), step // 2
        half = self.half + (1 - first) * (1 - 2 * self.half)
        low = self.low + (1 - second) * (1 - 2 * self.low)
        return 2 * half + low

    def side(self, name):
        return self.y if name == "y" else self.x


class Total:
    def __init__(self, where, order, got, mid, far, near, sems):
        self.where, self.order = where, order
        self.got, self.mid, self.far, self.near = got, mid, far, near
        self.core_out, self.core_in, self.out, self.inn, self.z_out, self.z_in, self.end = sems

    @staticmethod
    def scratch(order, rows, cols):
        shapes = [(2, 4, 2, rows, cols), (2, 4, rows, cols), (4, rows, cols), (4, rows, cols)]
        if order == "yzx":
            shapes[2:] = [(4, 2, rows, cols), (rows, cols)]
        sems = [(4,), (4,), (2, 4), (2, 4), (4,), (4,), (2,)]
        return [pltpu.VMEM(dims, BF16) for dims in shapes] + [pltpu.SemaphoreType.DMA(dims) for dims in sems]

    def core_copy(self, index, parts):
        source, target = parts(index)
        return remote(source, target, self.core_out.at[index], self.core_in.at[index], self.where.over["c"])

    def core_wait(self, index, target):
        arrived(target, self.core_in.at[index], self.where.over["c"])

    def part(self, ref, z, side):
        return ref.at[side, z] if self.order[0] == "x" else ref.at[:, z, side]

    def first_copy(self, step):
        w = self.where
        z = w.turn(step)
        source = self.part(self.got, z, 1 - w.side(self.order[0]))
        return remote(source, self.mid.at[:, z], self.out.at[0, step], self.inn.at[0, step], w.over[self.order[0]])

    def first(self, step):
        self.first_copy(step).start()

    def second_copy(self, step):
        w = self.where
        z = w.turn(step)
        source = self.mid.at[1 - w.side(self.order[1]), z]
        return remote(source, self.far.at[z], self.out.at[1, step], self.inn.at[1, step], w.over[self.order[1]])

    def second(self, step):
        w = self.where
        z = w.turn(step)
        arrived(self.mid.at[:, z], self.inn.at[0, step], w.over[self.order[0]])
        own = self.part(self.got, z, w.side(self.order[0]))
        self.mid[:, z] = (self.mid[:, z].astype(F32) + own[...].astype(F32)).astype(BF16)
        if self.order == "yzx":
            self.z_send(step)
        else:
            self.second_copy(step).start()

    def third(self, step):
        if self.order == "yzx":
            return
        w = self.where
        z = w.turn(step)
        arrived(self.far.at[z], self.inn.at[1, step], w.over[self.order[1]])
        own = self.mid[w.side(self.order[1]), z]
        self.far[z] = (self.far[z].astype(F32) + own.astype(F32)).astype(BF16)
        self.z_send(step)

    def z_slots(self):
        return self.far if self.order == "yzx" else self.near

    def z_block(self, step):
        z = self.where.turn(step)
        return self.mid.at[:, z] if self.order == "yzx" else self.far.at[z]

    def z_copy(self, step):
        device = self.where.next_z if step < 2 else self.where.far_z
        return remote(
            self.z_block(step), self.z_slots().at[step], self.z_out.at[step], self.z_in.at[step], device
        )

    def z_take(self, step):
        arrived(self.z_slots().at[step], self.z_in.at[step], self.where.next_z if step < 2 else self.where.far_z)
        return self.z_slots()[step].astype(F32)

    def z_send(self, step):
        if step < 2:
            self.z_copy(step).start()

    def relay(self):
        block = self.z_block(2)
        block[...] = (block[...].astype(F32) + self.z_take(0)).astype(BF16)
        self.z_copy(2).start()

    def z_sum(self):
        return self.z_block(3)[...].astype(F32) + self.z_take(1) + self.z_take(2)

    def x_copy(self):
        w = self.where
        return remote(self.far.at[3, 1 - w.x], self.near, self.end.at[0], self.end.at[1], w.over["x"])

    def fourth(self):
        if self.order != "yzx":
            return
        self.far[3] = self.z_sum().astype(BF16)
        self.x_copy().start()

    def result(self):
        w = self.where
        if self.order != "yzx":
            return self.z_sum()
        arrived(self.near, self.end.at[1], w.over["x"])
        return self.far[3, w.x].astype(F32) + self.near[...].astype(F32)

    def sent(self):
        for step in range(4):
            self.first_copy(step).wait_send()
            if self.order != "yzx":
                self.second_copy(step).wait_send()
        for step in range(3):
            self.z_copy(step).wait_send()
        if self.order == "yzx":
            self.x_copy().wait_send()


class Everyone:
    def __init__(self, where, by_head, by_row, sems):
        self.where, self.by_head, self.by_row, self.sems = where, by_head, by_row, sems
        self.own = by_head.at[where.head]

    @staticmethod
    def scratch(rows):
        return [pltpu.VMEM((4, rows, D), F32), pltpu.VMEM((8, rows, D), F32), pltpu.SemaphoreType.DMA((4, 8))]

    def head_copy(self, step):
        w = self.where
        return remote(
            self.own, self.own, self.sems.at[0, step], self.sems.at[1, w.head],
            {"rows": w.row, "heads": lax.rem(w.head + step, 4)},
        )

    def row_copy(self, step):
        w = self.where
        mine = self.by_row.at[w.row]
        return remote(
            mine, mine, self.sems.at[2, step], self.sems.at[3, w.row],
            {"rows": lax.rem(w.row + step, 8), "heads": w.head},
        )

    def start(self):
        for step in range(1, 4):
            self.head_copy(step).start()

    def middle(self):
        w = self.where
        for step in range(1, 4):
            head = lax.rem(w.head + step, 4)
            arrived(self.by_head.at[head], self.sems.at[1, head], {"rows": w.row, "heads": head})
        self.by_row[w.row] = (self.by_head[0] + self.by_head[1]) + (self.by_head[2] + self.by_head[3])
        for step in range(1, 8):
            self.row_copy(step).start()

    def result(self):
        w = self.where
        for step in range(1, 8):
            row = lax.rem(w.row + step, 8)
            arrived(self.by_row.at[row], self.sems.at[3, row], {"rows": row, "heads": w.head})
        total = self.by_row[0]
        for row in range(1, 8):
            total = total + self.by_row[row]
        return total

    def sent(self):
        for step in range(1, 4):
            self.head_copy(step).wait_send()
        for step in range(1, 8):
            self.row_copy(step).wait_send()


def rest_kernel(
    scale,
    r1_in, cotan, ctx_in, qkv_in, lse_in, x_in, lens, wup_in, wdown_in, wout_in, wqkv_in,
    g1v, s1v, g2v, s2v, bdv, bup,
    lay, xgr, down_to, up_to, out_to, qkv_to, vec_to,
    downo, upo, outo, qkvo, vec_out, mat_sem, r1, ycot, fb, act, slope, acc, dfb, dfbt, wup, wdown, down_send,
    load_sem, cot_sem, lay_sem, xg_sem, own_sem,
    *scratch,
):
    where = w = Place()
    scratch = list(scratch)

    def take(count):
        return [scratch.pop(0) for _ in range(count)]

    totals = []
    for order, _, _ in BLOCKS:
        refs = take(11)
        totals.append(Total(where, order, *refs[:4], refs[4:]))
    down, upa, upb, out = totals[:4]
    qkvs = (totals[4:6], totals[6:8])
    everyone = Everyone(where, *take(3))
    late = Everyone(where, *take(3))

    tokens = r1.shape[0]
    step_rows = 256
    parts = tokens // step_rows
    width = 768
    chunks = wup_in.shape[1] // width
    rows_mine = tokens // L
    part = lay.shape[1]
    r1_load = load(r1_in, r1, load_sem.at[0])
    wup_load = load(wup_in, wup, load_sem.at[1])
    wdown_load = load(wdown_in, wdown, load_sem.at[2])
    others = [lax.rem(w.head + step, 4) for step in range(1, 4)]
    partner = lambda other: {"rows": w.row, "heads": other}
    g1, s1, g2, s2, bd = (wide(item) for item in (g1v, s1v, g2v, s2v, bdv))
    mine = everyone.own
    mine[...] = jnp.zeros(mine.shape, F32)
    last = late.own
    last[...] = jnp.zeros(last.shape, F32)
    r1_load.wait()

    def lead(i, carry):
        rows = pl.ds(pl.multiple_of(i * step_rows, step_rows), step_rows)
        normed, _ = norm_parts(r1[rows, :])
        first = normed * g1 + s1
        fb[rows, :] = first.astype(BF16)
        acc[rows, :] = first + bd
        return carry

    lax.fori_loop(0, parts, lead, 0)
    meet([partner(other) for other in others] + [{"rows": lax.rem(w.row + step, 8), "heads": w.head} for step in range(1, 8)])

    def mine_in(row):
        place = pl.ds(row * L + w.head * part, part)
        return pltpu.make_async_copy(cotan.at[w.head * rows_mine + row], ycot.at[place], own_sem.at[2, row])

    def cot_copy(row, step):
        place = pl.ds(row * L + w.head * part, part)
        other = others[step]
        return remote(
            cotan.at[other * rows_mine + row], ycot.at[place], cot_sem.at[0, row, step], cot_sem.at[1, row, w.head],
            partner(other),
        )

    def give_back(source, target, sems, row, step):
        other = others[step]
        return remote(
            source.at[pl.ds(row * L + other * part, part)], target.at[w.head * rows_mine + row],
            sems.at[0, row, step], sems.at[1, row, w.head], partner(other),
        )

    def mine_out(source, target, index, row):
        place = pl.ds(row * L + w.head * part, part)
        return pltpu.make_async_copy(source.at[place], target.at[w.head * rows_mine + row], own_sem.at[index, row])

    for row in range(rows_mine):
        for step in range(3):
            cot_copy(row, step).start()
        mine_in(row).start()

    wup_load.wait()
    wdown_load.wait()

    def forward(c, carry):
        cols = pl.ds(pl.multiple_of(c * width, width), width)
        u, e = [None] * parts, [None] * parts
        for s in range(parts + 2):
            if s < parts:
                u[s] = mm(fb[s * step_rows : (s + 1) * step_rows, :], wup[:, cols]) + wide(bup.at[cols])
            if 0 <= s - 1 < parts:
                j = s - 1
                rows = slice(j * step_rows, (j + 1) * step_rows)
                cdf, pdf = normal_parts(u[j])
                e[j] = (u[j] * cdf).astype(BF16)
                act[rows, cols] = e[j]
                slope[rows, cols] = (cdf + u[j] * pdf).astype(BF16)
            if 0 <= s - 2 < parts:
                j = s - 2
                acc[j * step_rows : (j + 1) * step_rows, :] += mm(e[j], wdown[cols, :])
        return carry

    lax.fori_loop(0, chunks, forward, 0)
    for row in range(rows_mine):
        mine_in(row).wait()
        for other in others:
            arrived(ycot.at[pl.ds(row * L + other * part, part)], cot_sem.at[1, row, other], partner(other))

    def second(i, carry):
        rows = pl.ds(pl.multiple_of(i * step_rows, step_rows), step_rows)
        normed, spread = norm_parts(acc[rows, :])
        dy = ycot[rows, :].astype(F32)
        ycot[rows, :] = (normed * g2 + s2).astype(BF16)
        dr2 = norm_back(dy, normed, spread, g2)
        acc[rows, :] = dr2
        low = dr2.astype(BF16)
        dfb[rows, :] = low
        dfbt[:, :, rows] = low.T.reshape(4, D // 4, step_rows)
        mine[0:1, :] += jnp.sum(dy * normed, axis=0, keepdims=True)
        mine[1:2, :] += jnp.sum(dy, axis=0, keepdims=True)
        mine[2:3, :] += jnp.sum(low.astype(F32), axis=0, keepdims=True)
        return carry

    lax.fori_loop(0, parts, second, 0)

    for row in range(rows_mine):
        for step in range(3):
            give_back(ycot, lay, lay_sem, row, step).start()
        mine_out(ycot, lay, 0, row).start()

    def down_half(core, z):
        left = jnp.concatenate([dfbt[core], dfbt[2 + core]], axis=0)
        cols = pl.ds(pl.multiple_of(z * width, width), width)
        return mm(left, act[:, cols])

    quarter, eighth = D // 4, width // 2

    def down_parts(step):
        z = where.turn(step)
        return down_send.at[lax.rem(step, 2)], down.got.at[:, z]

    def down_other(step, carry):
        z = where.turn(step)
        total = down_half(1 - w.c, z)

        @pl.when(step >= 2)
        def _():
            down.core_copy(step - 2, down_parts).wait_send()

        slot = lax.rem(step, 2)
        for x in range(2):
            for y in range(2):
                piece = total[x * quarter : (x + 1) * quarter, y * eighth : (y + 1) * eighth]
                down_send[slot, x, y] = piece.astype(BF16)
        down.core_copy(step, down_parts).start()
        return carry

    def down_own(step, carry):
        z = where.turn(step)
        total = down_half(w.c, z)
        down.core_wait(step, down.got.at[:, z])
        for x in range(2):
            for y in range(2):
                piece = total[x * quarter : (x + 1) * quarter, y * eighth : (y + 1) * eighth]
                down.got[x, z, y] = (piece + down.got[x, z, y].astype(F32)).astype(BF16)
        down.first(step)
        return carry

    lax.fori_loop(0, 4, down_other, 0)
    lax.fori_loop(0, 4, down_own, 0)
    qkv_load = load(qkv_in, act.at[:, pl.ds(0, 3 * D)], load_sem.at[4])

    def backward(c, carry):
        cols = pl.ds(pl.multiple_of(c * width, width), width)
        de, du = [None] * parts, [None] * parts
        sums = jnp.zeros((1, width), F32)
        for s in range(parts + 2):
            if s < parts:
                de[s] = mm(dfb[s * step_rows : (s + 1) * step_rows, :], wdown[cols, :], NT)
            if 0 <= s - 1 < parts:
                j = s - 1
                rows = slice(j * step_rows, (j + 1) * step_rows)
                du[j] = (de[j] * slope[rows, cols].astype(F32)).astype(BF16)
                slope[rows, cols] = du[j]
                sums = sums + jnp.sum(du[j].astype(F32), axis=0, keepdims=True)
            if 0 <= s - 2 < parts:
                j = s - 2
                acc[j * step_rows : (j + 1) * step_rows, :] += mm(du[j], wup[:, cols], NT)
        mine[pl.ds(3 + c, 1), :] = sums
        return carry

    half = chunks // 2
    lax.fori_loop(0, half, backward, 0)
    down.second(0)
    lax.fori_loop(half, chunks, backward, 0)
    down.second(1)
    down.third(0)
    wqkv = wup.at[:, pl.ds(0, 3 * D)]
    x = wdown.at[pl.ds(2 * D, tokens)]
    wout = wup.at[:, pl.ds(3 * D, D)]
    wqkv_load = load(wqkv_in, wqkv, load_sem.at[5])
    wout_load = load(wout_in, wout, load_sem.at[3])
    x_load = load(x_in, x, load_sem.at[6])
    dab = dfb
    feats = wdown.at[pl.ds(2 * D + tokens, L)]
    for row in range(rows_mine):
        key_feat, query_feat = (feats.at[:, pl.ds((2 * row + item) * 128, 128)] for item in range(2))
        features(example_ends(lens, w.head * rows_mine + row), key_feat, query_feat, 0)

    def third(i, carry):
        rows = pl.ds(pl.multiple_of(i * step_rows, step_rows), step_rows)
        normed, spread = norm_parts(r1[rows, :])
        grad = acc[rows, :]
        dr = norm_back(grad, normed, spread, g1)
        acc[rows, :] = dr
        low = dr.astype(BF16)
        dab[rows, :] = low
        mine[7:8, :] += jnp.sum(grad * normed, axis=0, keepdims=True)
        last[2:3, :] += jnp.sum(grad, axis=0, keepdims=True)
        last[3:4, :] += jnp.sum(low.astype(F32), axis=0, keepdims=True)
        return carry

    lax.fori_loop(0, parts, third, 0)
    lse_load = [load(lse_in.at[g], r1.at[:, pl.ds(g * 128, 128)], load_sem.at[8 + g]) for g in range(2)]

    def up_half(core, x_side):
        cols = pl.ds(pl.multiple_of((2 * x_side + core) * width, width), width)
        return mm(fb[...], slope[:, cols], TN)

    ups = (upa, upb)

    def spot(side, index, cols, start):
        row = pl.multiple_of(side * D + index * (D // 2), D // 2)
        return wdown.at[pl.ds(row, D // 2), pl.ds(start, cols)]

    def pair_parts(each, index, cols, start):
        return lambda side: (spot(side, index, cols, start), each.got.at[side].reshape(D // 2, cols))

    def pair_other(pair, side, total, cols, start):
        total = total.astype(BF16).reshape(4, 2, 2, D // 16, cols)
        for index, each in enumerate(pair):
            spot(side, index, cols, start)[...] = total[:, :, index].reshape(D // 2, cols)
            each.core_copy(side, pair_parts(each, index, cols, start)).start()

    def pair_own(pair, side, turn, total, cols):
        total = total.reshape(4, 2, 2, D // 16, cols)
        for index, each in enumerate(pair):
            each.core_wait(side, each.got.at[side])
            each.got[side] = (total[:, :, index] + each.got[side].astype(F32)).astype(BF16)
        for when, each in enumerate((pair[1], pair[0])):

            @pl.when(turn == when)
            def _():
                for step in range(4):
                    each.first(step)

    def pair_sent(pair, cols, start):
        for index, each in enumerate(pair):
            for side in range(2):
                each.core_copy(side, pair_parts(each, index, cols, start)).wait_send()

    def far_first(turn):
        return lax.rem(w.x + 1 + turn, 2)

    def up_other(turn, carry):
        side = far_first(turn)
        pair_other(ups, side, up_half(1 - w.c, side), width, 0)
        return carry

    lax.fori_loop(0, 2, up_other, 0)
    down.second(2)
    down.third(1)

    def up_own(turn, carry):
        side = far_first(turn)
        pair_own(ups, side, turn, up_half(w.c, side), width)
        return carry

    lax.fori_loop(0, 2, up_own, 0)
    down.second(3)
    down.third(2)
    ctx = slope.at[:, pl.ds(3 * D, D)]
    grads = slope.at[:, pl.ds(0, 3 * D)]
    dctx = act.at[:, pl.ds(3 * D, D)]
    ctx_load = load(ctx_in, ctx, load_sem.at[7])
    wout_load.wait()

    def context_grad(row, carry):
        rows = pl.ds(pl.multiple_of(row * L, L), L)
        dctx[rows, :] = mm(dab[rows, :], wout[...], NT).astype(BF16)
        return carry

    lax.fori_loop(0, rows_mine, context_grad, 0)
    ctx_load.wait()
    wqkv_load.wait()

    def out_half(core, side):
        cols = pl.ds(pl.multiple_of(384 * side + 128 * core, 128), 256)
        return mm(ctx[...], dab[:, cols], TN)

    def out_parts(side):
        spot = wup.at[:, pl.ds(pl.multiple_of(3 * D + 256 * side, 256), 256)]
        return spot, out.got.at[side].reshape(D, 256)

    def out_other(side, carry):
        out_parts(side)[0][...] = out_half(1 - w.c, side).astype(BF16)
        out.core_copy(side, out_parts).start()
        return carry

    def out_own(side, carry):
        total = out_half(w.c, side).reshape(4, 2, D // 8, 256)
        out.core_wait(side, out.got.at[side])
        out.got[side] = (total + out.got[side].astype(F32)).astype(BF16)
        return carry

    lax.fori_loop(0, 2, out_other, 0)
    lax.fori_loop(0, 2, out_own, 0)
    for step in range(4):
        out.first(step)
    upa.second(0)
    everyone.start()

    qkv = act.at[:, pl.ds(0, 3 * D)]
    qkv_load.wait()
    for copy in lse_load:
        copy.wait()
    x_load.wait()

    def input_grad(row):
        rows = pl.ds(pl.multiple_of(row * L, L), L)
        fb[rows, :] = (mm(grads[rows, :], wqkv[...], NT) + acc[rows, :]).astype(BF16)
        for step in range(3):
            give_back(fb, xgr, xg_sem, row, step).start()
        mine_out(fb, xgr, 1, row).start()

    def qkv_half(core, side, group):
        if group == 0:
            start = side * 3 * 512 + (1 - side) * core * D
        else:
            start = side * (1152 + core * D) + (1 - side) * 384
        return mm(x[...], grads[:, pl.ds(pl.multiple_of(start, 128), 384)], TN)

    def qkv_other(group):
        def body(turn, carry):
            side = far_first(turn)
            pair_other(qkvs[group], side, qkv_half(1 - w.c, side, group), 384, group * 384)
            return carry

        lax.fori_loop(0, 2, body, 0)

    def qkv_own(group):
        def body(turn, carry):
            side = far_first(turn)
            pair_own(qkvs[group], side, turn, qkv_half(w.c, side, group), 384)
            return carry

        lax.fori_loop(0, 2, body, 0)

    def heads_back(i, carry):
        group, row = i // 2, lax.rem(i, 2)
        rows = pl.ds(pl.multiple_of(row * L, L), L)
        keep = r1[rows, pl.ds(pl.multiple_of(group * 128, 128), 128)]
        lanes = [pl.ds(pl.multiple_of(2 * row * 128 + 128 * item, 128), 128) for item in range(2)]
        attend_back(rows, group, 3, qkv, ctx, dctx, keep, grads, feats[:, lanes[0]], feats[:, lanes[1]])

        @pl.when(i == 0)
        def _():
            upa.second(1)
            upb.second(0)
            upb.second(1)
            down.relay()
            pair_sent(ups, width, 0)

        @pl.when(i == 1)
        def _():
            upa.second(2)
            upa.second(3)
            upb.second(2)
            qkv_other(0)
            qkv_own(0)

        @pl.when(i == 2)
        def _():
            upb.second(3)
            upb.third(0)
            for step in range(4):
                out.second(step)
            everyone.middle()
            upa.relay()
            down.fourth()

        @pl.when(i == 3)
        def _():
            last[0:1, :] = jnp.sum(grads[:, 0:D].astype(F32), axis=0, keepdims=True)
            last[1:2, :] = jnp.sum(grads[:, 2 * D : 3 * D].astype(F32), axis=0, keepdims=True)
            late.start()

        @pl.when(i == 2)
        def _():
            input_grad(0)

        return carry

    lax.fori_loop(0, 4, heads_back, 0)
    qkv_other(1)
    (qkva, qkvb), (ena, enb) = qkvs
    for step in range(1, 4):
        upb.third(step)
    for step in range(4):
        qkvb.second(step)
    out.relay()
    qkv_own(1)
    for step in range(4):
        qkva.second(step)
    upa.fourth()
    upb.relay()
    late.middle()
    input_grad(1)
    downo[...] = down.result() * scale
    kept = [load(downo, down_to, mat_sem.at[0])]
    eighth_rows = D // 16
    for step in range(4):
        qkvb.third(step)
    enb.second(0)
    enb.second(1)
    ena.second(0)
    ena.second(1)
    enb.second(2)
    enb.second(3)
    qkva.relay()
    qkvb.relay()
    ena.second(2)
    ena.second(3)
    enb.third(0)
    enb.third(1)
    out.fourth()
    ena.relay()
    enb.third(2)
    enb.third(3)
    upo[eighth_rows:, :] = upb.result() * scale
    enb.relay()
    qkva.fourth()
    outo[...] = pick(out.result() * scale, w.c, 192)
    kept.append(load(outo, out_to, mat_sem.at[1]))
    upo[0:eighth_rows, :] = upa.result() * scale
    kept.append(load(upo, up_to, mat_sem.at[2]))
    vectors = everyone.result() * scale
    vec_out[12:16, :] = jnp.zeros((4, D), F32)
    for index, item in ((3, 7), (5, 2), (6, 0), (7, 1), (8, 3), (9, 4), (10, 5), (11, 6)):
        vec_out[index : index + 1, :] = vectors[item : item + 1, :]
    for index in range(2):
        down.core_copy(2 + index, down_parts).wait_send()
        out.core_copy(index, out_parts).wait_send()
    for total in totals[:4]:
        total.sent()
    everyone.sent()
    for row in range(rows_mine):
        for step in range(3):
            cot_copy(row, step).wait_send()
            give_back(ycot, lay, lay_sem, row, step).wait_send()
        for other in others:
            arrived(lay.at[other * rows_mine + row], lay_sem.at[1, row, other], partner(other))
        mine_out(ycot, lay, 0, row).wait()
    for group in range(2):
        pair_sent(qkvs[group], 384, group * 384)
    early = jnp.concatenate([qkva.result(), qkvb.result()], axis=0) * scale
    qkva.sent()
    qkvb.sent()
    ends = late.result() * scale
    vec_out[0:2, :] = ends[0:2, :]
    vec_out[2:3, :] = ends[3:4, :]
    vec_out[4:5, :] = ends[2:3, :]
    kept.append(load(vec_out, vec_to, mat_sem.at[3]))
    late.sent()
    ena.fourth()
    late_part = jnp.concatenate([ena.result(), enb.result()], axis=0) * scale
    for corner, (one, two) in enumerate(
        (
            ((0, 384, 0), (384, 192, 0)), ((192, 384, 0), (0, 192, 192)),
            ((384, 192, 0), (0, 384, 0)), ((0, 192, 192), (192, 384, 0)),
        )
    ):

        @pl.when(w.head == corner)
        def _():
            for value, (place, size, start) in ((early, one), (late_part, two)):
                qkvo[:, place : place + size] = value[:, start : start + size]

    kept.append(load(qkvo, qkv_to, mat_sem.at[4]))
    for row in range(rows_mine):
        for other in others:
            arrived(xgr.at[other * rows_mine + row], xg_sem.at[1, row, other], partner(other))
        for step in range(3):
            give_back(fb, xgr, xg_sem, row, step).wait_send()
        mine_out(fb, xgr, 1, row).wait()
    ena.sent()
    enb.sent()
    for copy in kept:
        copy.wait()


def pick(values, core, width):
    return jnp.where(core == 0, values[:, :width], values[:, 64 : 64 + width])


VMEM = pl.BlockSpec(memory_space=pltpu.VMEM)
SMEM = pl.BlockSpec(memory_space=pltpu.SMEM)


def shape(dims, kind):
    return jax.ShapeDtypeStruct(dims, kind)


def params(**more):
    return pltpu.CompilerParams(vmem_limit_bytes=255 * 2**18, **more)


def local(
    hidden_in, lengths, qkv_weight, query_bias, value_bias, out_weight, out_bias, gain_one,
    shift_one, up_weight, up_bias, down_weight, down_bias, gain_two, shift_two, cotangent,
):
    row_count, part_len = hidden_in.shape[0], hidden_in.shape[1]
    heads = lax.axis_size("heads")
    mine = row_count // heads
    tokens = mine * L
    ff = up_weight.shape[1]
    place = lax.axis_index("heads")
    x = lax.all_to_all(hidden_in, "heads", split_axis=0, concat_axis=1, tiled=True).reshape(tokens, D)
    cot = lax.all_to_all(cotangent, "heads", split_axis=0, concat_axis=1, tiled=True).reshape(tokens, D)
    lens = lax.dynamic_slice_in_dim(lengths, place * mine, mine, 0)
    bqkv = jnp.concatenate([query_bias, jnp.zeros_like(query_bias), value_bias]).astype(F32)[None]
    qkv, ctx, r1, lse = pl.pallas_call(
        first_kernel,
        out_shape=(
            shape((tokens, 3 * D), BF16), shape((tokens, D), BF16), shape((tokens, D), F32),
            shape((2, tokens, 128), F32),
        ),
        in_specs=[VMEM, SMEM] + [VMEM] * 4,
        out_specs=(VMEM,) * 4,
        scratch_shapes=[pltpu.VMEM((tokens, 128), BF16)] * 2,
        compiler_params=params(),
        name="first",
    )(x, lens, qkv_weight, bqkv, out_weight, out_bias.astype(F32)[None])
    vecs = jnp.stack([gain_one, shift_one, gain_two, shift_two, down_bias]).astype(F32)
    y, dr1, dctx, downg, upg, outg, vec_mid, upb = pl.pallas_call(
        middle_kernel,
        out_shape=(
            shape((tokens, D), BF16), shape((tokens, D), F32), shape((tokens, D), BF16),
            shape((D, ff), BF16), shape((D, ff), BF16), shape((D, D), BF16),
            shape((8, D), F32), shape((1, ff), F32),
        ),
        in_specs=[VMEM] * 8,
        out_specs=(VMEM,) * 8,
        scratch_shapes=[
            pltpu.VMEM((tokens, D), BF16), pltpu.VMEM((tokens, ff), BF16), pltpu.VMEM((tokens, ff), BF16),
            pltpu.VMEM((tokens, D), F32), pltpu.VMEM((tokens, D), BF16), pltpu.VMEM((tokens, D), BF16),
        ],
        compiler_params=params(),
        name="middle",
    )(r1, ctx, cot, vecs, up_weight, up_bias.astype(F32)[None], down_weight, out_weight)
    xg, qkvg, vec_last = pl.pallas_call(
        last_kernel,
        out_shape=(shape((tokens, D), BF16), shape((D, 3 * D), BF16), shape((8, D), F32)),
        in_specs=[VMEM, SMEM] + [VMEM] * 6,
        out_specs=(VMEM,) * 3,
        scratch_shapes=[pltpu.VMEM((tokens, 3 * D), BF16)] + [pltpu.VMEM((tokens, 128), BF16)] * 2,
        compiler_params=params(),
        name="last",
    )(x, lens, qkv, ctx, dctx, lse, dr1, qkv_weight)

    def back(values):
        values = values.reshape(mine, L, D)
        return lax.all_to_all(values, "heads", split_axis=1, concat_axis=0, tiled=True)

    layer_out = back(y)
    input_grad = back(xg).astype(F32)
    scale = 1.0 / (row_count * lax.axis_size("rows"))
    vec_mid, vec_last, upb = lax.psum((vec_mid, vec_last, upb), ("rows", "heads"))

    def reduce(values, flip):
        one, two = (0, 1) if flip else (1, 0)
        half = lax.psum_scatter(values, "heads", scatter_dimension=one, tiled=True).astype(F32)
        total = lax.psum_scatter(half, "rows", scatter_dimension=two, tiled=True) * scale
        return total.T if flip else total

    vm, vl = vec_mid * scale, vec_last * scale
    return (
        layer_out, input_grad, reduce(qkvg, False), vl[0], vl[1], reduce(outg, False), vm[5], vm[3], vm[4],
        reduce(upg, False), upb[0] * scale, reduce(downg, True), vm[2], vm[0], vm[1],
    )


ANY = pl.BlockSpec(memory_space=pl.ANY)
DMA = pltpu.SemaphoreType.DMA
BLOCKS = (
    ("yzx", 192, 384), ("yzx", 48, 768), ("xyz", 48, 768), ("yzx", 96, 256), ("yzx", 48, 384), ("xyz", 48, 384),
    ("yzx", 48, 384), ("xyz", 48, 384),
)


def finish_kernel(count, *refs):
    lay, xgr, vec = refs[:3]
    mats = refs[3 : 3 + count]
    lay_out, xg_out = refs[3 + count : 5 + count]
    mats_out = refs[5 + count : 5 + 2 * count]
    vecs_out = refs[5 + 2 * count : 14 + 2 * count]
    through, low, full, sems = refs[14 + 2 * count : 18 + 2 * count]
    mats_here, mat_sems = refs[18 + 2 * count : 18 + 3 * count], refs[-1]
    blocks = xgr.shape[0]
    wides = [load(xgr.at[i], low.at[i], sems.at[0, i]) for i in range(blocks)]
    lays = [load(lay.at[i], through.at[i], sems.at[1, i]) for i in range(blocks)]
    arrive = [load(mats[i], mats_here[i], mat_sems.at[0, i]) for i in range(count)]
    for index in range(8):
        vecs_out[index][...] = vec[index, :]
    for index in range(4):
        vecs_out[8][index * D : (index + 1) * D] = vec[8 + index, :]
    copies = []
    for i in range(blocks):
        wides[i].wait()
        full[i] = low[i].astype(F32)
        copies.append(load(full.at[i], xg_out.at[i], sems.at[2, i]))
    for i in range(blocks):
        lays[i].wait()
        copies.append(load(through.at[i], lay_out.at[i], sems.at[3, i]))
    for i in range(count):
        arrive[i].wait()
        copies.append(load(mats_here[i], mats_out[i], mat_sems.at[1, i]))
    for copy in copies:
        copy.wait()


def local_fast(
    hidden_in, lengths, qkv_weight, query_bias, value_bias, out_weight, out_bias, gain_one,
    shift_one, up_weight, up_bias, down_weight, down_bias, gain_two, shift_two, cotangent,
):
    row_count, part_len = hidden_in.shape[0], hidden_in.shape[1]
    mine = row_count // lax.axis_size("heads")
    heads = lax.axis_size("heads")
    tokens = mine * L
    ff = up_weight.shape[1]
    bf = lambda *dims: pltpu.VMEM(dims, BF16)
    fl = lambda *dims: pltpu.VMEM(dims, F32)
    x, qkv, ctx, r1, lse = pl.pallas_call(
        gather_kernel,
        out_shape=(
            shape((tokens, D), BF16), shape((tokens, 3 * D), BF16),
            shape((tokens, D), BF16), shape((tokens, D), F32), shape((2, tokens, 128), F32),
        ),
        in_specs=[ANY, VMEM, ANY, VMEM, VMEM, ANY, VMEM],
        out_specs=(ANY,) * 5,
        scratch_shapes=[
            bf(tokens, D), bf(tokens, 3 * D), bf(tokens, D), fl(tokens, D), fl(2, tokens, 128), bf(D, 3 * D),
            bf(D, D), fl(8, D), bf(tokens, 128), bf(tokens, 128),
            DMA((2,)), DMA((mine,)), DMA((5, mine)), DMA((mine, heads - 1)), DMA((mine, heads)),
        ],
        compiler_params=params(collective_id=0, has_side_effects=True),
        name="gather",
    )(hidden_in, lengths.T, qkv_weight, query_bias, value_bias, out_weight, out_bias)
    scale = 1.0 / (row_count * lax.axis_size("rows"))
    totals = []
    for order, rows, cols in BLOCKS:
        totals += Total.scratch(order, rows, cols)
    mats = (shape((192, 384), F32), shape((96, 768), F32), shape((96, 192), F32), shape((96, 576), F32))
    wide_out = shape((row_count, part_len, D), BF16)
    lay, xgr, downg, upg, outg, qkvg, vec = pl.pallas_call(
        functools.partial(rest_kernel, scale),
        out_shape=(wide_out, wide_out) + mats + (shape((16, D), F32),),
        in_specs=[ANY] * 6 + [VMEM] + [ANY] * 4 + [VMEM] * 6,
        out_specs=(ANY,) * 7,
        scratch_shapes=[fl(*item.shape) for item in mats] + [
            fl(16, D), DMA((5,)),
            fl(tokens, D), bf(tokens, D), bf(tokens, D), bf(tokens, ff), bf(tokens, ff),
            fl(tokens, D), bf(tokens, D), bf(4, D // 4, tokens), bf(D, ff), bf(ff, D),
            bf(2, 2, 2, 192, 384), DMA((10,)), DMA((2, mine, 4)), DMA((2, mine, 4)), DMA((2, mine, 4)), DMA((3, mine)),
        ]
        + totals
        + Everyone.scratch(8)
        + Everyone.scratch(8),
        compiler_params=params(collective_id=1, has_side_effects=True),
        name="rest",
    )(
        r1, cotangent, ctx, qkv, lse, x, lengths.T, up_weight, down_weight, out_weight, qkv_weight,
        gain_one, shift_one, gain_two, shift_two, down_bias, up_bias,
    )
    results = pl.pallas_call(
        functools.partial(finish_kernel, 4),
        out_shape=(wide_out, shape((row_count, part_len, D), F32)) + mats + (shape((D,), F32),) * 8 + (shape((ff,), F32),),
        in_specs=[ANY, ANY, VMEM] + [ANY] * 4,
        out_specs=(ANY,) * 6 + (VMEM,) * 9,
        scratch_shapes=[
            bf(row_count, part_len, D), bf(row_count, part_len, D), fl(row_count, part_len, D), DMA((4, row_count)),
        ]
        + [fl(*item.shape) for item in mats]
        + [DMA((2, 4))],
        compiler_params=params(),
        name="finish",
    )(lay, xgr, vec, downg, upg, outg, qkvg)
    layer_out, input_grad, downg, upg, outg, qkvg, qb, vb, ob, go, so, db, gt, st, ub = results
    return layer_out, input_grad, qkvg, qb, vb, outg, ob, go, so, upg, ub, downg.T, db, gt, st


def solution(mesh):
    split = P("rows", "heads", None)
    grid = P("rows", "heads")
    in_specs = (split, P("rows", None)) + (P(),) * 13 + (split,)
    out_specs = (split, split, grid, P(), P(), grid, P(), P(), P(), grid, P(), grid, P(), P(), P())
    fast = mesh.shape["rows"] == 8 and mesh.shape["heads"] == 4
    return jax.shard_map(
        local_fast if fast else local, mesh=mesh, in_specs=in_specs, out_specs=out_specs, check_vma=False
    )
```

```python
import functools

import jax
import jax.numpy as jnp
from jax import lax
from jax.experimental import pallas as pl
from jax.experimental.pallas import tpu as pltpu
from jax.sharding import PartitionSpec as P

DH = 64
D = 768
L = 512
EPSILON = 1e-12
OFF = -(2.0**100)
F32 = jnp.float32
BF16 = jnp.bfloat16
NN = (((1,), (0,)), ((), ()))
NT = (((1,), (1,)), ((), ()))
TN = (((0,), (0,)), ((), ()))

RATE = 0.285
TAIL = (
    0.11576503423350087,
    0.08983941546025678,
    0.2103671707394457,
    -0.14882089196252246,
    0.3285619517018635,
    -0.09571266010718714,
)


def mm(left, right, dims=NN):
    return lax.dot_general(left, right, dims, preferred_element_type=F32)


def normal_parts(u):
    bell = jnp.exp2(u * u * -0.7213475204444817)
    t = pltpu.reciprocal(1.0 + RATE * jnp.abs(u))
    poly = TAIL[-1]
    for item in TAIL[-2::-1]:
        poly = poly * t + item
    tail = poly * t * bell
    return jnp.where(u >= 0, 1.0 - tail, tail), bell * 0.3989422804014327


def norm_parts(values):
    middle = jnp.mean(values, axis=-1, keepdims=True)
    center = values - middle
    spread = jnp.mean(center * center, axis=-1, keepdims=True)
    scale = lax.rsqrt(spread + EPSILON)
    return center * scale, scale


def norm_back(grad, normed, scale, gain):
    dn = grad * gain
    first = jnp.mean(dn, axis=-1, keepdims=True)
    second = jnp.mean(dn * normed, axis=-1, keepdims=True)
    return (dn - first - normed * second) * scale


def split3(values):
    high = values.astype(BF16)
    rest = values - high.astype(F32)
    mid = rest.astype(BF16)
    return high, mid, (rest - mid.astype(F32)).astype(BF16)


def features(ends, key_feat, query_feat, start):
    token = lax.broadcasted_iota(jnp.int32, (L, 128), 0)
    place = lax.broadcasted_iota(jnp.int32, (L, 128), 1) & (DH - 1)
    seg = jnp.zeros((L, 128), jnp.int32)
    for end in ends:
        seg = seg + (token >= end).astype(jnp.int32)
    count = len(ends)
    ones = (place == seg) | ((place >= count) & (place < count + 3))
    key_feat[pl.ds(start, L), :] = jnp.where(ones, 1.0, 0.0).astype(BF16)
    off = (place < count) & (place != seg)
    query_feat[pl.ds(start, L), :] = jnp.where(off, OFF, 0.0).astype(BF16)


def attend(rows, group, pairs, qkv, ctx, lse, key_feat, query_feat):
    lane = lax.broadcasted_iota(jnp.int32, (1, 128), 1)
    kf, qf = key_feat[rows, :], query_feat[rows, :]
    ops, values = [], []
    for pair in range(pairs):
        col = pl.multiple_of(group * (pairs * 128) + pair * 128, 128)
        q2 = qkv[rows, pl.ds(col, 128)]
        k2 = qkv[rows, pl.ds(D + col, 128)]
        values.append(qkv[rows, pl.ds(2 * D + col, 128)])
        for own in (lane < DH, lane >= DH):
            ops.append((jnp.where(own, q2, qf), jnp.where(own, k2, kf)))
    count = 2 * pairs
    scores = [None] * count
    outs, sums = [], []
    scores[0] = mm(*ops[0], NT)
    for head in range(count):
        if head + 1 < count:
            scores[head + 1] = mm(*ops[head + 1], NT)
        peak = jnp.max(scores[head], axis=1, keepdims=True)
        expo = jnp.exp(scores[head] - peak)
        total = jnp.sum(expo, axis=1, keepdims=True)
        out = mm(expo.astype(BF16), values[head // 2])
        outs.append(out * (1.0 / total))
        sums.append(peak + jnp.log(total))
    keep = jnp.zeros((L, 128), F32)
    for head in range(count):
        keep = jnp.where(lane == head, sums[head], keep)
    lse[group, rows, :] = keep
    for pair in range(pairs):
        col = pl.multiple_of(group * (pairs * 128) + pair * 128, 128)
        both = jnp.where(lane < DH, outs[2 * pair], outs[2 * pair + 1])
        ctx[rows, pl.ds(col, 128)] = both.astype(BF16)


def attend_back(rows, group, pairs, qkv, ctx, dctx, keep, grads, kf, qf):
    lane = lax.broadcasted_iota(jnp.int32, (1, 128), 1)
    place = lane & (DH - 1)
    vf = jnp.where((place >= 4) & (place < 7), 1.0, 0.0).astype(BF16)

    def spread(column, base):
        high, mid, small = split3(-column)
        return jnp.where(
            place == 4, high, jnp.where(place == 5, mid, jnp.where(place == 6, small, base))
        )

    ops = []
    for pair in range(pairs):
        col = pl.multiple_of(group * (pairs * 128) + pair * 128, 128)
        q2 = qkv[rows, pl.ds(col, 128)]
        k2 = qkv[rows, pl.ds(D + col, 128)]
        v2 = qkv[rows, pl.ds(2 * D + col, 128)]
        d2 = dctx[rows, pl.ds(col, 128)]
        both = d2.astype(F32) * ctx[rows, pl.ds(col, 128)].astype(F32)
        zero = jnp.zeros_like(q2)
        for side, own in enumerate((lane < DH, lane >= DH)):
            inner = jnp.sum(jnp.where(own, both, 0.0), axis=1, keepdims=True)
            total = keep[:, 2 * pair + side : 2 * pair + side + 1]
            ops.append(
                (
                    jnp.where(own, k2, kf),
                    jnp.where(own, q2, spread(total, qf)),
                    jnp.where(own, v2, vf),
                    jnp.where(own, d2, spread(inner, zero)),
                    jnp.where(own, q2, zero),
                    jnp.where(own, k2, zero),
                    jnp.where(own, d2, zero),
                )
            )
    count = 2 * pairs
    scores, chances = [None] * count, [None] * count
    dq, dk, dv = [0] * pairs, [0] * pairs, [0] * pairs

    def start(head):
        scores[head] = mm(ops[head][0], ops[head][1], NT)
        chances[head] = mm(ops[head][2], ops[head][3], NT)

    start(0)
    for head in range(count):
        if head + 1 < count:
            start(head + 1)
        chance = jnp.exp(scores[head])
        low = chance.astype(BF16)
        ds = (chance * chances[head]).astype(BF16)
        pair = head // 2
        dk[pair] += mm(ds, ops[head][4])
        dv[pair] += mm(low, ops[head][6])
        dq[pair] += mm(ds, ops[head][5], TN)
    for pair in range(pairs):
        col = pl.multiple_of(group * (pairs * 128) + pair * 128, 128)
        grads[rows, pl.ds(col, 128)] = (dq[pair] * DH**-0.5).astype(BF16)
        grads[rows, pl.ds(D + col, 128)] = dk[pair].astype(BF16)
        grads[rows, pl.ds(2 * D + col, 128)] = dv[pair].astype(BF16)


def first_kernel(x, lens, wqkv, bqkv, wout, bout, qkv, ctx, r1, lse, key_feat, query_feat):
    for row in range(x.shape[0] // L):
        ends, total = [], 0
        for item in range(lens.shape[1]):
            total = total + lens[row, item]
            ends.append(total)
        features(ends, key_feat, query_feat, row * L)

        rows = pl.ds(row * L, L)
        for part in range(3):
            cols = pl.ds(part * D, D)
            acc = mm(x[rows, :], wqkv[:, cols]) + bqkv[:, cols]
            if part == 0:
                acc = acc * DH**-0.5
            qkv[rows, cols] = acc.astype(BF16)

        def heads(group, carry):
            attend(rows, group, 3, qkv, ctx, lse, key_feat, query_feat)
            return carry

        lax.fori_loop(0, 2, heads, 0)
        r1[rows, :] = mm(ctx[rows, :], wout[...]) + bout[...] + x[rows, :].astype(F32)


def middle_kernel(
    r1, ctx, cot, vecs, wup, bup, wdown, wout,
    y, dr1, dctx, downg, upg, outg, vec_grads, upb_grad,
    fb, act, slope, acc, dfb, dab,
):
    tokens = r1.shape[0]
    step = 256
    parts = tokens // step
    width = 768
    chunks = wup.shape[1] // width
    g1, s1, g2, s2, bd = (vecs[i : i + 1, :] for i in range(5))
    vec_grads[...] = jnp.zeros_like(vec_grads)
    upb_grad[...] = jnp.zeros_like(upb_grad)

    def lead(i, carry):
        rows = pl.ds(pl.multiple_of(i * step, step), step)
        normed, _ = norm_parts(r1[rows, :])
        first = normed * g1 + s1
        fb[rows, :] = first.astype(BF16)
        acc[rows, :] = first + bd
        return carry

    lax.fori_loop(0, parts, lead, 0)

    def forward(c, carry):
        cols = pl.ds(pl.multiple_of(c * width, width), width)
        u, e = [None] * parts, [None] * parts
        for s in range(parts + 2):
            if s < parts:
                u[s] = mm(fb[s * step : (s + 1) * step, :], wup[:, cols]) + bup[:, cols]
            if 0 <= s - 1 < parts:
                j = s - 1
                rows = slice(j * step, (j + 1) * step)
                cdf, pdf = normal_parts(u[j])
                e[j] = (u[j] * cdf).astype(BF16)
                act[rows, cols] = e[j]
                slope[rows, cols] = (cdf + u[j] * pdf).astype(BF16)
            if 0 <= s - 2 < parts:
                j = s - 2
                acc[j * step : (j + 1) * step, :] += mm(e[j], wdown[cols, :])
        return carry

    lax.fori_loop(0, chunks, forward, 0)

    def second(i, carry):
        rows = pl.ds(pl.multiple_of(i * step, step), step)
        normed, scale = norm_parts(acc[rows, :])
        y[rows, :] = (normed * g2 + s2).astype(BF16)
        dy = cot[rows, :].astype(F32)
        dr2 = norm_back(dy, normed, scale, g2)
        acc[rows, :] = dr2
        low = dr2.astype(BF16)
        dfb[rows, :] = low
        vec_grads[0:1, :] += jnp.sum(dy * normed, axis=0, keepdims=True)
        vec_grads[1:2, :] += jnp.sum(dy, axis=0, keepdims=True)
        vec_grads[2:3, :] += jnp.sum(low.astype(F32), axis=0, keepdims=True)
        return carry

    lax.fori_loop(0, parts, second, 0)

    def down(c, carry):
        cols = pl.ds(pl.multiple_of(c * width, width), width)
        downg[:, cols] = mm(dfb[...], act[:, cols], TN).astype(BF16)
        return carry

    lax.fori_loop(0, chunks, down, 0)

    def backward(c, carry):
        cols = pl.ds(pl.multiple_of(c * width, width), width)
        de, du = [None] * parts, [None] * parts
        sums = jnp.zeros((1, width), F32)
        for s in range(parts + 2):
            if s < parts:
                de[s] = mm(dfb[s * step : (s + 1) * step, :], wdown[cols, :], NT)
            if 0 <= s - 1 < parts:
                j = s - 1
                rows = slice(j * step, (j + 1) * step)
                du[j] = (de[j] * slope[rows, cols].astype(F32)).astype(BF16)
                slope[rows, cols] = du[j]
                sums = sums + jnp.sum(du[j].astype(F32), axis=0, keepdims=True)
            if 0 <= s - 2 < parts:
                j = s - 2
                acc[j * step : (j + 1) * step, :] += mm(du[j], wup[:, cols], NT)
        upb_grad[:, cols] = sums
        return carry

    lax.fori_loop(0, chunks, backward, 0)

    def third(i, carry):
        rows = pl.ds(pl.multiple_of(i * step, step), step)
        normed, scale = norm_parts(r1[rows, :])
        grad = acc[rows, :]
        dr = norm_back(grad, normed, scale, g1)
        dr1[rows, :] = dr
        low = dr.astype(BF16)
        dab[rows, :] = low
        vec_grads[3:4, :] += jnp.sum(grad * normed, axis=0, keepdims=True)
        vec_grads[4:5, :] += jnp.sum(grad, axis=0, keepdims=True)
        vec_grads[5:6, :] += jnp.sum(low.astype(F32), axis=0, keepdims=True)
        return carry

    lax.fori_loop(0, parts, third, 0)
    dctx[...] = mm(dab[...], wout[...], NT).astype(BF16)
    outg[...] = mm(ctx[...], dab[...], TN).astype(BF16)

    def up(c, carry):
        cols = pl.ds(pl.multiple_of(c * width, width), width)
        upg[:, cols] = mm(fb[...], slope[:, cols], TN).astype(BF16)
        return carry

    lax.fori_loop(0, chunks, up, 0)


def last_kernel(x, lens, qkv, ctx, dctx, lse, dr1, wqkv, xg, qkvg, vec_grads, grads, key_feat, query_feat):
    vec_grads[...] = jnp.zeros_like(vec_grads)
    for row in range(x.shape[0] // L):
        ends, total = [], 0
        for item in range(lens.shape[1]):
            total = total + lens[row, item]
            ends.append(total)
        features(ends, key_feat, query_feat, row * L)

        rows = pl.ds(row * L, L)

        def heads(group, carry):
            attend_back(
                rows, group, 3, qkv, ctx, dctx, lse[group, rows, :], grads, key_feat[rows, :], query_feat[rows, :]
            )
            return carry

        lax.fori_loop(0, 2, heads, 0)
    vec_grads[0:1, :] = jnp.sum(grads[:, 0:D].astype(F32), axis=0, keepdims=True)
    vec_grads[1:2, :] = jnp.sum(grads[:, 2 * D : 3 * D].astype(F32), axis=0, keepdims=True)
    for part in range(3):
        cols = slice(part * D, (part + 1) * D)
        qkvg[:, cols] = mm(x[...], grads[:, cols], TN).astype(BF16)
    xg[...] = (mm(grads[...], wqkv[...], NT) + dr1[...]).astype(xg.dtype)


MESH = pl.DeviceIdType.MESH


def load(source, target, sem):
    copy = pltpu.make_async_copy(source, target, sem)
    copy.start()
    return copy


def remote(source, target, out_sem, in_sem, device):
    return pltpu.make_async_remote_copy(
        src_ref=source, dst_ref=target, send_sem=out_sem, recv_sem=in_sem,
        device_id=device, device_id_type=MESH,
    )


def arrived(target, in_sem, device):
    remote(target, target, in_sem, in_sem, device).wait_recv()


def meet(devices):
    barrier = pltpu.get_barrier_semaphore()
    for device in devices:
        pl.semaphore_signal(barrier, inc=1, device_id=device, device_id_type=MESH)
    pl.semaphore_wait(barrier, len(devices))


def example_ends(lens, row):
    place = lax.broadcasted_iota(jnp.int32, lens.shape, 1)
    counts = jnp.sum(jnp.where(place == row, lens[...], 0).astype(F32), axis=1, keepdims=True)
    ends, total = [], 0
    for item in range(lens.shape[0]):
        total = total + counts[item : item + 1, :]
        ends.append(total.astype(jnp.int32))
    return ends


def wide(vector):
    return vector[...].astype(F32).reshape(1, vector.shape[0])


def gather_kernel(
    hidden, lens, wqkv_in, bq, bv, wout_in, bout,
    x_out, qkv_out, ctx_out, r1_out, lse_out,
    x, qkv, ctx, r1, lse, wqkv, wout, bias, key_feat, query_feat,
    load_sem, own_sem, keep_sem, out_sems, in_sems,
):
    me = lax.axis_index("heads")
    row_id = lax.axis_index("rows")
    heads = lax.axis_size("heads")
    part = hidden.shape[1]
    rows_mine = x.shape[0] // L
    wqkv_load = load(wqkv_in, wqkv, load_sem.at[0])
    wout_load = load(wout_in, wout, load_sem.at[1])
    others = [lax.rem(me + step, heads) for step in range(1, heads)]
    device = lambda other: {"rows": row_id, "heads": other}

    def kept(row):
        return pltpu.make_async_copy(
            hidden.at[me * rows_mine + row], x.at[pl.ds(row * L + me * part, part)], own_sem.at[row]
        )

    def passed(row, step):
        other = others[step]
        return remote(
            hidden.at[other * rows_mine + row], x.at[pl.ds(row * L + me * part, part)],
            out_sems.at[row, step], in_sems.at[row, me], device(other),
        )

    def stores(row):
        rows = pl.ds(pl.multiple_of(row * L, L), L)
        return [
            pltpu.make_async_copy(source, target, keep_sem.at[index, row])
            for index, (source, target) in enumerate(
                (
                    (x.at[rows], x_out.at[rows]), (qkv.at[rows], qkv_out.at[rows]), (ctx.at[rows], ctx_out.at[rows]),
                    (lse.at[:, rows], lse_out.at[:, rows]), (r1.at[rows], r1_out.at[rows]),
                )
            )
        ]

    meet([device(other) for other in others])
    for row in range(rows_mine):
        for step in range(heads - 1):
            passed(row, step).start()
        kept(row).start()
    bias[0:1, :] = wide(bq)
    bias[1:2, :] = jnp.zeros((1, D), F32)
    bias[2:3, :] = wide(bv)
    out_bias = wide(bout)
    for row in range(rows_mine):
        features(example_ends(lens, me * rows_mine + row), key_feat, query_feat, row * L)
    wqkv_load.wait()
    side, sibling = me // 2, me + 1 - 2 * lax.rem(me, 2)
    near = L // (heads // 2)

    def project(row, half):
        rows = pl.ds(pl.multiple_of(row * L + half * near, near), near)
        for item in range(3):
            cols = pl.ds(item * D, D)
            acc = mm(x[rows, :], wqkv[:, cols]) + bias[item : item + 1, :]
            if item == 0:
                acc = acc * DH**-0.5
            qkv[rows, cols] = acc.astype(BF16)

    def take(row, other):
        arrived(x.at[pl.ds(row * L + other * part, part)], in_sems.at[row, other], device(other))

    def this_chip(row, carry):
        kept(row).wait()
        take(row, sibling)
        project(row, side)
        return carry

    lax.fori_loop(0, rows_mine, this_chip, 0)
    wout_load.wait()

    def whole_row(row, carry):
        rows = pl.ds(pl.multiple_of(row * L, L), L)
        for item in range(heads - 2):
            take(row, lax.rem(2 * side + 2 + item, heads))
        keep = stores(row)
        keep[0].start()
        project(row, 1 - side)
        keep[1].start()

        def group_heads(group, carry):
            attend(rows, group, 3, qkv, ctx, lse, key_feat, query_feat)
            return carry

        lax.fori_loop(0, 2, group_heads, 0)
        keep[2].start()
        keep[3].start()
        r1[rows, :] = mm(ctx[rows, :], wout[...]) + out_bias + x[rows, :].astype(F32)
        keep[4].start()
        return carry

    lax.fori_loop(0, rows_mine, whole_row, 0)
    for row in range(rows_mine):
        for step in range(heads - 1):
            passed(row, step).wait_send()
        for copy in stores(row):
            copy.wait()


class Place:
    def __init__(self):
        self.row, self.head = lax.axis_index("rows"), lax.axis_index("heads")
        self.z, self.y = self.row // 2, lax.rem(self.row, 2)
        self.x, self.c = self.head // 2, lax.rem(self.head, 2)
        self.half, self.low = self.z // 2, lax.rem(self.z, 2)
        self.next_z = self.at(z=2 * self.half + 1 - self.low)
        self.far_z = self.at(z=2 * (1 - self.half) + self.low)
        self.cross_z = self.at(z=2 * (1 - self.half) + 1 - self.low)
        self.over = {
            "c": self.at(c=1 - self.c), "y": self.at(y=1 - self.y), "x": self.at(x=1 - self.x),
        }

    def at(self, **new):
        z, y, x, c = (new.get(name, getattr(self, name)) for name in "zyxc")
        return {"rows": z * 2 + y, "heads": x * 2 + c}

    def turn(self, step):
        first, second = lax.rem(step, 2), step // 2
        half = self.half + (1 - first) * (1 - 2 * self.half)
        low = self.low + (1 - second) * (1 - 2 * self.low)
        return 2 * half + low

    def side(self, name):
        return self.y if name == "y" else self.x


class Total:
    def __init__(self, where, order, got, mid, far, near, sems, apart=False):
        self.where, self.order, self.direct = where, order.lower(), "Z" in order
        self.got, self.mid, self.far, self.near = got, mid, far, near
        self.core_out, self.core_in, self.out, self.inn, self.z_in = sems
        self.apart = apart

    @staticmethod
    def scratch(order, rows, cols, pieces, groups=()):
        shapes = [(2, 4, 2, rows, cols), (2, 4, rows, cols), (4, rows, cols), (4, rows, cols)]
        stages = 2
        if order[0] == "y":
            shapes[2:] = [(4, 2, rows, cols), (rows, cols)]
            stages = 1
        sems = [(pieces,) if pieces > 2 else (1,), (pieces,), (stages + 2,), (stages, 4), (4,)]
        spaces = [pltpu.VMEM(groups + dims, BF16) for dims in shapes]
        return spaces + [pltpu.SemaphoreType.DMA(groups + dims) for dims in sems]

    def core_copy(self, index, parts):
        source, target = parts(index)
        out = self.core_out.at[index if self.apart else 0]
        return remote(source, target, out, self.core_in.at[index], self.where.over["c"])

    def core_sent(self):
        remote(self.got, self.got, self.core_out.at[0], self.core_in.at[0], self.where.over["c"]).wait_send()

    def core_wait(self, index, target):
        arrived(target, self.core_in.at[index], self.where.over["c"])

    def part(self, ref, z, side):
        return ref.at[side, z] if self.order[0] == "x" else ref.at[:, z, side]

    def first_copy(self, step):
        w = self.where
        z = w.turn(step)
        source = self.part(self.got, z, 1 - w.side(self.order[0]))
        return remote(source, self.mid.at[:, z], self.out.at[0], self.inn.at[0, step], w.over[self.order[0]])

    def first(self, step):
        self.first_copy(step).start()

    def second_copy(self, step):
        w = self.where
        z = w.turn(step)
        source = self.mid.at[1 - w.side(self.order[1]), z]
        return remote(source, self.far.at[z], self.out.at[2], self.inn.at[1, step], w.over[self.order[1]])

    def second(self, step):
        w = self.where
        z = w.turn(step)
        arrived(self.mid.at[:, z], self.inn.at[0, step], w.over[self.order[0]])
        own = self.part(self.got, z, w.side(self.order[0]))
        self.mid[:, z] = (self.mid[:, z].astype(F32) + own[...].astype(F32)).astype(BF16)
        if self.order == "yzx":
            self.z_send(step)
        else:
            self.second_copy(step).start()

    def third(self, step):
        if self.order == "yzx":
            return
        w = self.where
        z = w.turn(step)
        arrived(self.far.at[z], self.inn.at[1, step], w.over[self.order[1]])
        own = self.mid[w.side(self.order[1]), z]
        self.far[z] = (self.far[z].astype(F32) + own.astype(F32)).astype(BF16)
        self.z_send(step)

    def z_slots(self):
        return self.far if self.order == "yzx" else self.near

    def z_block(self, step):
        z = self.where.turn(step)
        return self.mid.at[:, z] if self.order == "yzx" else self.far.at[z]

    def z_device(self, step):
        w = self.where
        return w.next_z if step == 1 else w.far_z if step == 2 else w.cross_z if self.direct else w.next_z

    def z_copy(self, step):
        return remote(
            self.z_block(step), self.z_slots().at[step], self.out.at[1], self.z_in.at[step], self.z_device(step)
        )

    def z_take(self, step):
        arrived(self.z_slots().at[step], self.z_in.at[step], self.z_device(step))
        return self.z_slots()[step].astype(F32)

    def z_send(self, step):
        if step < (3 if self.direct else 2):
            self.z_copy(step).start()

    def relay(self):
        if self.direct:
            return
        block = self.z_block(2)
        block[...] = (block[...].astype(F32) + self.z_take(0)).astype(BF16)
        self.z_copy(2).start()

    def z_sum(self):
        total = self.z_block(3)[...].astype(F32) + self.z_take(1) + self.z_take(2)
        return total + self.z_take(0) if self.direct else total

    def x_copy(self):
        w = self.where
        return remote(self.far.at[3, 1 - w.x], self.near, self.out.at[2], self.z_in.at[3], w.over["x"])

    def fourth(self):
        if self.order != "yzx":
            return
        self.far[3] = self.z_sum().astype(BF16)
        self.x_copy().start()

    def result(self):
        w = self.where
        if self.order != "yzx":
            return self.z_sum()
        arrived(self.near, self.z_in.at[3], w.over["x"])
        return self.far[3, w.x].astype(F32) + self.near[...].astype(F32)

    def sent(self):
        w = self.where
        remote(self.mid, self.mid, self.out.at[0], self.inn.at[0, 0], w.over["y"]).wait_send()
        blocks = self.z_slots().at[pl.ds(0, 3)]
        remote(blocks, blocks, self.out.at[1], self.z_in.at[0], w.next_z).wait_send()
        if self.order == "yzx":
            self.x_copy().wait_send()
        else:
            remote(self.far, self.far, self.out.at[2], self.inn.at[1, 0], w.over["y"]).wait_send()


class Everyone:
    def __init__(self, where, by_head, by_row, sems):
        self.where, self.by_head, self.by_row, self.sems = where, by_head, by_row, sems
        self.own = by_head.at[where.head]

    @staticmethod
    def scratch(rows):
        return [pltpu.VMEM((4, rows, D), F32), pltpu.VMEM((8, rows, D), F32), pltpu.SemaphoreType.DMA((14,))]

    def head_copy(self, step):
        w = self.where
        return remote(
            self.own, self.own, self.sems.at[0], self.sems.at[2 + w.head],
            {"rows": w.row, "heads": lax.rem(w.head + step, 4)},
        )

    def row_copy(self, step):
        w = self.where
        mine = self.by_row.at[w.row]
        return remote(
            mine, mine, self.sems.at[1], self.sems.at[6 + w.row],
            {"rows": lax.rem(w.row + step, 8), "heads": w.head},
        )

    def start(self):
        for step in range(1, 4):
            self.head_copy(step).start()

    def middle(self):
        w = self.where
        for step in range(1, 4):
            head = lax.rem(w.head + step, 4)
            arrived(self.by_head.at[head], self.sems.at[2 + head], {"rows": w.row, "heads": head})
        self.by_row[w.row] = (self.by_head[0] + self.by_head[1]) + (self.by_head[2] + self.by_head[3])
        for step in range(1, 8):
            self.row_copy(step).start()

    def result(self):
        w = self.where
        for step in range(1, 8):
            row = lax.rem(w.row + step, 8)
            arrived(self.by_row.at[row], self.sems.at[6 + row], {"rows": row, "heads": w.head})
        total = self.by_row[0]
        for row in range(1, 8):
            total = total + self.by_row[row]
        return total

    def sent(self):
        w = self.where
        for ref, count, sem in ((self.by_head, 3, 0), (self.by_row, 7, 1)):
            part = ref.at[pl.ds(0, count)]
            remote(part, part, self.sems.at[sem], self.sems.at[2], w.over["y"]).wait_send()


def rest_kernel(
    scale,
    r1_in, cotan, ctx_in, qkv_in, lse_in, x_in, lens, wup_in, wdown_in, wout_in, wqkv_in,
    g1v, s1v, g2v, s2v, bdv, bup,
    lay, xgr, down_to, up_to, out_to, qkv_to, vec_to,
    downo, upo, outo, qkvo, vec_out, mat_sem, r1, ycot, fb, act, slope, acc, dfb, dfbt, wup, wdown, down_send,
    load_sem, cot_sem, lay_sem, xg_sem, own_sem,
    *scratch,
):
    where = w = Place()
    scratch = list(scratch)

    def take(count):
        return [scratch.pop(0) for _ in range(count)]

    totals = []
    for order, *_ in BLOCKS:
        refs = take(9)
        totals.append(Total(where, order, *refs[:4], refs[4:], apart=not totals))
    down, upa, upb, out = totals
    joint = [(order, take(9)) for order, *_ in JOINT]

    def qkv_pair(group):
        made = []
        for order, refs in joint:
            refs = [ref.at[group] for ref in refs]
            made.append(Total(where, order, *refs[:4], refs[4:]))
        return made

    qkvs = (qkv_pair(0), qkv_pair(1))
    everyone = Everyone(where, *take(3))
    late = Everyone(where, *take(3))

    tokens = r1.shape[0]
    step_rows = 256
    parts = tokens // step_rows
    width = 768
    chunks = wup_in.shape[1] // width
    rows_mine = tokens // L
    part = lay.shape[1]
    r1_rows = [pl.ds(index * step_rows, step_rows) for index in range(parts)]
    r1_loads = [load(r1_in.at[rows], r1.at[rows], load_sem.at[9 + index]) for index, rows in enumerate(r1_rows)]
    wup_load = load(wup_in, wup, load_sem.at[1])
    wdown_load = load(wdown_in, wdown, load_sem.at[2])
    others = [lax.rem(w.head + step, 4) for step in range(1, 4)]
    partner = lambda other: {"rows": w.row, "heads": other}
    g1, s1, g2, s2, bd = (wide(item) for item in (g1v, s1v, g2v, s2v, bdv))
    mine = everyone.own
    mine[...] = jnp.zeros(mine.shape, F32)
    last = late.own
    last[...] = jnp.zeros(last.shape, F32)

    def lead(i, carry):
        rows = pl.ds(pl.multiple_of(i * step_rows, step_rows), step_rows)
        pltpu.make_async_copy(r1_in.at[rows], r1.at[rows], load_sem.at[9 + i]).wait()
        normed, _ = norm_parts(r1[rows, :])
        first = normed * g1 + s1
        fb[rows, :] = first.astype(BF16)
        acc[rows, :] = first + bd
        return carry

    lax.fori_loop(0, parts, lead, 0)
    meet([partner(other) for other in others] + [{"rows": lax.rem(w.row + step, 8), "heads": w.head} for step in range(1, 8)])

    def mine_in(row):
        place = pl.ds(row * L + w.head * part, part)
        return pltpu.make_async_copy(cotan.at[w.head * rows_mine + row], ycot.at[place], own_sem.at[2, row])

    def cot_copy(row, step):
        place = pl.ds(row * L + w.head * part, part)
        other = others[step]
        return remote(
            cotan.at[other * rows_mine + row], ycot.at[place], cot_sem.at[0], cot_sem.at[1 + row],
            partner(other),
        )

    def give_back(source, target, sems, row, step):
        other = others[step]
        return remote(
            source.at[pl.ds(row * L + other * part, part)], target.at[w.head * rows_mine + row],
            sems.at[0], sems.at[1 + row], partner(other),
        )

    def mine_out(source, target, index, row):
        place = pl.ds(row * L + w.head * part, part)
        return pltpu.make_async_copy(source.at[place], target.at[w.head * rows_mine + row], own_sem.at[index, row])

    for row in range(rows_mine):
        for step in range(3):
            cot_copy(row, step).start()
        mine_in(row).start()

    wup_load.wait()
    wdown_load.wait()

    def forward(c, carry):
        cols = pl.ds(pl.multiple_of(c * width, width), width)
        u, e = [None] * parts, [None] * parts
        for s in range(parts + 2):
            if s < parts:
                u[s] = mm(fb[s * step_rows : (s + 1) * step_rows, :], wup[:, cols]) + wide(bup.at[cols])
            if 0 <= s - 1 < parts:
                j = s - 1
                rows = slice(j * step_rows, (j + 1) * step_rows)
                cdf, pdf = normal_parts(u[j])
                e[j] = (u[j] * cdf).astype(BF16)
                act[rows, cols] = e[j]
                slope[rows, cols] = (cdf + u[j] * pdf).astype(BF16)
            if 0 <= s - 2 < parts:
                j = s - 2
                acc[j * step_rows : (j + 1) * step_rows, :] += mm(e[j], wdown[cols, :])
        return carry

    lax.fori_loop(0, chunks, forward, 0)
    for row in range(rows_mine):
        mine_in(row).wait()
        arrived(ycot.at[pl.ds(row * L, 3 * part)], cot_sem.at[1 + row], partner(others[0]))

    def second(i, carry):
        rows = pl.ds(pl.multiple_of(i * step_rows, step_rows), step_rows)
        normed, spread = norm_parts(acc[rows, :])
        dy = ycot[rows, :].astype(F32)
        ycot[rows, :] = (normed * g2 + s2).astype(BF16)
        dr2 = norm_back(dy, normed, spread, g2)
        acc[rows, :] = dr2
        low = dr2.astype(BF16)
        dfb[rows, :] = low
        dfbt[:, :, rows] = low.T.reshape(4, D // 4, step_rows)
        mine[0:1, :] += jnp.sum(dy * normed, axis=0, keepdims=True)
        mine[1:2, :] += jnp.sum(dy, axis=0, keepdims=True)
        mine[2:3, :] += jnp.sum(low.astype(F32), axis=0, keepdims=True)
        return carry

    lax.fori_loop(0, parts, second, 0)

    for row in range(rows_mine):
        for step in range(3):
            give_back(ycot, lay, lay_sem, row, step).start()
        mine_out(ycot, lay, 0, row).start()

    def down_half(core, z):
        left = jnp.concatenate([dfbt[core], dfbt[2 + core]], axis=0)
        cols = pl.ds(pl.multiple_of(z * width, width), width)
        return mm(left, act[:, cols])

    quarter, eighth = D // 4, width // 2

    def down_parts(step):
        z = where.turn(step)
        return down_send.at[lax.rem(step, 2)], down.got.at[:, z]

    def down_other(step, carry):
        z = where.turn(step)
        total = down_half(1 - w.c, z)

        @pl.when(step >= 2)
        def _():
            down.core_copy(step - 2, down_parts).wait_send()

        slot = lax.rem(step, 2)
        for x in range(2):
            for y in range(2):
                piece = total[x * quarter : (x + 1) * quarter, y * eighth : (y + 1) * eighth]
                down_send[slot, x, y] = piece.astype(BF16)
        down.core_copy(step, down_parts).start()
        return carry

    def down_own(step, carry):
        z = where.turn(step)
        total = down_half(w.c, z)
        down.core_wait(step, down.got.at[:, z])
        for x in range(2):
            for y in range(2):
                piece = total[x * quarter : (x + 1) * quarter, y * eighth : (y + 1) * eighth]
                down.got[x, z, y] = (piece + down.got[x, z, y].astype(F32)).astype(BF16)
        down.first(step)
        return carry

    lax.fori_loop(0, 4, down_other, 0)
    lax.fori_loop(0, 4, down_own, 0)
    qkv_load = load(qkv_in, act.at[:, pl.ds(0, 3 * D)], load_sem.at[4])

    def backward(c, carry):
        cols = pl.ds(pl.multiple_of(c * width, width), width)
        de, du = [None] * parts, [None] * parts
        sums = jnp.zeros((1, width), F32)
        for s in range(parts + 2):
            if s < parts:
                de[s] = mm(dfb[s * step_rows : (s + 1) * step_rows, :], wdown[cols, :], NT)
            if 0 <= s - 1 < parts:
                j = s - 1
                rows = slice(j * step_rows, (j + 1) * step_rows)
                du[j] = (de[j] * slope[rows, cols].astype(F32)).astype(BF16)
                slope[rows, cols] = du[j]
                sums = sums + jnp.sum(du[j].astype(F32), axis=0, keepdims=True)
            if 0 <= s - 2 < parts:
                j = s - 2
                acc[j * step_rows : (j + 1) * step_rows, :] += mm(du[j], wup[:, cols], NT)
        mine[pl.ds(3 + c, 1), :] = sums
        return carry

    half = chunks // 2
    lax.fori_loop(0, half, backward, 0)
    down.second(0)
    lax.fori_loop(half, chunks, backward, 0)
    down.second(1)
    down.third(0)
    wqkv = wup.at[:, pl.ds(0, 3 * D)]
    x = wdown.at[pl.ds(2 * D, tokens)]
    wout = wup.at[:, pl.ds(3 * D, D)]
    wqkv_load = load(wqkv_in, wqkv, load_sem.at[5])
    wout_load = load(wout_in, wout, load_sem.at[3])
    x_load = load(x_in, x, load_sem.at[6])
    dab = dfb
    feats = wdown.at[pl.ds(2 * D + tokens, L)]
    for row in range(rows_mine):
        key_feat, query_feat = (feats.at[:, pl.ds((2 * row + item) * 128, 128)] for item in range(2))
        features(example_ends(lens, w.head * rows_mine + row), key_feat, query_feat, 0)

    def third(i, carry):
        rows = pl.ds(pl.multiple_of(i * step_rows, step_rows), step_rows)
        normed, spread = norm_parts(r1[rows, :])
        grad = acc[rows, :]
        dr = norm_back(grad, normed, spread, g1)
        acc[rows, :] = dr
        low = dr.astype(BF16)
        dab[rows, :] = low
        mine[7:8, :] += jnp.sum(grad * normed, axis=0, keepdims=True)
        last[2:3, :] += jnp.sum(grad, axis=0, keepdims=True)
        last[3:4, :] += jnp.sum(low.astype(F32), axis=0, keepdims=True)
        return carry

    lax.fori_loop(0, parts, third, 0)
    lse_load = [load(lse_in.at[g], r1.at[:, pl.ds(g * 128, 128)], load_sem.at[7 + g]) for g in range(2)]

    def up_half(core, x_side):
        cols = pl.ds(pl.multiple_of((2 * x_side + core) * width, width), width)
        return mm(fb[...], slope[:, cols], TN)

    ups = (upa, upb)

    def spot(side, index, cols, start):
        row = pl.multiple_of(side * D + index * (D // 2), D // 2)
        return wdown.at[pl.ds(row, D // 2), pl.ds(start, cols)]

    def pair_parts(each, index, cols, start):
        return lambda side: (spot(side, index, cols, start), each.got.at[side].reshape(D // 2, cols))

    def pair_other(pair, side, total, cols, start):
        total = total.astype(BF16).reshape(4, 2, 2, D // 16, cols)
        for index, each in enumerate(pair):
            spot(side, index, cols, start)[...] = total[:, :, index].reshape(D // 2, cols)
            each.core_copy(side, pair_parts(each, index, cols, start)).start()

    def pair_own(pair, side, turn, total, cols):
        total = total.reshape(4, 2, 2, D // 16, cols)
        for index, each in enumerate(pair):
            each.core_wait(side, each.got.at[side])
            each.got[side] = (total[:, :, index] + each.got[side].astype(F32)).astype(BF16)
        for when, each in enumerate((pair[1], pair[0])):

            @pl.when(turn == when)
            def _():
                for step in range(4):
                    each.first(step)

    def pair_sent(pair):
        for each in pair:
            each.core_sent()

    def far_first(turn):
        return lax.rem(w.x + 1 + turn, 2)

    def up_other(turn, carry):
        side = far_first(turn)
        pair_other(ups, side, up_half(1 - w.c, side), width, 0)
        return carry

    lax.fori_loop(0, 2, up_other, 0)
    down.second(2)
    down.relay()
    down.third(1)

    def up_own(turn, carry):
        side = far_first(turn)
        pair_own(ups, side, turn, up_half(w.c, side), width)
        return carry

    lax.fori_loop(0, 2, up_own, 0)
    down.second(3)
    down.third(2)
    ctx = slope.at[:, pl.ds(3 * D, D)]
    grads = slope.at[:, pl.ds(0, 3 * D)]
    dctx = act.at[:, pl.ds(3 * D, D)]
    ctx_load = load(ctx_in, ctx, load_sem.at[0])
    wout_load.wait()

    def context_grad(row, carry):
        rows = pl.ds(pl.multiple_of(row * L, L), L)
        dctx[rows, :] = mm(dab[rows, :], wout[...], NT).astype(BF16)
        return carry

    lax.fori_loop(0, rows_mine, context_grad, 0)
    ctx_load.wait()
    wqkv_load.wait()

    def out_half(core, side):
        cols = pl.ds(pl.multiple_of(384 * side + 128 * core, 128), 256)
        return mm(ctx[...], dab[:, cols], TN)

    def out_parts(side):
        spot = wup.at[:, pl.ds(pl.multiple_of(3 * D + 256 * side, 256), 256)]
        return spot, out.got.at[side].reshape(D, 256)

    def out_other(side, carry):
        out_parts(side)[0][...] = out_half(1 - w.c, side).astype(BF16)
        out.core_copy(side, out_parts).start()
        return carry

    def out_own(side, carry):
        total = out_half(w.c, side).reshape(4, 2, D // 8, 256)
        out.core_wait(side, out.got.at[side])
        out.got[side] = (total + out.got[side].astype(F32)).astype(BF16)
        return carry

    lax.fori_loop(0, 2, out_other, 0)
    lax.fori_loop(0, 2, out_own, 0)
    for step in range(4):
        out.first(step)
    upa.second(0)
    everyone.start()

    qkv = act.at[:, pl.ds(0, 3 * D)]
    qkv_load.wait()
    for copy in lse_load:
        copy.wait()
    x_load.wait()

    def input_grad(row):
        rows = pl.ds(pl.multiple_of(row * L, L), L)
        fb[rows, :] = (mm(grads[rows, :], wqkv[...], NT) + acc[rows, :]).astype(BF16)
        for step in range(3):
            give_back(fb, xgr, xg_sem, row, step).start()
        mine_out(fb, xgr, 1, row).start()

    def qkv_half(core, side, group):
        early = side * 1536 + (1 - side) * core * D
        later = side * (1152 + core * D) + (1 - side) * 384
        start = pl.multiple_of((1 - group) * early + group * later, 128)
        return mm(x[...], grads[:, pl.ds(start, 384)], TN)

    def qkv_sums(group):
        pair = qkv_pair(group)
        start = pl.multiple_of(group * 384, 128)

        def other(turn, carry):
            side = far_first(turn)
            pair_other(pair, side, qkv_half(1 - w.c, side, group), 384, start)
            return carry

        def own(turn, carry):
            side = far_first(turn)
            pair_own(pair, side, turn, qkv_half(w.c, side, group), 384)
            return carry

        lax.fori_loop(0, 2, other, 0)
        lax.fori_loop(0, 2, own, 0)

    def heads_back(i, carry):
        group, row = i // 2, lax.rem(i, 2)
        rows = pl.ds(pl.multiple_of(row * L, L), L)
        keep = r1[rows, pl.ds(pl.multiple_of(group * 128, 128), 128)]
        lanes = [pl.ds(pl.multiple_of(2 * row * 128 + 128 * item, 128), 128) for item in range(2)]
        attend_back(rows, group, 3, qkv, ctx, dctx, keep, grads, feats[:, lanes[0]], feats[:, lanes[1]])

        @pl.when(i == 0)
        def _():
            upa.second(1)
            upb.second(0)
            upb.second(1)
            pair_sent(ups)

        @pl.when(i == 1)
        def _():
            upa.second(2)
            upa.second(3)
            upa.relay()
            upb.second(2)
            down.fourth()

        @pl.when(i == 2)
        def _():
            upb.second(3)
            upb.third(0)
            for step in range(4):
                out.second(step)
            everyone.middle()

        @pl.when(i == 3)
        def _():
            last[0:1, :] = jnp.sum(grads[:, 0:D].astype(F32), axis=0, keepdims=True)
            last[1:2, :] = jnp.sum(grads[:, 2 * D : 3 * D].astype(F32), axis=0, keepdims=True)
            late.start()
            out.relay()
            for step in range(1, 4):
                upb.third(step)
            upa.fourth()

        @pl.when(row == 1)
        def _():
            qkv_sums(group)

        @pl.when(i == 3)
        def _():
            for step in range(4):
                qkvs[0][0].second(step)
            upb.relay()
            out.fourth()
            late.middle()

        @pl.when(group == 1)
        def _():
            input_grad(row)

        @pl.when(i == 2)
        def _():
            for step in range(4):
                qkvs[0][1].second(step)

        return carry

    lax.fori_loop(0, 4, heads_back, 0)
    (qkva, qkvb), (ena, enb) = qkvs
    downo[...] = down.result() * scale
    kept = [load(downo, down_to, mat_sem.at[0])]
    eighth_rows = D // 16
    for step in range(4):
        qkvb.third(step)
    enb.second(0)
    enb.second(1)
    ena.second(0)
    ena.second(1)
    enb.second(2)
    enb.second(3)
    qkva.relay()
    qkvb.relay()
    ena.second(2)
    ena.second(3)
    enb.third(0)
    enb.third(1)
    enb.third(2)
    enb.third(3)
    qkva.fourth()
    upo[eighth_rows:, :] = upb.result() * scale
    ena.fourth()
    outo[...] = pick(out.result() * scale, w.c, 192)
    kept.append(load(outo, out_to, mat_sem.at[1]))
    upo[0:eighth_rows, :] = upa.result() * scale
    kept.append(load(upo, up_to, mat_sem.at[2]))
    vectors = everyone.result() * scale
    vec_out[12:16, :] = jnp.zeros((4, D), F32)
    for index, item in ((3, 7), (5, 2), (6, 0), (7, 1), (8, 3), (9, 4), (10, 5), (11, 6)):
        vec_out[index : index + 1, :] = vectors[item : item + 1, :]
    for index in range(2):
        down.core_copy(2 + index, down_parts).wait_send()
    out.core_sent()
    for total in totals[:4]:
        total.sent()
    everyone.sent()

    def all_sent(source, sem):
        part_sent = source.at[pl.ds(0, 3 * rows_mine * part)]
        remote(part_sent, part_sent, sem, sem, partner(others[0])).wait_send()

    all_sent(ycot, cot_sem.at[0])
    all_sent(ycot, lay_sem.at[0])
    for row in range(rows_mine):
        arrived(lay.at[pl.ds(3 * row, 3)], lay_sem.at[1 + row], partner(others[0]))
        mine_out(ycot, lay, 0, row).wait()
    for group in range(2):
        pair_sent(qkvs[group])
    early = jnp.concatenate([qkva.result(), qkvb.result()], axis=0) * scale
    qkva.sent()
    qkvb.sent()
    ends = late.result() * scale
    vec_out[0:2, :] = ends[0:2, :]
    vec_out[2:3, :] = ends[3:4, :]
    vec_out[4:5, :] = ends[2:3, :]
    kept.append(load(vec_out, vec_to, mat_sem.at[3]))
    late.sent()
    late_part = jnp.concatenate([ena.result(), enb.result()], axis=0) * scale
    for corner, (one, two) in enumerate(
        (
            ((0, 384, 0), (384, 192, 0)), ((192, 384, 0), (0, 192, 192)),
            ((384, 192, 0), (0, 384, 0)), ((0, 192, 192), (192, 384, 0)),
        )
    ):

        @pl.when(w.head == corner)
        def _():
            for value, (place, size, start) in ((early, one), (late_part, two)):
                qkvo[:, place : place + size] = value[:, start : start + size]

    kept.append(load(qkvo, qkv_to, mat_sem.at[4]))
    for row in range(rows_mine):
        arrived(xgr.at[pl.ds(3 * row, 3)], xg_sem.at[1 + row], partner(others[0]))
        mine_out(fb, xgr, 1, row).wait()
    all_sent(fb, xg_sem.at[0])
    ena.sent()
    enb.sent()
    for copy in kept:
        copy.wait()


def pick(values, core, width):
    return jnp.where(core == 0, values[:, :width], values[:, 64 : 64 + width])


VMEM = pl.BlockSpec(memory_space=pltpu.VMEM)
SMEM = pl.BlockSpec(memory_space=pltpu.SMEM)


def shape(dims, kind):
    return jax.ShapeDtypeStruct(dims, kind)


def params(**more):
    return pltpu.CompilerParams(vmem_limit_bytes=255 * 2**18, **more)


def local(
    hidden_in, lengths, qkv_weight, query_bias, value_bias, out_weight, out_bias, gain_one,
    shift_one, up_weight, up_bias, down_weight, down_bias, gain_two, shift_two, cotangent,
):
    row_count, part_len = hidden_in.shape[0], hidden_in.shape[1]
    heads = lax.axis_size("heads")
    mine = row_count // heads
    tokens = mine * L
    ff = up_weight.shape[1]
    place = lax.axis_index("heads")
    x = lax.all_to_all(hidden_in, "heads", split_axis=0, concat_axis=1, tiled=True).reshape(tokens, D)
    cot = lax.all_to_all(cotangent, "heads", split_axis=0, concat_axis=1, tiled=True).reshape(tokens, D)
    lens = lax.dynamic_slice_in_dim(lengths, place * mine, mine, 0)
    bqkv = jnp.concatenate([query_bias, jnp.zeros_like(query_bias), value_bias]).astype(F32)[None]
    qkv, ctx, r1, lse = pl.pallas_call(
        first_kernel,
        out_shape=(
            shape((tokens, 3 * D), BF16), shape((tokens, D), BF16), shape((tokens, D), F32),
            shape((2, tokens, 128), F32),
        ),
        in_specs=[VMEM, SMEM] + [VMEM] * 4,
        out_specs=(VMEM,) * 4,
        scratch_shapes=[pltpu.VMEM((tokens, 128), BF16)] * 2,
        compiler_params=params(),
        name="first",
    )(x, lens, qkv_weight, bqkv, out_weight, out_bias.astype(F32)[None])
    vecs = jnp.stack([gain_one, shift_one, gain_two, shift_two, down_bias]).astype(F32)
    y, dr1, dctx, downg, upg, outg, vec_mid, upb = pl.pallas_call(
        middle_kernel,
        out_shape=(
            shape((tokens, D), BF16), shape((tokens, D), F32), shape((tokens, D), BF16),
            shape((D, ff), BF16), shape((D, ff), BF16), shape((D, D), BF16),
            shape((8, D), F32), shape((1, ff), F32),
        ),
        in_specs=[VMEM] * 8,
        out_specs=(VMEM,) * 8,
        scratch_shapes=[
            pltpu.VMEM((tokens, D), BF16), pltpu.VMEM((tokens, ff), BF16), pltpu.VMEM((tokens, ff), BF16),
            pltpu.VMEM((tokens, D), F32), pltpu.VMEM((tokens, D), BF16), pltpu.VMEM((tokens, D), BF16),
        ],
        compiler_params=params(),
        name="middle",
    )(r1, ctx, cot, vecs, up_weight, up_bias.astype(F32)[None], down_weight, out_weight)
    xg, qkvg, vec_last = pl.pallas_call(
        last_kernel,
        out_shape=(shape((tokens, D), BF16), shape((D, 3 * D), BF16), shape((8, D), F32)),
        in_specs=[VMEM, SMEM] + [VMEM] * 6,
        out_specs=(VMEM,) * 3,
        scratch_shapes=[pltpu.VMEM((tokens, 3 * D), BF16)] + [pltpu.VMEM((tokens, 128), BF16)] * 2,
        compiler_params=params(),
        name="last",
    )(x, lens, qkv, ctx, dctx, lse, dr1, qkv_weight)

    def back(values):
        values = values.reshape(mine, L, D)
        return lax.all_to_all(values, "heads", split_axis=1, concat_axis=0, tiled=True)

    layer_out = back(y)
    input_grad = back(xg).astype(F32)
    scale = 1.0 / (row_count * lax.axis_size("rows"))
    vec_mid, vec_last, upb = lax.psum((vec_mid, vec_last, upb), ("rows", "heads"))

    def reduce(values, flip):
        one, two = (0, 1) if flip else (1, 0)
        half = lax.psum_scatter(values, "heads", scatter_dimension=one, tiled=True).astype(F32)
        total = lax.psum_scatter(half, "rows", scatter_dimension=two, tiled=True) * scale
        return total.T if flip else total

    vm, vl = vec_mid * scale, vec_last * scale
    return (
        layer_out, input_grad, reduce(qkvg, False), vl[0], vl[1], reduce(outg, False), vm[5], vm[3], vm[4],
        reduce(upg, False), upb[0] * scale, reduce(downg, True), vm[2], vm[0], vm[1],
    )


ANY = pl.BlockSpec(memory_space=pl.ANY)
DMA = pltpu.SemaphoreType.DMA
BLOCKS = (("yzx", 192, 384, 4), ("yzx", 48, 768, 2), ("xyz", 48, 768, 2), ("yzx", 96, 256, 2))
JOINT = (("yZx", 48, 384, 2), ("xyZ", 48, 384, 2))


def finish_kernel(count, *refs):
    lay, xgr, vec = refs[:3]
    mats = refs[3 : 3 + count]
    lay_out, xg_out = refs[3 + count : 5 + count]
    mats_out = refs[5 + count : 5 + 2 * count]
    vecs_out = refs[5 + 2 * count : 14 + 2 * count]
    through, low, full, sems = refs[14 + 2 * count : 18 + 2 * count]
    mats_here, (vec_here, mat_sems) = refs[18 + 2 * count : 18 + 3 * count], refs[-2:]
    vec_load = load(vec, vec_here, mat_sems.at[0, count])
    blocks = xgr.shape[0]
    wides = [load(xgr.at[i], low.at[i], sems.at[0, i]) for i in range(blocks)]
    lays = [load(lay.at[i], through.at[i], sems.at[1, i]) for i in range(blocks)]
    arrive = [load(mats[i], mats_here[i], mat_sems.at[0, i]) for i in range(count)]
    copies = []
    for i in range(blocks):
        wides[i].wait()
        full[i] = low[i].astype(F32)
        copies.append(load(full.at[i], xg_out.at[i], sems.at[2, i]))
    for i in range(blocks):
        lays[i].wait()
        copies.append(load(through.at[i], lay_out.at[i], sems.at[3, i]))
    for i in range(count):
        arrive[i].wait()
        copies.append(load(mats_here[i], mats_out[i], mat_sems.at[1, i]))
    vec_load.wait()
    for index in range(8):
        vecs_out[index][...] = vec_here[index, :]
    for index in range(4):
        vecs_out[8][index * D : (index + 1) * D] = vec_here[8 + index, :]
    for copy in copies:
        copy.wait()


def local_fast(
    hidden_in, lengths, qkv_weight, query_bias, value_bias, out_weight, out_bias, gain_one,
    shift_one, up_weight, up_bias, down_weight, down_bias, gain_two, shift_two, cotangent,
):
    row_count, part_len = hidden_in.shape[0], hidden_in.shape[1]
    mine = row_count // lax.axis_size("heads")
    heads = lax.axis_size("heads")
    tokens = mine * L
    ff = up_weight.shape[1]
    bf = lambda *dims: pltpu.VMEM(dims, BF16)
    fl = lambda *dims: pltpu.VMEM(dims, F32)
    x, qkv, ctx, r1, lse = pl.pallas_call(
        gather_kernel,
        out_shape=(
            shape((tokens, D), BF16), shape((tokens, 3 * D), BF16),
            shape((tokens, D), BF16), shape((tokens, D), F32), shape((2, tokens, 128), F32),
        ),
        in_specs=[ANY, VMEM, ANY, VMEM, VMEM, ANY, VMEM],
        out_specs=(ANY,) * 5,
        scratch_shapes=[
            bf(tokens, D), bf(tokens, 3 * D), bf(tokens, D), fl(tokens, D), fl(2, tokens, 128), bf(D, 3 * D),
            bf(D, D), fl(8, D), bf(tokens, 128), bf(tokens, 128),
            DMA((2,)), DMA((mine,)), DMA((5, mine)), DMA((mine, heads - 1)), DMA((mine, heads)),
        ],
        compiler_params=params(collective_id=0, has_side_effects=True),
        name="gather",
    )(hidden_in, lengths.T, qkv_weight, query_bias, value_bias, out_weight, out_bias)
    scale = 1.0 / (row_count * lax.axis_size("rows"))
    totals = []
    for block in BLOCKS:
        totals += Total.scratch(*block)
    for block in JOINT:
        totals += Total.scratch(*block, groups=(2,))
    mats = (shape((192, 384), F32), shape((96, 768), F32), shape((96, 192), F32), shape((96, 576), F32))
    wide_out = shape((row_count, part_len, D), BF16)
    lay, xgr, downg, upg, outg, qkvg, vec = pl.pallas_call(
        functools.partial(rest_kernel, scale),
        out_shape=(wide_out, wide_out) + mats + (shape((16, D), F32),),
        in_specs=[ANY] * 6 + [VMEM] + [ANY] * 4 + [VMEM] * 6,
        out_specs=(ANY,) * 7,
        scratch_shapes=[fl(*item.shape) for item in mats] + [
            fl(16, D), DMA((5,)),
            fl(tokens, D), bf(tokens, D), bf(tokens, D), bf(tokens, ff), bf(tokens, ff),
            fl(tokens, D), bf(tokens, D), bf(4, D // 4, tokens), bf(D, ff), bf(ff, D),
            bf(2, 2, 2, 192, 384), DMA((13,)), DMA((1 + mine,)), DMA((1 + mine,)), DMA((1 + mine,)), DMA((3, mine)),
        ]
        + totals
        + Everyone.scratch(8)
        + Everyone.scratch(8),
        compiler_params=params(collective_id=1, has_side_effects=True),
        name="rest",
    )(
        r1, cotangent, ctx, qkv, lse, x, lengths.T, up_weight, down_weight, out_weight, qkv_weight,
        gain_one, shift_one, gain_two, shift_two, down_bias, up_bias,
    )
    results = pl.pallas_call(
        functools.partial(finish_kernel, 4),
        out_shape=(wide_out, shape((row_count, part_len, D), F32)) + mats + (shape((D,), F32),) * 8 + (shape((ff,), F32),),
        in_specs=[ANY] * 7,
        out_specs=(ANY,) * 6 + (VMEM,) * 9,
        scratch_shapes=[
            bf(row_count, part_len, D), bf(row_count, part_len, D), fl(row_count, part_len, D), DMA((4, row_count)),
        ]
        + [fl(*item.shape) for item in mats]
        + [fl(16, D), DMA((2, 5))],
        compiler_params=params(),
        name="finish",
    )(lay, xgr, vec, downg, upg, outg, qkvg)
    layer_out, input_grad, downg, upg, outg, qkvg, qb, vb, ob, go, so, db, gt, st, ub = results
    return layer_out, input_grad, qkvg, qb, vb, outg, ob, go, so, upg, ub, downg.T, db, gt, st


def solution(mesh):
    split = P("rows", "heads", None)
    grid = P("rows", "heads")
    in_specs = (split, P("rows", None)) + (P(),) * 13 + (split,)
    out_specs = (split, split, grid, P(), P(), grid, P(), P(), P(), grid, P(), grid, P(), P(), P())
    fast = mesh.shape["rows"] == 8 and mesh.shape["heads"] == 4
    return jax.shard_map(
        local_fast if fast else local, mesh=mesh, in_specs=in_specs, out_specs=out_specs, check_vma=False
    )
```

```python
import functools

import jax
import jax.numpy as jnp
from jax import lax
from jax.experimental import pallas as pl
from jax.experimental.pallas import tpu as pltpu
from jax.sharding import PartitionSpec as P

DH = 64
D = 768
L = 512
EPSILON = 1e-12
OFF = -(2.0**100)
F32 = jnp.float32
BF16 = jnp.bfloat16
NN = (((1,), (0,)), ((), ()))
NT = (((1,), (1,)), ((), ()))
TN = (((0,), (0,)), ((), ()))

RATE = 0.285
TAIL = (
    0.11576503423350087,
    0.08983941546025678,
    0.2103671707394457,
    -0.14882089196252246,
    0.3285619517018635,
    -0.09571266010718714,
)


def mm(left, right, dims=NN):
    return lax.dot_general(left, right, dims, preferred_element_type=F32)


def normal_parts(u):
    bell = jnp.exp2(u * u * -0.7213475204444817)
    t = pltpu.reciprocal(1.0 + RATE * jnp.abs(u))
    poly = TAIL[-1]
    for item in TAIL[-2::-1]:
        poly = poly * t + item
    tail = poly * t * bell
    return jnp.where(u >= 0, 1.0 - tail, tail), bell * 0.3989422804014327


def norm_parts(values):
    middle = jnp.mean(values, axis=-1, keepdims=True)
    center = values - middle
    spread = jnp.mean(center * center, axis=-1, keepdims=True)
    scale = lax.rsqrt(spread + EPSILON)
    return center * scale, scale


def norm_back(grad, normed, scale, gain):
    dn = grad * gain
    first = jnp.mean(dn, axis=-1, keepdims=True)
    second = jnp.mean(dn * normed, axis=-1, keepdims=True)
    return (dn - first - normed * second) * scale


def split3(values):
    high = values.astype(BF16)
    rest = values - high.astype(F32)
    mid = rest.astype(BF16)
    return high, mid, (rest - mid.astype(F32)).astype(BF16)


def features(ends, key_feat, query_feat, start):
    token = lax.broadcasted_iota(jnp.int32, (L, 128), 0)
    place = lax.broadcasted_iota(jnp.int32, (L, 128), 1) & (DH - 1)
    seg = jnp.zeros((L, 128), jnp.int32)
    for end in ends:
        seg = seg + (token >= end).astype(jnp.int32)
    count = len(ends)
    ones = (place == seg) | ((place >= count) & (place < count + 3))
    key_feat[pl.ds(start, L), :] = jnp.where(ones, 1.0, 0.0).astype(BF16)
    off = (place < count) & (place != seg)
    query_feat[pl.ds(start, L), :] = jnp.where(off, OFF, 0.0).astype(BF16)


def attend(rows, group, pairs, qkv, ctx, lse, key_feat, query_feat):
    lane = lax.broadcasted_iota(jnp.int32, (1, 128), 1)
    kf, qf = key_feat[rows, :], query_feat[rows, :]
    ops, values = [], []
    for pair in range(pairs):
        col = pl.multiple_of(group * (pairs * 128) + pair * 128, 128)
        q2 = qkv[rows, pl.ds(col, 128)]
        k2 = qkv[rows, pl.ds(D + col, 128)]
        values.append(qkv[rows, pl.ds(2 * D + col, 128)])
        for own in (lane < DH, lane >= DH):
            ops.append((jnp.where(own, q2, qf), jnp.where(own, k2, kf)))
    count = 2 * pairs
    scores = [None] * count
    outs, sums = [], []
    scores[0] = mm(*ops[0], NT)
    for head in range(count):
        if head + 1 < count:
            scores[head + 1] = mm(*ops[head + 1], NT)
        peak = jnp.max(scores[head], axis=1, keepdims=True)
        expo = jnp.exp(scores[head] - peak)
        total = jnp.sum(expo, axis=1, keepdims=True)
        out = mm(expo.astype(BF16), values[head // 2])
        outs.append(out * (1.0 / total))
        sums.append(peak + jnp.log(total))
    keep = jnp.zeros((L, 128), F32)
    for head in range(count):
        keep = jnp.where(lane == head, sums[head], keep)
    lse[group, rows, :] = keep
    for pair in range(pairs):
        col = pl.multiple_of(group * (pairs * 128) + pair * 128, 128)
        both = jnp.where(lane < DH, outs[2 * pair], outs[2 * pair + 1])
        ctx[rows, pl.ds(col, 128)] = both.astype(BF16)


def attend_back(rows, group, pairs, qkv, ctx, dctx, keep, grads, kf, qf):
    lane = lax.broadcasted_iota(jnp.int32, (1, 128), 1)
    place = lane & (DH - 1)
    vf = jnp.where((place >= 4) & (place < 7), 1.0, 0.0).astype(BF16)

    def spread(column, base):
        high, mid, small = split3(-column)
        return jnp.where(
            place == 4, high, jnp.where(place == 5, mid, jnp.where(place == 6, small, base))
        )

    ops = []
    for pair in range(pairs):
        col = pl.multiple_of(group * (pairs * 128) + pair * 128, 128)
        q2 = qkv[rows, pl.ds(col, 128)]
        k2 = qkv[rows, pl.ds(D + col, 128)]
        v2 = qkv[rows, pl.ds(2 * D + col, 128)]
        d2 = dctx[rows, pl.ds(col, 128)]
        both = d2.astype(F32) * ctx[rows, pl.ds(col, 128)].astype(F32)
        zero = jnp.zeros_like(q2)
        for side, own in enumerate((lane < DH, lane >= DH)):
            inner = jnp.sum(jnp.where(own, both, 0.0), axis=1, keepdims=True)
            total = keep[:, 2 * pair + side : 2 * pair + side + 1]
            ops.append(
                (
                    jnp.where(own, k2, kf),
                    jnp.where(own, q2, spread(total, qf)),
                    jnp.where(own, v2, vf),
                    jnp.where(own, d2, spread(inner, zero)),
                    jnp.where(own, q2, zero),
                    jnp.where(own, k2, zero),
                    jnp.where(own, d2, zero),
                )
            )
    count = 2 * pairs
    scores, chances = [None] * count, [None] * count
    dq, dk, dv = [0] * pairs, [0] * pairs, [0] * pairs

    def start(head):
        scores[head] = mm(ops[head][0], ops[head][1], NT)
        chances[head] = mm(ops[head][2], ops[head][3], NT)

    start(0)
    for head in range(count):
        if head + 1 < count:
            start(head + 1)
        chance = jnp.exp(scores[head])
        low = chance.astype(BF16)
        ds = (chance * chances[head]).astype(BF16)
        pair = head // 2
        dk[pair] += mm(ds, ops[head][4])
        dv[pair] += mm(low, ops[head][6])
        dq[pair] += mm(ds, ops[head][5], TN)
    for pair in range(pairs):
        col = pl.multiple_of(group * (pairs * 128) + pair * 128, 128)
        grads[rows, pl.ds(col, 128)] = (dq[pair] * DH**-0.5).astype(BF16)
        grads[rows, pl.ds(D + col, 128)] = dk[pair].astype(BF16)
        grads[rows, pl.ds(2 * D + col, 128)] = dv[pair].astype(BF16)


def first_kernel(x, lens, wqkv, bqkv, wout, bout, qkv, ctx, r1, lse, key_feat, query_feat):
    for row in range(x.shape[0] // L):
        ends, total = [], 0
        for item in range(lens.shape[1]):
            total = total + lens[row, item]
            ends.append(total)
        features(ends, key_feat, query_feat, row * L)

        rows = pl.ds(row * L, L)
        for part in range(3):
            cols = pl.ds(part * D, D)
            acc = mm(x[rows, :], wqkv[:, cols]) + bqkv[:, cols]
            if part == 0:
                acc = acc * DH**-0.5
            qkv[rows, cols] = acc.astype(BF16)

        def heads(group, carry):
            attend(rows, group, 3, qkv, ctx, lse, key_feat, query_feat)
            return carry

        lax.fori_loop(0, 2, heads, 0)
        r1[rows, :] = mm(ctx[rows, :], wout[...]) + bout[...] + x[rows, :].astype(F32)


def middle_kernel(
    r1, ctx, cot, vecs, wup, bup, wdown, wout,
    y, dr1, dctx, downg, upg, outg, vec_grads, upb_grad,
    fb, act, slope, acc, dfb, dab,
):
    tokens = r1.shape[0]
    step = 256
    parts = tokens // step
    width = 768
    chunks = wup.shape[1] // width
    g1, s1, g2, s2, bd = (vecs[i : i + 1, :] for i in range(5))
    vec_grads[...] = jnp.zeros_like(vec_grads)
    upb_grad[...] = jnp.zeros_like(upb_grad)

    def lead(i, carry):
        rows = pl.ds(pl.multiple_of(i * step, step), step)
        normed, _ = norm_parts(r1[rows, :])
        first = normed * g1 + s1
        fb[rows, :] = first.astype(BF16)
        acc[rows, :] = first + bd
        return carry

    lax.fori_loop(0, parts, lead, 0)

    def forward(c, carry):
        cols = pl.ds(pl.multiple_of(c * width, width), width)
        u, e = [None] * parts, [None] * parts
        for s in range(parts + 2):
            if s < parts:
                u[s] = mm(fb[s * step : (s + 1) * step, :], wup[:, cols]) + bup[:, cols]
            if 0 <= s - 1 < parts:
                j = s - 1
                rows = slice(j * step, (j + 1) * step)
                cdf, pdf = normal_parts(u[j])
                e[j] = (u[j] * cdf).astype(BF16)
                act[rows, cols] = e[j]
                slope[rows, cols] = (cdf + u[j] * pdf).astype(BF16)
            if 0 <= s - 2 < parts:
                j = s - 2
                acc[j * step : (j + 1) * step, :] += mm(e[j], wdown[cols, :])
        return carry

    lax.fori_loop(0, chunks, forward, 0)

    def second(i, carry):
        rows = pl.ds(pl.multiple_of(i * step, step), step)
        normed, scale = norm_parts(acc[rows, :])
        y[rows, :] = (normed * g2 + s2).astype(BF16)
        dy = cot[rows, :].astype(F32)
        dr2 = norm_back(dy, normed, scale, g2)
        acc[rows, :] = dr2
        low = dr2.astype(BF16)
        dfb[rows, :] = low
        vec_grads[0:1, :] += jnp.sum(dy * normed, axis=0, keepdims=True)
        vec_grads[1:2, :] += jnp.sum(dy, axis=0, keepdims=True)
        vec_grads[2:3, :] += jnp.sum(low.astype(F32), axis=0, keepdims=True)
        return carry

    lax.fori_loop(0, parts, second, 0)

    def down(c, carry):
        cols = pl.ds(pl.multiple_of(c * width, width), width)
        downg[:, cols] = mm(dfb[...], act[:, cols], TN).astype(BF16)
        return carry

    lax.fori_loop(0, chunks, down, 0)

    def backward(c, carry):
        cols = pl.ds(pl.multiple_of(c * width, width), width)
        de, du = [None] * parts, [None] * parts
        sums = jnp.zeros((1, width), F32)
        for s in range(parts + 2):
            if s < parts:
                de[s] = mm(dfb[s * step : (s + 1) * step, :], wdown[cols, :], NT)
            if 0 <= s - 1 < parts:
                j = s - 1
                rows = slice(j * step, (j + 1) * step)
                du[j] = (de[j] * slope[rows, cols].astype(F32)).astype(BF16)
                slope[rows, cols] = du[j]
                sums = sums + jnp.sum(du[j].astype(F32), axis=0, keepdims=True)
            if 0 <= s - 2 < parts:
                j = s - 2
                acc[j * step : (j + 1) * step, :] += mm(du[j], wup[:, cols], NT)
        upb_grad[:, cols] = sums
        return carry

    lax.fori_loop(0, chunks, backward, 0)

    def third(i, carry):
        rows = pl.ds(pl.multiple_of(i * step, step), step)
        normed, scale = norm_parts(r1[rows, :])
        grad = acc[rows, :]
        dr = norm_back(grad, normed, scale, g1)
        dr1[rows, :] = dr
        low = dr.astype(BF16)
        dab[rows, :] = low
        vec_grads[3:4, :] += jnp.sum(grad * normed, axis=0, keepdims=True)
        vec_grads[4:5, :] += jnp.sum(grad, axis=0, keepdims=True)
        vec_grads[5:6, :] += jnp.sum(low.astype(F32), axis=0, keepdims=True)
        return carry

    lax.fori_loop(0, parts, third, 0)
    dctx[...] = mm(dab[...], wout[...], NT).astype(BF16)
    outg[...] = mm(ctx[...], dab[...], TN).astype(BF16)

    def up(c, carry):
        cols = pl.ds(pl.multiple_of(c * width, width), width)
        upg[:, cols] = mm(fb[...], slope[:, cols], TN).astype(BF16)
        return carry

    lax.fori_loop(0, chunks, up, 0)


def last_kernel(x, lens, qkv, ctx, dctx, lse, dr1, wqkv, xg, qkvg, vec_grads, grads, key_feat, query_feat):
    vec_grads[...] = jnp.zeros_like(vec_grads)
    for row in range(x.shape[0] // L):
        ends, total = [], 0
        for item in range(lens.shape[1]):
            total = total + lens[row, item]
            ends.append(total)
        features(ends, key_feat, query_feat, row * L)

        rows = pl.ds(row * L, L)

        def heads(group, carry):
            attend_back(
                rows, group, 3, qkv, ctx, dctx, lse[group, rows, :], grads, key_feat[rows, :], query_feat[rows, :]
            )
            return carry

        lax.fori_loop(0, 2, heads, 0)
    vec_grads[0:1, :] = jnp.sum(grads[:, 0:D].astype(F32), axis=0, keepdims=True)
    vec_grads[1:2, :] = jnp.sum(grads[:, 2 * D : 3 * D].astype(F32), axis=0, keepdims=True)
    for part in range(3):
        cols = slice(part * D, (part + 1) * D)
        qkvg[:, cols] = mm(x[...], grads[:, cols], TN).astype(BF16)
    xg[...] = (mm(grads[...], wqkv[...], NT) + dr1[...]).astype(xg.dtype)


MESH = pl.DeviceIdType.MESH


def load(source, target, sem):
    copy = pltpu.make_async_copy(source, target, sem)
    copy.start()
    return copy


def remote(source, target, out_sem, in_sem, device):
    return pltpu.make_async_remote_copy(
        src_ref=source, dst_ref=target, send_sem=out_sem, recv_sem=in_sem,
        device_id=device, device_id_type=MESH,
    )


def arrived(target, in_sem, device):
    remote(target, target, in_sem, in_sem, device).wait_recv()


def meet(devices):
    barrier = pltpu.get_barrier_semaphore()
    for device in devices:
        pl.semaphore_signal(barrier, inc=1, device_id=device, device_id_type=MESH)
    pl.semaphore_wait(barrier, len(devices))


def example_ends(lens, row):
    place = lax.broadcasted_iota(jnp.int32, lens.shape, 1)
    counts = jnp.sum(jnp.where(place == row, lens[...], 0).astype(F32), axis=1, keepdims=True)
    ends, total = [], 0
    for item in range(lens.shape[0]):
        total = total + counts[item : item + 1, :]
        ends.append(total.astype(jnp.int32))
    return ends


def wide(vector):
    return vector[...].astype(F32).reshape(1, vector.shape[0])


def gather_kernel(
    hidden, lens, wqkv_in, bq, bv, wout_in, bout,
    x_out, qkv_out, ctx_out, r1_out, lse_out,
    x, qkv, ctx, r1, lse, wqkv, wout, bias, key_feat, query_feat,
    load_sem, own_sem, keep_sem, out_sems, in_sems,
):
    me = lax.axis_index("heads")
    row_id = lax.axis_index("rows")
    heads = lax.axis_size("heads")
    part = hidden.shape[1]
    rows_mine = x.shape[0] // L
    wqkv_load = load(wqkv_in, wqkv, load_sem.at[0])
    wout_load = load(wout_in, wout, load_sem.at[1])
    others = [lax.rem(me + step, heads) for step in range(1, heads)]
    device = lambda other: {"rows": row_id, "heads": other}

    def kept(row):
        return pltpu.make_async_copy(
            hidden.at[me * rows_mine + row], x.at[pl.ds(row * L + me * part, part)], own_sem.at[row]
        )

    def passed(row, step):
        other = others[step]
        return remote(
            hidden.at[other * rows_mine + row], x.at[pl.ds(row * L + me * part, part)],
            out_sems.at[row, step], in_sems.at[row, me], device(other),
        )

    def stores(row):
        rows = pl.ds(pl.multiple_of(row * L, L), L)
        return [
            pltpu.make_async_copy(source, target, keep_sem.at[index, row])
            for index, (source, target) in enumerate(
                (
                    (x.at[rows], x_out.at[rows]), (qkv.at[rows], qkv_out.at[rows]), (ctx.at[rows], ctx_out.at[rows]),
                    (lse.at[:, rows], lse_out.at[:, rows]), (r1.at[rows], r1_out.at[rows]),
                )
            )
        ]

    meet([device(other) for other in others])
    for row in range(rows_mine):
        for step in range(heads - 1):
            passed(row, step).start()
        kept(row).start()
    bias[0:1, :] = wide(bq)
    bias[1:2, :] = jnp.zeros((1, D), F32)
    bias[2:3, :] = wide(bv)
    out_bias = wide(bout)
    for row in range(rows_mine):
        features(example_ends(lens, me * rows_mine + row), key_feat, query_feat, row * L)
    wqkv_load.wait()
    side, sibling = me // 2, me + 1 - 2 * lax.rem(me, 2)
    near = L // (heads // 2)

    def project(row, half):
        rows = pl.ds(pl.multiple_of(row * L + half * near, near), near)
        for item in range(3):
            cols = pl.ds(item * D, D)
            acc = mm(x[rows, :], wqkv[:, cols]) + bias[item : item + 1, :]
            if item == 0:
                acc = acc * DH**-0.5
            qkv[rows, cols] = acc.astype(BF16)

    def take(row, other):
        arrived(x.at[pl.ds(row * L + other * part, part)], in_sems.at[row, other], device(other))

    def this_chip(row, carry):
        kept(row).wait()
        take(row, sibling)
        project(row, side)
        return carry

    lax.fori_loop(0, rows_mine, this_chip, 0)
    wout_load.wait()

    def whole_row(row, carry):
        rows = pl.ds(pl.multiple_of(row * L, L), L)
        for item in range(heads - 2):
            take(row, lax.rem(2 * side + 2 + item, heads))
        keep = stores(row)
        keep[0].start()
        project(row, 1 - side)
        keep[1].start()

        def group_heads(group, carry):
            attend(rows, group, 3, qkv, ctx, lse, key_feat, query_feat)
            return carry

        lax.fori_loop(0, 2, group_heads, 0)
        keep[2].start()
        keep[3].start()
        r1[rows, :] = mm(ctx[rows, :], wout[...]) + out_bias + x[rows, :].astype(F32)
        keep[4].start()
        return carry

    lax.fori_loop(0, rows_mine, whole_row, 0)
    for row in range(rows_mine):
        for step in range(heads - 1):
            passed(row, step).wait_send()
        for copy in stores(row):
            copy.wait()


class Place:
    def __init__(self):
        self.row, self.head = lax.axis_index("rows"), lax.axis_index("heads")
        self.z, self.y = self.row // 2, lax.rem(self.row, 2)
        self.x, self.c = self.head // 2, lax.rem(self.head, 2)
        self.half, self.low = self.z // 2, lax.rem(self.z, 2)
        self.next_z = self.at(z=2 * self.half + 1 - self.low)
        self.far_z = self.at(z=2 * (1 - self.half) + self.low)
        self.cross_z = self.at(z=2 * (1 - self.half) + 1 - self.low)
        self.over = {
            "c": self.at(c=1 - self.c), "y": self.at(y=1 - self.y), "x": self.at(x=1 - self.x),
        }

    def at(self, **new):
        z, y, x, c = (new.get(name, getattr(self, name)) for name in "zyxc")
        return {"rows": z * 2 + y, "heads": x * 2 + c}

    def turn(self, step):
        first, second = lax.rem(step, 2), step // 2
        half = self.half + (1 - first) * (1 - 2 * self.half)
        low = self.low + (1 - second) * (1 - 2 * self.low)
        return 2 * half + low

    def side(self, name):
        return self.y if name == "y" else self.x


class Total:
    def __init__(self, where, order, got, mid, far, near, sems, apart=False):
        self.where, self.order, self.direct = where, order.lower(), "Z" in order
        self.got, self.mid, self.far, self.near = got, mid, far, near
        self.core_out, self.core_in, self.out, self.inn, self.z_in = sems
        self.apart = apart

    @staticmethod
    def scratch(order, rows, cols, pieces, groups=()):
        shapes = [(2, 4, 2, rows, cols), (2, 4, rows, cols), (4, rows, cols), (4, rows, cols)]
        stages = 2
        if order[0] == "y":
            shapes[2:] = [(4, 2, rows, cols), (rows, cols)]
            stages = 1
        sems = [(pieces,) if pieces > 2 else (1,), (pieces,), (stages + 2,), (stages, 4), (4,)]
        spaces = [pltpu.VMEM(groups + dims, BF16) for dims in shapes]
        return spaces + [pltpu.SemaphoreType.DMA(groups + dims) for dims in sems]

    def core_copy(self, index, parts):
        source, target = parts(index)
        out = self.core_out.at[index if self.apart else 0]
        return remote(source, target, out, self.core_in.at[index], self.where.over["c"])

    def core_sent(self):
        remote(self.got, self.got, self.core_out.at[0], self.core_in.at[0], self.where.over["c"]).wait_send()

    def core_wait(self, index, target):
        arrived(target, self.core_in.at[index], self.where.over["c"])

    def part(self, ref, z, side):
        return ref.at[side, z] if self.order[0] == "x" else ref.at[:, z, side]

    def first_copy(self, step):
        w = self.where
        z = w.turn(step)
        source = self.part(self.got, z, 1 - w.side(self.order[0]))
        return remote(source, self.mid.at[:, z], self.out.at[0], self.inn.at[0, step], w.over[self.order[0]])

    def first(self, step):
        self.first_copy(step).start()

    def second_copy(self, step):
        w = self.where
        z = w.turn(step)
        source = self.mid.at[1 - w.side(self.order[1]), z]
        return remote(source, self.far.at[z], self.out.at[2], self.inn.at[1, step], w.over[self.order[1]])

    def second(self, step):
        w = self.where
        z = w.turn(step)
        arrived(self.mid.at[:, z], self.inn.at[0, step], w.over[self.order[0]])
        own = self.part(self.got, z, w.side(self.order[0]))
        self.mid[:, z] = (self.mid[:, z].astype(F32) + own[...].astype(F32)).astype(BF16)
        if self.order == "yzx":
            self.z_send(step)
        else:
            self.second_copy(step).start()

    def third(self, step):
        if self.order == "yzx":
            return
        w = self.where
        z = w.turn(step)
        arrived(self.far.at[z], self.inn.at[1, step], w.over[self.order[1]])
        own = self.mid[w.side(self.order[1]), z]
        self.far[z] = (self.far[z].astype(F32) + own.astype(F32)).astype(BF16)
        self.z_send(step)

    def z_slots(self):
        return self.far if self.order == "yzx" else self.near

    def z_block(self, step):
        z = self.where.turn(step)
        return self.mid.at[:, z] if self.order == "yzx" else self.far.at[z]

    def z_device(self, step):
        w = self.where
        return w.next_z if step == 1 else w.far_z if step == 2 else w.cross_z if self.direct else w.next_z

    def z_copy(self, step):
        return remote(
            self.z_block(step), self.z_slots().at[step], self.out.at[1], self.z_in.at[step], self.z_device(step)
        )

    def z_take(self, step):
        arrived(self.z_slots().at[step], self.z_in.at[step], self.z_device(step))
        return self.z_slots()[step].astype(F32)

    def z_send(self, step):
        if step < (3 if self.direct else 2):
            self.z_copy(step).start()

    def relay(self):
        if self.direct:
            return
        block = self.z_block(2)
        block[...] = (block[...].astype(F32) + self.z_take(0)).astype(BF16)
        self.z_copy(2).start()

    def z_sum(self):
        total = self.z_block(3)[...].astype(F32) + self.z_take(1) + self.z_take(2)
        return total + self.z_take(0) if self.direct else total

    def x_copy(self):
        w = self.where
        return remote(self.far.at[3, 1 - w.x], self.near, self.out.at[2], self.z_in.at[3], w.over["x"])

    def fourth(self):
        if self.order != "yzx":
            return
        self.far[3] = self.z_sum().astype(BF16)
        self.x_copy().start()

    def result(self):
        w = self.where
        if self.order != "yzx":
            return self.z_sum()
        arrived(self.near, self.z_in.at[3], w.over["x"])
        return self.far[3, w.x].astype(F32) + self.near[...].astype(F32)

    def sent(self):
        w = self.where
        remote(self.mid, self.mid, self.out.at[0], self.inn.at[0, 0], w.over["y"]).wait_send()
        blocks = self.z_slots().at[pl.ds(0, 3)]
        remote(blocks, blocks, self.out.at[1], self.z_in.at[0], w.next_z).wait_send()
        if self.order == "yzx":
            self.x_copy().wait_send()
        else:
            remote(self.far, self.far, self.out.at[2], self.inn.at[1, 0], w.over["y"]).wait_send()


class Everyone:
    def __init__(self, where, by_head, by_row, sems):
        self.where, self.by_head, self.by_row, self.sems = where, by_head, by_row, sems
        self.own = by_head.at[where.head]

    @staticmethod
    def scratch(rows):
        return [pltpu.VMEM((4, rows, D), F32), pltpu.VMEM((8, rows, D), F32), pltpu.SemaphoreType.DMA((14,))]

    def head_copy(self, step):
        w = self.where
        return remote(
            self.own, self.own, self.sems.at[0], self.sems.at[2 + w.head],
            {"rows": w.row, "heads": lax.rem(w.head + step, 4)},
        )

    def row_copy(self, step):
        w = self.where
        mine = self.by_row.at[w.row]
        return remote(
            mine, mine, self.sems.at[1], self.sems.at[6 + w.row],
            {"rows": lax.rem(w.row + step, 8), "heads": w.head},
        )

    def start(self):
        for step in range(1, 4):
            self.head_copy(step).start()

    def middle(self):
        w = self.where
        for step in range(1, 4):
            head = lax.rem(w.head + step, 4)
            arrived(self.by_head.at[head], self.sems.at[2 + head], {"rows": w.row, "heads": head})
        self.by_row[w.row] = (self.by_head[0] + self.by_head[1]) + (self.by_head[2] + self.by_head[3])
        for step in range(1, 8):
            self.row_copy(step).start()

    def result(self):
        w = self.where
        for step in range(1, 8):
            row = lax.rem(w.row + step, 8)
            arrived(self.by_row.at[row], self.sems.at[6 + row], {"rows": row, "heads": w.head})
        total = self.by_row[0]
        for row in range(1, 8):
            total = total + self.by_row[row]
        return total

    def sent(self):
        w = self.where
        for ref, count, sem in ((self.by_head, 3, 0), (self.by_row, 7, 1)):
            part = ref.at[pl.ds(0, count)]
            remote(part, part, self.sems.at[sem], self.sems.at[2], w.over["y"]).wait_send()


def rest_kernel(
    scale,
    r1_in, cotan, ctx_in, qkv_in, lse_in, x_in, lens, wup_in, wdown_in, wout_in, wqkv_in,
    g1v, s1v, g2v, s2v, bdv, bup,
    lay, xgr, down_to, up_to, out_to, qkv_to, vec_to,
    downo, upo, outo, qkvo, vec_out, mat_sem, r1, ycot, fb, act, slope, acc, dfb, dfbt, wup, wdown, down_send,
    load_sem, cot_sem, lay_sem, xg_sem, own_sem,
    *scratch,
):
    where = w = Place()
    scratch = list(scratch)

    def take(count):
        return [scratch.pop(0) for _ in range(count)]

    totals = []
    for order, *_ in BLOCKS:
        refs = take(9)
        totals.append(Total(where, order, *refs[:4], refs[4:], apart=not totals))
    down, upa, upb, out = totals
    joint = [(order, take(9)) for order, *_ in JOINT]

    def qkv_pair(group):
        made = []
        for order, refs in joint:
            refs = [ref.at[group] for ref in refs]
            made.append(Total(where, order, *refs[:4], refs[4:]))
        return made

    qkvs = (qkv_pair(0), qkv_pair(1))
    everyone = Everyone(where, *take(3))
    late = Everyone(where, *take(3))

    tokens = r1.shape[0]
    step_rows = 256
    parts = tokens // step_rows
    width = 768
    chunks = wup_in.shape[1] // width
    rows_mine = tokens // L
    part = lay.shape[1]
    r1_rows = [pl.ds(index * step_rows, step_rows) for index in range(parts)]
    r1_loads = [load(r1_in.at[rows], r1.at[rows], load_sem.at[9 + index]) for index, rows in enumerate(r1_rows)]
    wup_load = load(wup_in, wup, load_sem.at[1])
    wdown_load = load(wdown_in, wdown, load_sem.at[2])
    others = [lax.rem(w.head + step, 4) for step in range(1, 4)]
    partner = lambda other: {"rows": w.row, "heads": other}
    g1, s1, g2, s2, bd = (wide(item) for item in (g1v, s1v, g2v, s2v, bdv))
    mine = everyone.own
    mine[...] = jnp.zeros(mine.shape, F32)
    last = late.own
    last[...] = jnp.zeros(last.shape, F32)

    def lead(i, carry):
        rows = pl.ds(pl.multiple_of(i * step_rows, step_rows), step_rows)
        pltpu.make_async_copy(r1_in.at[rows], r1.at[rows], load_sem.at[9 + i]).wait()
        normed, _ = norm_parts(r1[rows, :])
        first = normed * g1 + s1
        fb[rows, :] = first.astype(BF16)
        acc[rows, :] = first + bd
        return carry

    lax.fori_loop(0, parts, lead, 0)
    meet([partner(other) for other in others] + [{"rows": lax.rem(w.row + step, 8), "heads": w.head} for step in range(1, 8)])

    def mine_in(row):
        place = pl.ds(row * L + w.head * part, part)
        return pltpu.make_async_copy(cotan.at[w.head * rows_mine + row], ycot.at[place], own_sem.at[2, row])

    def cot_copy(row, step):
        place = pl.ds(row * L + w.head * part, part)
        other = others[step]
        return remote(
            cotan.at[other * rows_mine + row], ycot.at[place], cot_sem.at[0], cot_sem.at[1 + row],
            partner(other),
        )

    def give_back(source, target, sems, row, step):
        other = others[step]
        return remote(
            source.at[pl.ds(row * L + other * part, part)], target.at[w.head * rows_mine + row],
            sems.at[0], sems.at[1 + row], partner(other),
        )

    def mine_out(source, target, index, row):
        place = pl.ds(row * L + w.head * part, part)
        return pltpu.make_async_copy(source.at[place], target.at[w.head * rows_mine + row], own_sem.at[index, row])

    for row in range(rows_mine):
        for step in range(3):
            cot_copy(row, step).start()
        mine_in(row).start()

    wup_load.wait()
    wdown_load.wait()

    def forward(c, carry):
        cols = pl.ds(pl.multiple_of(c * width, width), width)
        u, e = [None] * parts, [None] * parts
        for s in range(parts + 2):
            if s < parts:
                u[s] = mm(fb[s * step_rows : (s + 1) * step_rows, :], wup[:, cols]) + wide(bup.at[cols])
            if 0 <= s - 1 < parts:
                j = s - 1
                rows = slice(j * step_rows, (j + 1) * step_rows)
                cdf, pdf = normal_parts(u[j])
                e[j] = (u[j] * cdf).astype(BF16)
                act[rows, cols] = e[j]
                slope[rows, cols] = (cdf + u[j] * pdf).astype(BF16)
            if 0 <= s - 2 < parts:
                j = s - 2
                acc[j * step_rows : (j + 1) * step_rows, :] += mm(e[j], wdown[cols, :])
        return carry

    lax.fori_loop(0, chunks, forward, 0)
    for row in range(rows_mine):
        mine_in(row).wait()
        arrived(ycot.at[pl.ds(row * L, 3 * part)], cot_sem.at[1 + row], partner(others[0]))

    def second(i, carry):
        rows = pl.ds(pl.multiple_of(i * step_rows, step_rows), step_rows)
        normed, spread = norm_parts(acc[rows, :])
        dy = ycot[rows, :].astype(F32)
        ycot[rows, :] = (normed * g2 + s2).astype(BF16)
        dr2 = norm_back(dy, normed, spread, g2)
        acc[rows, :] = dr2
        low = dr2.astype(BF16)
        dfb[rows, :] = low
        dfbt[:, :, rows] = low.T.reshape(4, D // 4, step_rows)
        mine[0:1, :] += jnp.sum(dy * normed, axis=0, keepdims=True)
        mine[1:2, :] += jnp.sum(dy, axis=0, keepdims=True)
        mine[2:3, :] += jnp.sum(low.astype(F32), axis=0, keepdims=True)
        return carry

    lax.fori_loop(0, parts, second, 0)

    for row in range(rows_mine):
        for step in range(3):
            give_back(ycot, lay, lay_sem, row, step).start()
        mine_out(ycot, lay, 0, row).start()

    def down_half(core, z):
        left = jnp.concatenate([dfbt[core], dfbt[2 + core]], axis=0)
        cols = pl.ds(pl.multiple_of(z * width, width), width)
        return mm(left, act[:, cols])

    quarter, eighth = D // 4, width // 2

    def down_parts(step):
        z = where.turn(step)
        return down_send.at[lax.rem(step, 2)], down.got.at[:, z]

    def down_other(step, carry):
        z = where.turn(step)
        total = down_half(1 - w.c, z)

        @pl.when(step >= 2)
        def _():
            down.core_copy(step - 2, down_parts).wait_send()

        slot = lax.rem(step, 2)
        for x in range(2):
            for y in range(2):
                piece = total[x * quarter : (x + 1) * quarter, y * eighth : (y + 1) * eighth]
                down_send[slot, x, y] = piece.astype(BF16)
        down.core_copy(step, down_parts).start()
        return carry

    def down_own(step, carry):
        z = where.turn(step)
        total = down_half(w.c, z)
        down.core_wait(step, down.got.at[:, z])
        for x in range(2):
            for y in range(2):
                piece = total[x * quarter : (x + 1) * quarter, y * eighth : (y + 1) * eighth]
                down.got[x, z, y] = (piece + down.got[x, z, y].astype(F32)).astype(BF16)
        down.first(step)
        return carry

    lax.fori_loop(0, 4, down_other, 0)
    lax.fori_loop(0, 4, down_own, 0)
    qkv_load = load(qkv_in, act.at[:, pl.ds(0, 3 * D)], load_sem.at[4])

    def backward(c, carry):
        cols = pl.ds(pl.multiple_of(c * width, width), width)
        de, du = [None] * parts, [None] * parts
        sums = jnp.zeros((1, width), F32)
        for s in range(parts + 2):
            if s < parts:
                de[s] = mm(dfb[s * step_rows : (s + 1) * step_rows, :], wdown[cols, :], NT)
            if 0 <= s - 1 < parts:
                j = s - 1
                rows = slice(j * step_rows, (j + 1) * step_rows)
                du[j] = (de[j] * slope[rows, cols].astype(F32)).astype(BF16)
                slope[rows, cols] = du[j]
                sums = sums + jnp.sum(du[j].astype(F32), axis=0, keepdims=True)
            if 0 <= s - 2 < parts:
                j = s - 2
                acc[j * step_rows : (j + 1) * step_rows, :] += mm(du[j], wup[:, cols], NT)
        mine[pl.ds(3 + c, 1), :] = sums
        return carry

    half = chunks // 2
    lax.fori_loop(0, half, backward, 0)
    down.second(0)
    lax.fori_loop(half, chunks, backward, 0)
    down.second(1)
    down.third(0)
    wqkv = wup.at[:, pl.ds(0, 3 * D)]
    x = wdown.at[pl.ds(2 * D, tokens)]
    wout = wup.at[:, pl.ds(3 * D, D)]
    wqkv_load = load(wqkv_in, wqkv, load_sem.at[5])
    wout_load = load(wout_in, wout, load_sem.at[3])
    x_load = load(x_in, x, load_sem.at[6])
    dab = dfb
    feats = wdown.at[pl.ds(2 * D + tokens, L)]
    for row in range(rows_mine):
        key_feat, query_feat = (feats.at[:, pl.ds((2 * row + item) * 128, 128)] for item in range(2))
        features(example_ends(lens, w.head * rows_mine + row), key_feat, query_feat, 0)

    def third(i, carry):
        rows = pl.ds(pl.multiple_of(i * step_rows, step_rows), step_rows)
        normed, spread = norm_parts(r1[rows, :])
        grad = acc[rows, :]
        dr = norm_back(grad, normed, spread, g1)
        acc[rows, :] = dr
        low = dr.astype(BF16)
        dab[rows, :] = low
        mine[7:8, :] += jnp.sum(grad * normed, axis=0, keepdims=True)
        last[2:3, :] += jnp.sum(grad, axis=0, keepdims=True)
        last[3:4, :] += jnp.sum(low.astype(F32), axis=0, keepdims=True)
        return carry

    lax.fori_loop(0, parts, third, 0)
    lse_load = [load(lse_in.at[g], r1.at[:, pl.ds(g * 128, 128)], load_sem.at[7 + g]) for g in range(2)]

    def up_half(core, x_side):
        cols = pl.ds(pl.multiple_of((2 * x_side + core) * width, width), width)
        return mm(fb[...], slope[:, cols], TN)

    ups = (upa, upb)

    def spot(side, index, pair, start):
        rows, cols = pair[index].got.shape[-2:]
        row = pl.multiple_of(side * D + index * (D - 8 * rows), 128)
        return wdown.at[pl.ds(row, 8 * rows), pl.ds(start, cols)], each_got(pair[index], side)

    def each_got(each, side):
        rows, cols = each.got.shape[-2:]
        return each.got.at[side].reshape(8 * rows, cols)

    def pair_rows(pair, total):
        edge, cols = pair[0].got.shape[-2:]
        total = total.reshape(4, 2, D // 8, cols)
        return total[:, :, :edge], total[:, :, edge:]

    def pair_other(pair, side, total, start):
        for index, rows in enumerate(pair_rows(pair, total.astype(BF16))):
            place, target = spot(side, index, pair, start)
            place[...] = rows.reshape(place.shape)
            pair[index].core_copy(side, lambda _: (place, target)).start()

    def pair_own(pair, side, turn, total):
        for each, rows in zip(pair, pair_rows(pair, total)):
            each.core_wait(side, each.got.at[side])
            each.got[side] = (rows + each.got[side].astype(F32)).astype(BF16)
        for when, each in enumerate((pair[1], pair[0])):

            @pl.when(turn == when)
            def _():
                for step in range(4):
                    each.first(step)

    def pair_sent(pair):
        for each in pair:
            each.core_sent()

    def far_first(turn):
        return lax.rem(w.x + 1 + turn, 2)

    def up_other(turn, carry):
        side = far_first(turn)
        pair_other(ups, side, up_half(1 - w.c, side), 0)
        return carry

    lax.fori_loop(0, 2, up_other, 0)
    down.second(2)
    down.relay()
    down.third(1)

    def up_own(turn, carry):
        side = far_first(turn)
        pair_own(ups, side, turn, up_half(w.c, side))
        return carry

    lax.fori_loop(0, 2, up_own, 0)
    down.second(3)
    down.third(2)
    ctx = slope.at[:, pl.ds(3 * D, D)]
    grads = slope.at[:, pl.ds(0, 3 * D)]
    dctx = act.at[:, pl.ds(3 * D, D)]
    ctx_load = load(ctx_in, ctx, load_sem.at[0])
    wout_load.wait()

    def context_grad(row, carry):
        rows = pl.ds(pl.multiple_of(row * L, L), L)
        dctx[rows, :] = mm(dab[rows, :], wout[...], NT).astype(BF16)
        return carry

    lax.fori_loop(0, rows_mine, context_grad, 0)
    ctx_load.wait()
    wqkv_load.wait()

    def out_half(core, side):
        cols = pl.ds(pl.multiple_of(384 * side + 128 * core, 128), 256)
        return mm(ctx[...], dab[:, cols], TN)

    def out_parts(side):
        spot = wup.at[:, pl.ds(pl.multiple_of(3 * D + 256 * side, 256), 256)]
        return spot, out.got.at[side].reshape(D, 256)

    def out_other(side, carry):
        out_parts(side)[0][...] = out_half(1 - w.c, side).astype(BF16)
        out.core_copy(side, out_parts).start()
        return carry

    def out_own(side, carry):
        total = out_half(w.c, side).reshape(4, 2, D // 8, 256)
        out.core_wait(side, out.got.at[side])
        out.got[side] = (total + out.got[side].astype(F32)).astype(BF16)
        return carry

    lax.fori_loop(0, 2, out_other, 0)
    lax.fori_loop(0, 2, out_own, 0)
    for step in range(4):
        out.first(step)
    upa.second(0)
    everyone.start()

    qkv = act.at[:, pl.ds(0, 3 * D)]
    qkv_load.wait()
    for copy in lse_load:
        copy.wait()
    x_load.wait()

    def input_grad(row):
        rows = pl.ds(pl.multiple_of(row * L, L), L)
        fb[rows, :] = (mm(grads[rows, :], wqkv[...], NT) + acc[rows, :]).astype(BF16)
        for step in range(3):
            give_back(fb, xgr, xg_sem, row, step).start()
        mine_out(fb, xgr, 1, row).start()

    def qkv_half(core, side, group):
        early = side * 1536 + (1 - side) * core * D
        later = side * (1152 + core * D) + (1 - side) * 384
        start = pl.multiple_of((1 - group) * early + group * later, 128)
        return mm(x[...], grads[:, pl.ds(start, 384)], TN)

    def qkv_sums(group):
        pair = qkv_pair(group)
        start = pl.multiple_of(group * 384, 128)

        def other(turn, carry):
            side = far_first(turn)
            pair_other(pair, side, qkv_half(1 - w.c, side, group), start)
            return carry

        def own(turn, carry):
            side = far_first(turn)
            pair_own(pair, side, turn, qkv_half(w.c, side, group))
            return carry

        lax.fori_loop(0, 2, other, 0)
        lax.fori_loop(0, 2, own, 0)

    def heads_back(i, carry):
        group, row = i // 2, lax.rem(i, 2)
        rows = pl.ds(pl.multiple_of(row * L, L), L)
        keep = r1[rows, pl.ds(pl.multiple_of(group * 128, 128), 128)]
        lanes = [pl.ds(pl.multiple_of(2 * row * 128 + 128 * item, 128), 128) for item in range(2)]
        attend_back(rows, group, 3, qkv, ctx, dctx, keep, grads, feats[:, lanes[0]], feats[:, lanes[1]])

        @pl.when(i == 0)
        def _():
            upa.second(1)
            upb.second(0)
            upb.second(1)
            pair_sent(ups)

        @pl.when(i == 1)
        def _():
            upa.second(2)
            upa.second(3)
            upa.relay()
            upb.second(2)
            down.fourth()

        @pl.when(i == 2)
        def _():
            upb.second(3)
            upb.third(0)
            for step in range(4):
                out.second(step)
            everyone.middle()

        @pl.when(i == 3)
        def _():
            last[0:1, :] = jnp.sum(grads[:, 0:D].astype(F32), axis=0, keepdims=True)
            last[1:2, :] = jnp.sum(grads[:, 2 * D : 3 * D].astype(F32), axis=0, keepdims=True)
            late.start()
            out.relay()
            for step in range(1, 4):
                upb.third(step)
            upa.fourth()

        @pl.when(row == 1)
        def _():
            qkv_sums(group)

        @pl.when(i == 3)
        def _():
            for step in range(4):
                qkvs[0][0].second(step)
            upb.relay()
            out.fourth()
            late.middle()

        @pl.when(group == 1)
        def _():
            input_grad(row)

        @pl.when(i == 2)
        def _():
            for step in range(4):
                qkvs[0][1].second(step)

        return carry

    lax.fori_loop(0, 4, heads_back, 0)
    (qkva, qkvb), (ena, enb) = qkvs
    downo[...] = down.result() * scale
    kept = [load(downo, down_to, mat_sem.at[0])]
    edge = upa.got.shape[-2]
    for step in range(4):
        qkvb.third(step)
    enb.second(0)
    enb.second(1)
    ena.second(0)
    ena.second(1)
    enb.second(2)
    enb.second(3)
    qkva.relay()
    qkvb.relay()
    ena.second(2)
    ena.second(3)
    enb.third(0)
    enb.third(1)
    enb.third(2)
    enb.third(3)
    qkva.fourth()
    upo[edge:, :] = upb.result() * scale
    ena.fourth()
    outo[...] = pick(out.result() * scale, w.c, 192)
    kept.append(load(outo, out_to, mat_sem.at[1]))
    upo[0:edge, :] = upa.result() * scale
    kept.append(load(upo, up_to, mat_sem.at[2]))
    vectors = everyone.result() * scale
    vec_out[12:16, :] = jnp.zeros((4, D), F32)
    for index, item in ((3, 7), (5, 2), (6, 0), (7, 1), (8, 3), (9, 4), (10, 5), (11, 6)):
        vec_out[index : index + 1, :] = vectors[item : item + 1, :]
    for index in range(2):
        down.core_copy(2 + index, down_parts).wait_send()
    out.core_sent()
    for total in totals[:4]:
        total.sent()
    everyone.sent()

    def all_sent(source, sem):
        part_sent = source.at[pl.ds(0, 3 * rows_mine * part)]
        remote(part_sent, part_sent, sem, sem, partner(others[0])).wait_send()

    all_sent(ycot, cot_sem.at[0])
    all_sent(ycot, lay_sem.at[0])
    for row in range(rows_mine):
        arrived(lay.at[pl.ds(3 * row, 3)], lay_sem.at[1 + row], partner(others[0]))
        mine_out(ycot, lay, 0, row).wait()
    for group in range(2):
        pair_sent(qkvs[group])
    early = jnp.concatenate([qkva.result(), qkvb.result()], axis=0) * scale
    qkva.sent()
    qkvb.sent()
    ends = late.result() * scale
    vec_out[0:2, :] = ends[0:2, :]
    vec_out[2:3, :] = ends[3:4, :]
    vec_out[4:5, :] = ends[2:3, :]
    kept.append(load(vec_out, vec_to, mat_sem.at[3]))
    late.sent()
    late_part = jnp.concatenate([ena.result(), enb.result()], axis=0) * scale
    for corner, (one, two) in enumerate(
        (
            ((0, 384, 0), (384, 192, 0)), ((192, 384, 0), (0, 192, 192)),
            ((384, 192, 0), (0, 384, 0)), ((0, 192, 192), (192, 384, 0)),
        )
    ):

        @pl.when(w.head == corner)
        def _():
            for value, (place, size, start) in ((early, one), (late_part, two)):
                qkvo[:, place : place + size] = value[:, start : start + size]

    kept.append(load(qkvo, qkv_to, mat_sem.at[4]))
    for row in range(rows_mine):
        arrived(xgr.at[pl.ds(3 * row, 3)], xg_sem.at[1 + row], partner(others[0]))
        mine_out(fb, xgr, 1, row).wait()
    all_sent(fb, xg_sem.at[0])
    ena.sent()
    enb.sent()
    for copy in kept:
        copy.wait()


def pick(values, core, width):
    return jnp.where(core == 0, values[:, :width], values[:, 64 : 64 + width])


VMEM = pl.BlockSpec(memory_space=pltpu.VMEM)
SMEM = pl.BlockSpec(memory_space=pltpu.SMEM)


def shape(dims, kind):
    return jax.ShapeDtypeStruct(dims, kind)


def params(**more):
    return pltpu.CompilerParams(vmem_limit_bytes=255 * 2**18, **more)


def local(
    hidden_in, lengths, qkv_weight, query_bias, value_bias, out_weight, out_bias, gain_one,
    shift_one, up_weight, up_bias, down_weight, down_bias, gain_two, shift_two, cotangent,
):
    row_count, part_len = hidden_in.shape[0], hidden_in.shape[1]
    heads = lax.axis_size("heads")
    mine = row_count // heads
    tokens = mine * L
    ff = up_weight.shape[1]
    place = lax.axis_index("heads")
    x = lax.all_to_all(hidden_in, "heads", split_axis=0, concat_axis=1, tiled=True).reshape(tokens, D)
    cot = lax.all_to_all(cotangent, "heads", split_axis=0, concat_axis=1, tiled=True).reshape(tokens, D)
    lens = lax.dynamic_slice_in_dim(lengths, place * mine, mine, 0)
    bqkv = jnp.concatenate([query_bias, jnp.zeros_like(query_bias), value_bias]).astype(F32)[None]
    qkv, ctx, r1, lse = pl.pallas_call(
        first_kernel,
        out_shape=(
            shape((tokens, 3 * D), BF16), shape((tokens, D), BF16), shape((tokens, D), F32),
            shape((2, tokens, 128), F32),
        ),
        in_specs=[VMEM, SMEM] + [VMEM] * 4,
        out_specs=(VMEM,) * 4,
        scratch_shapes=[pltpu.VMEM((tokens, 128), BF16)] * 2,
        compiler_params=params(),
        name="first",
    )(x, lens, qkv_weight, bqkv, out_weight, out_bias.astype(F32)[None])
    vecs = jnp.stack([gain_one, shift_one, gain_two, shift_two, down_bias]).astype(F32)
    y, dr1, dctx, downg, upg, outg, vec_mid, upb = pl.pallas_call(
        middle_kernel,
        out_shape=(
            shape((tokens, D), BF16), shape((tokens, D), F32), shape((tokens, D), BF16),
            shape((D, ff), BF16), shape((D, ff), BF16), shape((D, D), BF16),
            shape((8, D), F32), shape((1, ff), F32),
        ),
        in_specs=[VMEM] * 8,
        out_specs=(VMEM,) * 8,
        scratch_shapes=[
            pltpu.VMEM((tokens, D), BF16), pltpu.VMEM((tokens, ff), BF16), pltpu.VMEM((tokens, ff), BF16),
            pltpu.VMEM((tokens, D), F32), pltpu.VMEM((tokens, D), BF16), pltpu.VMEM((tokens, D), BF16),
        ],
        compiler_params=params(),
        name="middle",
    )(r1, ctx, cot, vecs, up_weight, up_bias.astype(F32)[None], down_weight, out_weight)
    xg, qkvg, vec_last = pl.pallas_call(
        last_kernel,
        out_shape=(shape((tokens, D), BF16), shape((D, 3 * D), BF16), shape((8, D), F32)),
        in_specs=[VMEM, SMEM] + [VMEM] * 6,
        out_specs=(VMEM,) * 3,
        scratch_shapes=[pltpu.VMEM((tokens, 3 * D), BF16)] + [pltpu.VMEM((tokens, 128), BF16)] * 2,
        compiler_params=params(),
        name="last",
    )(x, lens, qkv, ctx, dctx, lse, dr1, qkv_weight)

    def back(values):
        values = values.reshape(mine, L, D)
        return lax.all_to_all(values, "heads", split_axis=1, concat_axis=0, tiled=True)

    layer_out = back(y)
    input_grad = back(xg).astype(F32)
    scale = 1.0 / (row_count * lax.axis_size("rows"))
    vec_mid, vec_last, upb = lax.psum((vec_mid, vec_last, upb), ("rows", "heads"))

    def reduce(values, flip):
        one, two = (0, 1) if flip else (1, 0)
        half = lax.psum_scatter(values, "heads", scatter_dimension=one, tiled=True).astype(F32)
        total = lax.psum_scatter(half, "rows", scatter_dimension=two, tiled=True) * scale
        return total.T if flip else total

    vm, vl = vec_mid * scale, vec_last * scale
    return (
        layer_out, input_grad, reduce(qkvg, False), vl[0], vl[1], reduce(outg, False), vm[5], vm[3], vm[4],
        reduce(upg, False), upb[0] * scale, reduce(downg, True), vm[2], vm[0], vm[1],
    )


ANY = pl.BlockSpec(memory_space=pl.ANY)
DMA = pltpu.SemaphoreType.DMA
BLOCKS = (("yzx", 192, 384, 4), ("yzx", 48, 768, 2), ("xyz", 48, 768, 2), ("yzx", 96, 256, 2))
JOINT = (("yZx", 32, 384, 2), ("xyZ", 64, 384, 2))


def finish_kernel(count, *refs):
    lay, xgr, vec = refs[:3]
    mats = refs[3 : 3 + count]
    lay_out, xg_out = refs[3 + count : 5 + count]
    mats_out = refs[5 + count : 5 + 2 * count]
    vecs_out = refs[5 + 2 * count : 14 + 2 * count]
    through, low, full, sems = refs[14 + 2 * count : 18 + 2 * count]
    mats_here, (vec_here, mat_sems) = refs[18 + 2 * count : 18 + 3 * count], refs[-2:]
    vec_load = load(vec, vec_here, mat_sems.at[0, count])
    blocks = xgr.shape[0]
    wides = [load(xgr.at[i], low.at[i], sems.at[0, i]) for i in range(blocks)]
    lays = [load(lay.at[i], through.at[i], sems.at[1, i]) for i in range(blocks)]
    arrive = [load(mats[i], mats_here[i], mat_sems.at[0, i]) for i in range(count)]
    copies = []
    for i in range(blocks):
        wides[i].wait()
        full[i] = low[i].astype(F32)
        copies.append(load(full.at[i], xg_out.at[i], sems.at[2, i]))
    for i in range(blocks):
        lays[i].wait()
        copies.append(load(through.at[i], lay_out.at[i], sems.at[3, i]))
    for i in range(count):
        arrive[i].wait()
        copies.append(load(mats_here[i], mats_out[i], mat_sems.at[1, i]))
    vec_load.wait()
    for index in range(8):
        vecs_out[index][...] = vec_here[index, :]
    for index in range(4):
        vecs_out[8][index * D : (index + 1) * D] = vec_here[8 + index, :]
    for copy in copies:
        copy.wait()


def local_fast(
    hidden_in, lengths, qkv_weight, query_bias, value_bias, out_weight, out_bias, gain_one,
    shift_one, up_weight, up_bias, down_weight, down_bias, gain_two, shift_two, cotangent,
):
    row_count, part_len = hidden_in.shape[0], hidden_in.shape[1]
    mine = row_count // lax.axis_size("heads")
    heads = lax.axis_size("heads")
    tokens = mine * L
    ff = up_weight.shape[1]
    bf = lambda *dims: pltpu.VMEM(dims, BF16)
    fl = lambda *dims: pltpu.VMEM(dims, F32)
    x, qkv, ctx, r1, lse = pl.pallas_call(
        gather_kernel,
        out_shape=(
            shape((tokens, D), BF16), shape((tokens, 3 * D), BF16),
            shape((tokens, D), BF16), shape((tokens, D), F32), shape((2, tokens, 128), F32),
        ),
        in_specs=[ANY, VMEM, ANY, VMEM, VMEM, ANY, VMEM],
        out_specs=(ANY,) * 5,
        scratch_shapes=[
            bf(tokens, D), bf(tokens, 3 * D), bf(tokens, D), fl(tokens, D), fl(2, tokens, 128), bf(D, 3 * D),
            bf(D, D), fl(8, D), bf(tokens, 128), bf(tokens, 128),
            DMA((2,)), DMA((mine,)), DMA((5, mine)), DMA((mine, heads - 1)), DMA((mine, heads)),
        ],
        compiler_params=params(collective_id=0, has_side_effects=True),
        name="gather",
    )(hidden_in, lengths.T, qkv_weight, query_bias, value_bias, out_weight, out_bias)
    scale = 1.0 / (row_count * lax.axis_size("rows"))
    totals = []
    for block in BLOCKS:
        totals += Total.scratch(*block)
    for block in JOINT:
        totals += Total.scratch(*block, groups=(2,))
    mats = (shape((192, 384), F32), shape((96, 768), F32), shape((96, 192), F32), shape((96, 576), F32))
    wide_out = shape((row_count, part_len, D), BF16)
    lay, xgr, downg, upg, outg, qkvg, vec = pl.pallas_call(
        functools.partial(rest_kernel, scale),
        out_shape=(wide_out, wide_out) + mats + (shape((16, D), F32),),
        in_specs=[ANY] * 6 + [VMEM] + [ANY] * 4 + [VMEM] * 6,
        out_specs=(ANY,) * 7,
        scratch_shapes=[fl(*item.shape) for item in mats] + [
            fl(16, D), DMA((5,)),
            fl(tokens, D), bf(tokens, D), bf(tokens, D), bf(tokens, ff), bf(tokens, ff),
            fl(tokens, D), bf(tokens, D), bf(4, D // 4, tokens), bf(D, ff), bf(ff, D),
            bf(2, 2, 2, 192, 384), DMA((13,)), DMA((1 + mine,)), DMA((1 + mine,)), DMA((1 + mine,)), DMA((3, mine)),
        ]
        + totals
        + Everyone.scratch(8)
        + Everyone.scratch(8),
        compiler_params=params(collective_id=1, has_side_effects=True),
        name="rest",
    )(
        r1, cotangent, ctx, qkv, lse, x, lengths.T, up_weight, down_weight, out_weight, qkv_weight,
        gain_one, shift_one, gain_two, shift_two, down_bias, up_bias,
    )
    results = pl.pallas_call(
        functools.partial(finish_kernel, 4),
        out_shape=(wide_out, shape((row_count, part_len, D), F32)) + mats + (shape((D,), F32),) * 8 + (shape((ff,), F32),),
        in_specs=[ANY] * 7,
        out_specs=(ANY,) * 6 + (VMEM,) * 9,
        scratch_shapes=[
            bf(row_count, part_len, D), bf(row_count, part_len, D), fl(row_count, part_len, D), DMA((4, row_count)),
        ]
        + [fl(*item.shape) for item in mats]
        + [fl(16, D), DMA((2, 5))],
        compiler_params=params(),
        name="finish",
    )(lay, xgr, vec, downg, upg, outg, qkvg)
    layer_out, input_grad, downg, upg, outg, qkvg, qb, vb, ob, go, so, db, gt, st, ub = results
    return layer_out, input_grad, qkvg, qb, vb, outg, ob, go, so, upg, ub, downg.T, db, gt, st


def solution(mesh):
    split = P("rows", "heads", None)
    grid = P("rows", "heads")
    in_specs = (split, P("rows", None)) + (P(),) * 13 + (split,)
    out_specs = (split, split, grid, P(), P(), grid, P(), P(), P(), grid, P(), grid, P(), P(), P())
    fast = mesh.shape["rows"] == 8 and mesh.shape["heads"] == 4
    return jax.shard_map(
        local_fast if fast else local, mesh=mesh, in_specs=in_specs, out_specs=out_specs, check_vma=False
    )
```
